32 devices in a mesh: dp: 8 (over y, x, core), fsdp: 4 (over z).
Axes of the slice: x: 2, y: 2, z: 4, core: 2. Of those that a mesh axis runs over, the one named last changes fastest.
Arguments:
- tokens: bfloat16 [2, 4, 1024, 2048], P(None, 'fsdp', 'dp'), may hold values from -6 to 6
- cotangent: bfloat16 [2, 4, 1024, 2048], P(None, 'fsdp', 'dp'), may hold values from -6 to 6
- lengths: int32 [2, 4, 1], P(None, 'fsdp'), may hold values from 256 to 1024, as said below
- norm1_gain: bfloat16 [2048], P('dp'), may hold values from 0.25 to 1.75
- in_weight: bfloat16 [2048, 3, 2048], P('dp', None, 'fsdp'), may hold values from -0.125 to 0.125
- conv_taps: bfloat16 [3, 2048], P(None, 'fsdp'), may hold values from -1 to 1
- out_weight: bfloat16 [2048, 2048], P('fsdp', 'dp'), may hold values from -0.125 to 0.125
- norm2_gain: bfloat16 [2048], P('dp'), may hold values from 0.25 to 1.75
- gate_weight: bfloat16 [2048, 8192], P('dp', 'fsdp'), may hold values from -0.125 to 0.125
- up_weight: bfloat16 [2048, 8192], P('dp', 'fsdp'), may hold values from -0.125 to 0.125
- down_weight: bfloat16 [8192, 2048], P('fsdp', 'dp'), may hold values from -0.125 to 0.125
Outputs:
- block_out: bfloat16 [2, 4, 1024, 2048], P(None, 'fsdp', 'dp')
- token_grad: bfloat16 [2, 4, 1024, 2048], P(None, 'fsdp', 'dp')
- norm1_gain_grad: float32 [2048], P('dp')
- in_weight_grad: float32 [2048, 3, 2048], P('dp', None, 'fsdp')
- conv_taps_grad: float32 [3, 2048], P(None, 'fsdp')
- out_weight_grad: float32 [2048, 2048], P('fsdp', 'dp')
- norm2_gain_grad: float32 [2048], P('dp')
- gate_weight_grad: float32 [2048, 8192], P('dp', 'fsdp')
- up_weight_grad: float32 [2048, 8192], P('dp', 'fsdp')
- down_weight_grad: float32 [8192, 2048], P('fsdp', 'dp')
The draws below stay inside these ranges and needn't reach their ends.
Inputs may be any that keep to these rules, and one draw needn't show every extreme that they name: `lengths`: valid slots of each sequence, counted from its first slot; some sequence is full and some has 256.
All inputs are finite; a program needn't handle non-finite values.
Results may differ from the reference program's by a relative error of at most 0.01.
Values may be sent and summed in bfloat16 or wider, within the bound.
A program may use at most 256 MiB of HBM per device.

```python
import jax
import jax.numpy as jnp
from jax import lax

D = 2048
FF = 8192
SEQ_LEN = 1024
MICRO = 2
LINE = 1024
GROUPS = 4


def draw_lengths(key, part):
    seq_count = LINE // SEQ_LEN
    drawn = jax.random.randint(key, (MICRO, GROUPS, seq_count), SEQ_LEN // 4, SEQ_LEN + 1, dtype=jnp.int32)
    drawn = drawn.at[0, 0, 0].set(SEQ_LEN)
    drawn = drawn.at[MICRO - 1, GROUPS - 1, seq_count - 1].set(SEQ_LEN // 4)
    return drawn


def level_of(rng, dims, split, smallest, largest):
    level = 1.0
    for axis_at, parts in split:
        draws = jax.random.uniform(jax.random.fold_in(jax.random.fold_in(rng, 6), axis_at), (parts,), jnp.float32, smallest / len(split), largest / len(split))
        level = level * jnp.repeat(jnp.exp(draws), dims[axis_at] // parts).reshape((-1,) + (1,) * (len(dims) - 1 - axis_at))
    return level


def noise(rng, shape, scale, most, split=(), kind=jnp.bfloat16):
    level = level_of(rng, shape, split, -0.22, 0.18) if split else 1.0
    values = jax.random.normal(rng, shape, jnp.float32) * scale * level
    return jnp.minimum(jnp.maximum(values, -most), most).astype(kind)


def setup_inputs(seed: int = 0) -> dict:
    keys = jax.random.split(jax.random.key(seed), 12)
    tokens = noise(keys[0], (MICRO, GROUPS, LINE, D), 1.0, 6.0, ((1, 4), (2, 8)))
    cotangent = noise(keys[1], (MICRO, GROUPS, LINE, D), 1.0, 6.0, ((1, 4), (2, 8)))
    lengths = draw_lengths(jax.random.fold_in(keys[11], 71), 0)
    norm1_gain = jnp.clip(1.0 + 0.15 * jax.random.normal(keys[3], (D,), jnp.float32), 0.25, 1.75).astype(jnp.bfloat16)
    in_weight = noise(keys[4], (D, 3, D), D ** -0.5, 0.125, ((0, 8), (2, 4)))
    conv_taps = jnp.clip(jax.random.uniform(keys[5], (3, D), jnp.float32, -1.0, 1.0) * level_of(keys[5], (3, D), ((1, 4),), -0.4, 0.0), -1.0, 1.0).astype(jnp.bfloat16)
    out_weight = noise(keys[6], (D, D), D ** -0.5, 0.125, ((0, 4), (1, 8)))
    norm2_gain = jnp.clip(1.0 + 0.15 * jax.random.normal(keys[7], (D,), jnp.float32), 0.25, 1.75).astype(jnp.bfloat16)
    gate_weight = noise(keys[8], (D, FF), D ** -0.5, 0.125, ((0, 8), (1, 4)))
    up_weight = noise(keys[9], (D, FF), D ** -0.5, 0.125, ((0, 8), (1, 4)))
    down_weight = noise(keys[10], (FF, D), (FF // 4) ** -0.5, 0.125, ((0, 4), (1, 8)))
    return {"tokens": tokens, "cotangent": cotangent, "lengths": lengths, "norm1_gain": norm1_gain, "in_weight": in_weight, "conv_taps": conv_taps, "out_weight": out_weight, "norm2_gain": norm2_gain, "gate_weight": gate_weight, "up_weight": up_weight, "down_weight": down_weight}


@jax.custom_vjp
def low(v):
    return lax.optimization_barrier(v.astype(jnp.bfloat16)).astype(jnp.float32)

@jax.custom_vjp
def low_back(v):
    return v

def low_keep(v):
    return (low(v), None)

def low_pass(kept, grad):
    return (grad,)

def back_keep(v):
    return (v, None)

def back_low(kept, grad):
    return (low(grad),)
low.defvjp(low_keep, low_pass)
low_back.defvjp(back_keep, back_low)
norm_eps = 1e-05

def product(left, right):
    return jnp.dot(left, right, precision=lax.Precision.HIGHEST, preferred_element_type=jnp.float32)

def rms_scale(values):
    return lax.rsqrt(lax.optimization_barrier(jnp.mean(values * values, axis=-1, keepdims=True)) + norm_eps)

def line_forward(inputs_f, gain_one, in_full, taps_full, out_full, gain_two, gate_full, up_full, down_full, live_mask, position):
    model_width = inputs_f.shape[1]
    slot_count = inputs_f.shape[0]
    normed_one = low(inputs_f * rms_scale(inputs_f) * gain_one)
    projected = low_back(product(normed_one, in_full.reshape(model_width, 3 * model_width))).reshape(slot_count, 3, model_width)
    b_part = projected[:, 0]
    c_part = projected[:, 1]
    x_part = projected[:, 2]
    mixed_in = b_part * x_part
    padded = jnp.concatenate([jnp.zeros((2, model_width), jnp.float32), mixed_in], 0)
    convolved = jnp.zeros_like(mixed_in)
    for tap_index in range(3):
        valid_tap = (position >= tap_index).astype(jnp.float32)[:, None]
        convolved = convolved + taps_full[tap_index] * padded[2 - tap_index:2 - tap_index + slot_count] * valid_tap
    gated = low(c_part * convolved)
    mixer_out = low_back(product(gated, out_full))
    hidden_one = inputs_f + mixer_out
    normed_two = low(hidden_one * rms_scale(hidden_one) * gain_two)
    gate_pre = low_back(product(normed_two, gate_full))
    up_pre = low_back(product(normed_two, up_full))
    inner_act = low(jax.nn.silu(gate_pre) * up_pre)
    ffn_out = low_back(product(inner_act, down_full))
    return live_mask * (hidden_one + ffn_out)

def reference(tokens, cotangent, lengths, norm1_gain, in_weight, conv_taps, out_weight, norm2_gain, gate_weight, up_weight, down_weight):
    weights_f = (norm1_gain.astype(jnp.float32), in_weight.astype(jnp.float32), conv_taps.astype(jnp.float32), out_weight.astype(jnp.float32), norm2_gain.astype(jnp.float32), gate_weight.astype(jnp.float32), up_weight.astype(jnp.float32), down_weight.astype(jnp.float32))
    line_count = MICRO * GROUPS
    line_tokens = tokens.reshape(line_count, LINE, D)
    line_cot = cotangent.reshape(line_count, LINE, D)
    line_lens = lengths.reshape(line_count, LINE // SEQ_LEN)
    slot_index = jnp.arange(LINE, dtype=jnp.int32)
    position = slot_index % SEQ_LEN
    seq_of = slot_index // SEQ_LEN

    def scan_step(totals, line_item):
        token_line, cot_line, len_line = line_item
        live_mask = (position < len_line[seq_of]).astype(jnp.float32)[:, None]

        def forward_fn(inputs_f, *weights):
            return line_forward(inputs_f, *weights, live_mask, position)
        result, pullback = jax.vjp(forward_fn, token_line.astype(jnp.float32), *weights_f)
        gradients = pullback(cot_line.astype(jnp.float32))
        totals = tuple((total + grad_part for total, grad_part in zip(totals, gradients[1:])))
        return (totals, (result.astype(jnp.bfloat16), gradients[0].astype(jnp.bfloat16)))
    initial = tuple((jnp.zeros_like(weight) for weight in weights_f))
    totals, (results, input_grads) = lax.scan(scan_step, initial, (line_tokens, line_cot, line_lens))
    return (results.reshape(tokens.shape), input_grads.reshape(tokens.shape), totals[0], totals[1], totals[2], totals[3], totals[4], totals[5], totals[6], totals[7])
```

```python
import jax
import jax.numpy as jnp
from jax import lax
from jax.sharding import PartitionSpec as P

SEQ_LEN = 1024
TAPS = 3

norm_eps = 1e-05
f32 = jnp.float32
bf16 = jnp.bfloat16


def passed_along(value, axis, steps):
    count = lax.axis_size(axis)
    first, last = (max(0, -steps), min(count, count - steps))
    return lax.ppermute(value, axis, [(source, source + steps) for source in range(first, last)])


def passed_round(value, axis):
    count = lax.axis_size(axis)
    return lax.ppermute(value, axis, [(source, (source + 1) % count) for source in range(count)])


def ring_gather(value, axis):
    chunks = [value]
    for _ in range(lax.axis_size(axis) - 1):
        chunks.append(passed_round(chunks[-1], axis))
    return chunks


def ring_collect(terms, axis):
    count = lax.axis_size(axis)
    total = terms[1 % count]
    for step in range(1, count):
        moved = passed_round(total.astype(bf16), axis)
        total = moved.astype(f32) + terms[(step + 1) % count]
    return total


def rms_scale(values):
    return lax.rsqrt(jnp.mean(values * values, axis=-1, keepdims=True) + norm_eps)


def times(left, right):
    return jnp.dot(left, right, preferred_element_type=f32)


def times_transposed(left, right):
    return lax.dot_general(left, right, (((1,), (1,)), ((), ())), preferred_element_type=f32)


def contract_rows(left, right):
    return lax.dot_general(left, right, (((0,), (0,)), ((), ())), preferred_element_type=f32)


def shards(
    tokens,
    cotangent,
    lengths,
    norm1_gain,
    in_weight,
    conv_taps,
    out_weight,
    norm2_gain,
    gate_weight,
    up_weight,
    down_weight,
):
    micro_count, group_count, span_len, model_width = tokens.shape
    line_count = micro_count * group_count
    row_count = line_count * span_len
    local_width = conv_taps.shape[1]
    slot_index = lax.axis_index("dp") * span_len + jnp.arange(span_len, dtype=jnp.int32)
    position = slot_index % SEQ_LEN
    seq_count = lengths.shape[2]
    seq_pick = (
        slot_index[:, None] // SEQ_LEN == jnp.arange(seq_count, dtype=jnp.int32)[None, :]
    ).astype(jnp.int32)
    valid_taps = [(position >= tap).astype(f32)[None, :, None] for tap in range(TAPS)]
    taps_f = conv_taps.astype(f32)

    def from_owners(value):
        return lax.all_gather(value, "dp", axis=0, tiled=True)

    def to_owners(value):
        return lax.psum_scatter(value.astype(bf16), "dp", scatter_dimension=0, tiled=True).astype(f32)

    gains = from_owners(jnp.stack([norm1_gain, norm2_gain], 1)).astype(f32)
    gain_one, gain_two = gains[:, 0], gains[:, 1]
    in_full = from_owners(in_weight.reshape(in_weight.shape[0], -1))
    out_back = from_owners(out_weight.T)
    gate_full = from_owners(gate_weight)
    up_full = from_owners(up_weight)
    down_back = from_owners(down_weight.T)

    inputs_f = tokens.reshape(row_count, model_width).astype(f32)
    lens = lengths.reshape(line_count, seq_count)
    seq_lens = jnp.sum(seq_pick[None, :, :] * lens[:, None, :], axis=2)
    live_mask = (position[None, :] < seq_lens).astype(f32).reshape(row_count, 1)
    scale_one = rms_scale(inputs_f)
    sens_own = live_mask * cotangent.reshape(row_count, model_width).astype(f32)

    normed_one = ring_gather((inputs_f * scale_one * gain_one).astype(bf16), "fsdp")
    sens_all = ring_gather(sens_own.astype(bf16), "fsdp")

    kept = []
    terms = []
    for normed in normed_one:
        projected = times(normed, in_full)
        b_part = projected[:, :local_width]
        c_part = projected[:, local_width : 2 * local_width]
        x_part = projected[:, 2 * local_width :]
        mixed_in = (b_part * x_part).reshape(line_count, span_len, local_width)
        rim_in = passed_along(mixed_in[:, span_len - (TAPS - 1) :], "dp", 1)
        padded = jnp.concatenate([rim_in, mixed_in], 1)
        convolved = jnp.zeros_like(mixed_in)
        for tap in range(TAPS):
            convolved = (
                convolved
                + taps_f[tap][None, None, :]
                * padded[:, TAPS - 1 - tap : TAPS - 1 - tap + span_len]
                * valid_taps[tap]
            )
        convolved = convolved.reshape(row_count, local_width)
        gated = (c_part * convolved).astype(bf16)
        kept.append((b_part, c_part, x_part, padded, convolved, gated))
        terms.append(times_transposed(gated, out_back))
    hidden_one = inputs_f + ring_collect(terms, "fsdp")
    scale_two = rms_scale(hidden_one)
    normed_two = ring_gather((hidden_one * scale_two * gain_two).astype(bf16), "fsdp")

    inner, d_gates, d_ups, terms, back_terms = [], [], [], [], []
    for normed, sens in zip(normed_two, sens_all):
        gate_pre = times(normed, gate_full)
        up_pre = times(normed, up_full)
        sigmoid_gate = jax.nn.sigmoid(gate_pre)
        silu_gate = gate_pre * sigmoid_gate
        inner.append((silu_gate * up_pre).astype(bf16))
        terms.append(times_transposed(inner[-1], down_back))
        d_inner = times(sens, down_back)
        d_gates.append(
            (d_inner * up_pre * (sigmoid_gate * (1.0 + gate_pre * (1.0 - sigmoid_gate)))).astype(bf16)
        )
        d_ups.append((d_inner * silu_gate).astype(bf16))
        back_terms.append(
            times_transposed(d_gates[-1], gate_full) + times_transposed(d_ups[-1], up_full)
        )
    d_normed_two = ring_collect(back_terms, "fsdp")
    ffn_out = ring_collect(terms, "fsdp")
    block_out = (live_mask * (hidden_one + ffn_out)).astype(bf16)

    gain_two_part = jnp.sum(d_normed_two * hidden_one * scale_two, axis=0)
    d_hidden = (
        sens_own
        + scale_two * gain_two * d_normed_two
        - hidden_one
        * scale_two**3
        * jnp.mean(hidden_one * gain_two * d_normed_two, axis=-1, keepdims=True)
    )
    d_mix = ring_gather(d_hidden.astype(bf16), "fsdp")

    sens_rows = jnp.concatenate(sens_all, 0)
    down_grad = to_owners(contract_rows(sens_rows, jnp.concatenate(inner, 0))).T
    normed_rows = jnp.concatenate(normed_two, 0)
    gate_grad = to_owners(contract_rows(normed_rows, jnp.concatenate(d_gates, 0)))
    up_grad = to_owners(contract_rows(normed_rows, jnp.concatenate(d_ups, 0)))

    taps_part = jnp.zeros((TAPS, local_width), f32)
    d_projs, terms = [], []
    for d_mixed_out, (b_part, c_part, x_part, padded, convolved, gated) in zip(d_mix, kept):
        d_gated = times(d_mixed_out, out_back)
        d_c_part = d_gated * convolved
        d_conv = (d_gated * c_part).reshape(line_count, span_len, local_width)
        d_padded = jnp.zeros_like(padded)
        tap_rows = []
        for tap in range(TAPS):
            weighted = d_conv * valid_taps[tap]
            d_padded = d_padded + jnp.pad(
                taps_f[tap][None, None, :] * weighted,
                ((0, 0), (TAPS - 1 - tap, tap), (0, 0)),
            )
            tap_rows.append(
                jnp.sum(weighted * padded[:, TAPS - 1 - tap : TAPS - 1 - tap + span_len], axis=(0, 1))
            )
        taps_part = taps_part + jnp.stack(tap_rows, 0)
        rim_back = passed_along(d_padded[:, : TAPS - 1], "dp", -1)
        d_mixed = (
            d_padded[:, TAPS - 1 :]
            + jnp.pad(rim_back, ((0, 0), (span_len - (TAPS - 1), 0), (0, 0)))
        ).reshape(row_count, local_width)
        d_projs.append(
            jnp.concatenate([d_mixed * x_part, d_c_part, d_mixed * b_part], axis=1).astype(bf16)
        )
        terms.append(times_transposed(d_projs[-1], in_full))

    out_grad = to_owners(
        contract_rows(jnp.concatenate(d_mix, 0), jnp.concatenate([k[5] for k in kept], 0))
    ).T
    in_grad = to_owners(
        contract_rows(jnp.concatenate(normed_one, 0), jnp.concatenate(d_projs, 0))
    ).reshape(in_weight.shape)

    d_normed_one = ring_collect(terms, "fsdp")
    gain_one_part = jnp.sum(d_normed_one * inputs_f * scale_one, axis=0)
    token_grad = (
        d_hidden
        + scale_one * gain_one * d_normed_one
        - inputs_f
        * scale_one**3
        * jnp.mean(inputs_f * gain_one * d_normed_one, axis=-1, keepdims=True)
    ).astype(bf16)
    gain_grads = lax.psum_scatter(
        jnp.stack([gain_one_part, gain_two_part], 1), "dp", scatter_dimension=0, tiled=True
    )
    gain_grads = lax.psum(gain_grads, "fsdp")
    taps_grad = lax.psum(taps_part, "dp")
    return (
        block_out.reshape(tokens.shape),
        token_grad.reshape(tokens.shape),
        gain_grads[:, 0],
        in_grad,
        taps_grad,
        out_grad,
        gain_grads[:, 1],
        gate_grad,
        up_grad,
        down_grad,
    )


def solution(mesh):
    rows = P(None, "fsdp", "dp", None)
    return jax.shard_map(
        shards,
        mesh=mesh,
        in_specs=(
            rows,
            rows,
            P(None, "fsdp", None),
            P("dp"),
            P("dp", None, "fsdp"),
            P(None, "fsdp"),
            P("fsdp", "dp"),
            P("dp"),
            P("dp", "fsdp"),
            P("dp", "fsdp"),
            P("fsdp", "dp"),
        ),
        out_specs=(
            rows,
            rows,
            P("dp"),
            P("dp", None, "fsdp"),
            P(None, "fsdp"),
            P("fsdp", "dp"),
            P("dp"),
            P("dp", "fsdp"),
            P("dp", "fsdp"),
            P("fsdp", "dp"),
        ),
        check_vma=False,
    )
```

```python
import jax
import jax.numpy as jnp
from jax import lax
from jax.experimental import pallas as pl
from jax.experimental.pallas import tpu as pltpu
from jax.sharding import PartitionSpec as P

SEQ_LEN = 1024
TAPS = 3

norm_eps = 1e-05
f32 = jnp.float32
bf16 = jnp.bfloat16


def passed_along(value, axis, steps):
    count = lax.axis_size(axis)
    first, last = (max(0, -steps), min(count, count - steps))
    return lax.ppermute(value, axis, [(source, source + steps) for source in range(first, last)])


def passed_round(value, axis):
    count = lax.axis_size(axis)
    return lax.ppermute(value, axis, [(source, (source + 1) % count) for source in range(count)])


def ring_gather(value, axis):
    chunks = [value]
    for _ in range(lax.axis_size(axis) - 1):
        chunks.append(passed_round(chunks[-1], axis))
    return chunks


def ring_collect(terms, axis):
    count = lax.axis_size(axis)
    total = terms[1 % count]
    for step in range(1, count):
        moved = passed_round(total.astype(bf16), axis)
        total = moved.astype(f32) + terms[(step + 1) % count]
    return total


def rms_scale(values):
    return lax.rsqrt(jnp.mean(values * values, axis=-1, keepdims=True) + norm_eps)


def times(left, right):
    return jnp.dot(left, right, preferred_element_type=f32)


def times_transposed(left, right):
    return lax.dot_general(left, right, (((1,), (1,)), ((), ())), preferred_element_type=f32)


def contract_rows(left, right):
    return lax.dot_general(left, right, (((0,), (0,)), ((), ())), preferred_element_type=f32)


def ffn_kernel(a_ref, e_ref, gate_ref, up_ref, down_ref, m_ref, dg_ref, du_ref, out_ref, da_ref):
    @pl.when(pl.program_id(0) == 0)
    def _():
        out_ref[...] = jnp.zeros_like(out_ref)
        da_ref[...] = jnp.zeros_like(da_ref)

    rows, sens = a_ref[...], e_ref[...]
    gate_pre = times(rows, gate_ref[...])
    up_pre = times(rows, up_ref[...])
    d_inner = times(sens, down_ref[...])
    sigmoid_gate = 1.0 / (1.0 + jnp.exp(-gate_pre))
    silu_gate = gate_pre * sigmoid_gate
    inner = (silu_gate * up_pre).astype(bf16)
    d_gate = (d_inner * up_pre * (sigmoid_gate * (1.0 + gate_pre * (1.0 - sigmoid_gate)))).astype(bf16)
    d_up = (d_inner * silu_gate).astype(bf16)
    m_ref[...] = inner
    dg_ref[...] = d_gate
    du_ref[...] = d_up
    out_ref[...] += times_transposed(inner, down_ref[...])
    da_ref[...] += times_transposed(d_gate, gate_ref[...]) + times_transposed(d_up, up_ref[...])


def ffn_chunk(normed, sens, gate_full, up_full, down_back, tile=512):
    rows, width = normed.shape
    hidden = gate_full.shape[1]
    whole = pl.BlockSpec((rows, width), lambda i: (0, 0))
    weight = pl.BlockSpec((width, tile), lambda i: (0, i))
    part = pl.BlockSpec((rows, tile), lambda i: (0, i))
    act = jax.ShapeDtypeStruct((rows, hidden), bf16)
    total = jax.ShapeDtypeStruct((rows, width), f32)
    return pl.pallas_call(
        ffn_kernel,
        grid=(hidden // tile,),
        in_specs=[whole, whole, weight, weight, weight],
        out_specs=[part, part, part, whole, whole],
        out_shape=[act, act, act, total, total],
        compiler_params=pltpu.CompilerParams(vmem_limit_bytes=48 * 2**20),
        cost_estimate=pl.CostEstimate(
            flops=12 * rows * width * hidden,
            bytes_accessed=6 * width * hidden + 12 * rows * width + 6 * rows * hidden,
            transcendentals=rows * hidden,
        ),
    )(normed, sens, gate_full, up_full, down_back)


def swapped(value, axis, offset):
    count = lax.axis_size(axis)
    return lax.ppermute(value, axis, [(source, source ^ offset) for source in range(count)])


CORE, XLINK, YLINK = 1, 2, 4


def gather_cube(shard, widths):
    if lax.axis_size("dp") != 8:
        full = lax.all_gather(shard, "dp", axis=0, tiled=True)
        ends = [sum(widths[: i + 1]) for i in range(len(widths))]
        return [full[:, end - width : end] for end, width in zip(ends, widths)]
    rows = shard.shape[0]
    half = rows // 2
    over_x = swapped(shard, "dp", XLINK)
    over_y = swapped(shard, "dp", YLINK)
    diag_top = swapped(over_x[:half], "dp", YLINK)
    diag_low = swapped(over_y[half:], "dp", XLINK)
    pieces = [
        (shard, 0, 0),
        (over_x, XLINK, 0),
        (over_y, YLINK, 0),
        (diag_top, XLINK | YLINK, 0),
        (diag_low, XLINK | YLINK, half),
    ]
    pieces += [(swapped(v, "dp", CORE), offset ^ CORE, at) for v, offset, at in pieces]

    count = len(pieces)

    def kernel(*refs):
        ins, outs = refs[:count], refs[count : count + len(widths)]
        held, in_sems, out_sems = refs[count + len(widths) :]
        me = lax.axis_index("dp")
        copies = []
        for i, (value, offset, at) in enumerate(pieces):
            start = pl.multiple_of(lax.bitwise_xor(me, offset) * rows + at, half)
            copies.append(
                pltpu.make_async_copy(
                    ins[i], held.at[pl.ds(start, value.shape[0]), :], in_sems.at[i]
                )
            )
        for copy in copies:
            copy.start()
        for copy in copies:
            copy.wait()
        copies, first = [], 0
        for j, width in enumerate(widths):
            copies.append(
                pltpu.make_async_copy(held.at[:, pl.ds(first, width)], outs[j], out_sems.at[j])
            )
            first += width
        for copy in copies:
            copy.start()
        for copy in copies:
            copy.wait()

    spec = pl.BlockSpec(memory_space=pl.ANY)
    return pl.pallas_call(
        kernel,
        in_specs=[spec] * count,
        out_specs=[spec] * len(widths),
        out_shape=[jax.ShapeDtypeStruct((8 * rows, width), shard.dtype) for width in widths],
        scratch_shapes=[
            pltpu.VMEM((8 * rows, sum(widths)), shard.dtype),
            pltpu.SemaphoreType.DMA((count,)),
            pltpu.SemaphoreType.DMA((len(widths),)),
        ],
        cost_estimate=pl.CostEstimate(
            flops=0, bytes_accessed=32 * rows * sum(widths), transcendentals=0
        ),
    )(*[value for value, _, _ in pieces])


def pick(value, axis, index):
    return lax.dynamic_index_in_dim(value, index, axis, keepdims=False)


def mixer_grad_kernel(order_ref, na_ref, da_ref, nb_ref, db_ref, proj_ref, gated_ref, keep_ref, send_ref):
    width = proj_ref.shape[1]
    keep_ref[0, :, :width] = contract_rows(na_ref[...], proj_ref[...]).astype(bf16)
    keep_ref[0, :, width:] = contract_rows(da_ref[...], gated_ref[...]).astype(bf16)
    send_ref[0, :, :width] = contract_rows(nb_ref[...], proj_ref[...]).astype(bf16)
    send_ref[0, :, width:] = contract_rows(db_ref[...], gated_ref[...]).astype(bf16)


def mixer_grad(normed, d_mix, d_proj, gated, piece):
    width = d_proj.shape[1] + gated.shape[1]
    if lax.axis_size("dp") != 8:
        part = jnp.concatenate([contract_rows(normed, d_proj), contract_rows(d_mix, gated)], 1)
        return lax.psum_scatter(part.astype(bf16), "dp", scatter_dimension=0, tiled=True).astype(f32)
    rows = normed.shape[0]
    half = piece // 2
    me = lax.axis_index("dp")
    order = jnp.stack([me % 2, me // 2]).astype(jnp.int32)
    kept = pl.BlockSpec((rows, piece), lambda i, o: (0, 2 * (i ^ o[1]) + o[0]))
    sent = pl.BlockSpec((rows, piece), lambda i, o: (0, 2 * (i ^ o[1]) + 1 - o[0]))
    out = pl.BlockSpec((1, piece, width), lambda i, o: (i, 0, 0))
    chip = jax.ShapeDtypeStruct((4, piece, width), bf16)
    keep, send = pl.pallas_call(
        mixer_grad_kernel,
        grid_spec=pltpu.PrefetchScalarGridSpec(
            num_scalar_prefetch=1,
            grid=(4,),
            in_specs=[
                kept,
                kept,
                sent,
                sent,
                pl.BlockSpec(d_proj.shape, lambda i, o: (0, 0)),
                pl.BlockSpec(gated.shape, lambda i, o: (0, 0)),
            ],
            out_specs=[out, out],
        ),
        out_shape=[chip, chip],
        compiler_params=pltpu.CompilerParams(vmem_limit_bytes=40 * 2**20),
        cost_estimate=pl.CostEstimate(
            flops=16 * rows * piece * width,
            bytes_accessed=16 * piece * width + 64 * rows * piece,
            transcendentals=0,
        ),
    )(order, normed, d_mix, normed, d_mix, d_proj, gated)
    own, over_x, over_y, diag = keep.astype(f32) + swapped(send, "dp", CORE).astype(f32)
    top = swapped(diag[:half].astype(bf16), "dp", XLINK)
    low = swapped(diag[half:].astype(bf16), "dp", YLINK)
    over_x = jnp.concatenate([over_x[:half], over_x[half:] + low.astype(f32)], 0).astype(bf16)
    over_y = jnp.concatenate([over_y[:half] + top.astype(f32), over_y[half:]], 0).astype(bf16)
    return (
        own
        + swapped(over_x, "dp", XLINK).astype(f32)
        + swapped(over_y, "dp", YLINK).astype(f32)
    )


def total_all(value, axis):
    count = lax.axis_size(axis)
    offset = 1
    while offset < count:
        value = value + swapped(value, axis, offset)
        offset *= 2
    return value


def total_blocks(value, axis):
    count = lax.axis_size(axis)
    me = lax.axis_index(axis)
    offset = count // 2
    while offset:
        mine = me // offset % 2
        value = value.reshape((2, -1) + value.shape[1:])
        value = pick(value, 0, mine) + swapped(pick(value, 0, 1 - mine), axis, offset)
        offset //= 2
    return value[0]


def shards(
    tokens,
    cotangent,
    lengths,
    norm1_gain,
    in_weight,
    conv_taps,
    out_weight,
    norm2_gain,
    gate_weight,
    up_weight,
    down_weight,
):
    micro_count, group_count, span_len, model_width = tokens.shape
    line_count = micro_count * group_count
    row_count = line_count * span_len
    local_width = conv_taps.shape[1]
    piece = in_weight.shape[0]
    ring = lax.axis_size("fsdp")
    slices = range(0, ring, 2)
    my_line = lax.axis_index("fsdp")
    my_span = lax.axis_index("dp")
    slot_index = my_span * span_len + jnp.arange(span_len, dtype=jnp.int32)
    position = slot_index % SEQ_LEN
    seq_count = lengths.shape[2]
    seq_pick = (
        slot_index[:, None] // SEQ_LEN == jnp.arange(seq_count, dtype=jnp.int32)[None, :]
    ).astype(jnp.int32)
    valid_taps = [(position >= tap).astype(f32)[None, :, None] for tap in range(TAPS)]

    def from_owners(value):
        return lax.all_gather(value, "dp", axis=0, tiled=True)

    def to_owners(value):
        return lax.psum_scatter(value, "dp", scatter_dimension=0, tiled=True)

    gains = from_owners(jnp.stack([norm1_gain, norm2_gain], 1)).astype(f32)
    gain_one, gain_two = gains[:, 0], gains[:, 1]
    mixer_shard = jnp.concatenate([in_weight.reshape(piece, -1), out_weight.T], 1)
    gain_one, mixer_shard, gate_weight, up_weight, down_weight = lax.optimization_barrier(
        (gain_one, mixer_shard, gate_weight, up_weight, down_weight)
    )
    gate_full = from_owners(gate_weight)
    up_full = from_owners(up_weight)
    down_back = from_owners(down_weight.T)

    inputs_f = tokens.reshape(row_count, model_width).astype(f32)
    lens = lengths.reshape(line_count, seq_count)
    seq_lens = jnp.sum(seq_pick[None, :, :] * lens[:, None, :], axis=2)
    live_mask = (position[None, :] < seq_lens).astype(f32).reshape(row_count, 1)
    scale_one = rms_scale(inputs_f)
    sens_own = live_mask * cotangent.reshape(row_count, model_width).astype(f32)

    shards_of = [mixer_shard] + [swapped(mixer_shard, "fsdp", c) for c in slices[1:]]
    taps_of = [conv_taps] + [swapped(conv_taps, "fsdp", c) for c in slices[1:]]
    normed_own = (inputs_f * scale_one * gain_one).astype(bf16)
    normed_pair = jnp.concatenate([normed_own, swapped(normed_own, "fsdp", 1)], 0)
    sens_low, shards_of[-1] = lax.optimization_barrier((sens_own.astype(bf16), shards_of[-1]))
    sens_all = ring_gather(sens_low, "fsdp")

    pair_lines, pair_rows = 2 * line_count, 2 * row_count
    kept = []
    mixed = jnp.zeros((pair_rows, model_width), f32)
    for shard, taps in zip(shards_of, taps_of):
        in_full, out_back = gather_cube(shard, (3 * local_width, local_width))
        taps_f = taps.astype(f32)
        if kept:
            normed_pair, sens_all[ring // 2] = lax.optimization_barrier(
                (normed_pair, sens_all[ring // 2])
            )
        projected = times(normed_pair, in_full)
        b_part = projected[:, :local_width]
        c_part = projected[:, local_width : 2 * local_width]
        x_part = projected[:, 2 * local_width :]
        mixed_in = (b_part * x_part).reshape(pair_lines, span_len, local_width)
        rim_in = passed_along(mixed_in[:, span_len - (TAPS - 1) :], "dp", 1)
        padded = jnp.concatenate([rim_in, mixed_in], 1)
        convolved = jnp.zeros_like(mixed_in)
        for tap in range(TAPS):
            convolved = (
                convolved
                + taps_f[tap][None, None, :]
                * padded[:, TAPS - 1 - tap : TAPS - 1 - tap + span_len]
                * valid_taps[tap]
            )
        convolved = convolved.reshape(pair_rows, local_width)
        gated = (c_part * convolved).astype(bf16)
        kept.append((in_full, out_back, taps_f, b_part, c_part, x_part, padded, convolved, gated))
        mixed = mixed + times_transposed(gated, out_back)
    mixed, sens_all[-1] = lax.optimization_barrier((mixed, sens_all[-1]))
    moved = swapped(mixed[row_count:].astype(bf16), "fsdp", 1)
    hidden_one = inputs_f + mixed[:row_count] + moved.astype(f32)
    scale_two = rms_scale(hidden_one)
    normed = (hidden_one * scale_two * gain_two).astype(bf16)

    normed_two, inner, d_gates, d_ups, terms, back_terms = [], [], [], [], [], []
    for step, sens in enumerate(sens_all):
        normed_two.append(normed)
        coming = passed_round(normed, "fsdp") if step < ring - 1 else None
        inner_part, d_gate, d_up, term, back_term = ffn_chunk(
            normed, sens, gate_full, up_full, down_back
        )
        if step < ring - 1:
            normed, d_up = lax.optimization_barrier((coming, d_up))
        inner.append(inner_part)
        d_gates.append(d_gate)
        d_ups.append(d_up)
        terms.append(term)
        back_terms.append(back_term)
    sens_rows = jnp.concatenate(sens_all, 0)
    normed_rows = jnp.concatenate(normed_two, 0)
    down_part = contract_rows(sens_rows, jnp.concatenate(inner, 0)).astype(bf16)
    gate_part = contract_rows(normed_rows, jnp.concatenate(d_gates, 0)).astype(bf16)
    up_part = contract_rows(normed_rows, jnp.concatenate(d_ups, 0)).astype(bf16)
    back_terms[0], down_part, gate_part = lax.optimization_barrier(
        (back_terms[0], down_part, gate_part)
    )
    d_normed_two = ring_collect(back_terms, "fsdp")

    gain_two_part = jnp.sum(d_normed_two * hidden_one * scale_two, axis=0)
    d_hidden = (
        sens_own
        + scale_two * gain_two * d_normed_two
        - hidden_one
        * scale_two**3
        * jnp.mean(hidden_one * gain_two * d_normed_two, axis=-1, keepdims=True)
    )
    d_hidden_low, up_part = lax.optimization_barrier((d_hidden.astype(bf16), up_part))
    d_mix = jnp.concatenate([d_hidden_low, swapped(d_hidden_low, "fsdp", 1)], 0)
    d_mix, terms[1] = lax.optimization_barrier((d_mix, terms[1]))
    down_grad = to_owners(down_part).astype(f32).T
    gate_grad = to_owners(gate_part).astype(f32)
    up_grad = to_owners(up_part).astype(f32)

    tap_parts, d_projs = [], []
    d_normed = jnp.zeros((pair_rows, model_width), f32)
    for in_full, out_back, taps_f, b_part, c_part, x_part, padded, convolved, gated in kept[::-1]:
        d_gated = times(d_mix, out_back)
        d_c_part = d_gated * convolved
        d_conv = (d_gated * c_part).reshape(pair_lines, span_len, local_width)
        d_padded = jnp.zeros_like(padded)
        tap_rows = []
        for tap in range(TAPS):
            weighted = d_conv * valid_taps[tap]
            d_padded = d_padded + jnp.pad(
                taps_f[tap][None, None, :] * weighted,
                ((0, 0), (TAPS - 1 - tap, tap), (0, 0)),
            )
            tap_rows.append(
                jnp.sum(weighted * padded[:, TAPS - 1 - tap : TAPS - 1 - tap + span_len], axis=(0, 1))
            )
        tap_parts.append(jnp.stack(tap_rows, 0))
        rim_back = passed_along(d_padded[:, : TAPS - 1], "dp", -1)
        d_mixed = (
            d_padded[:, TAPS - 1 :]
            + jnp.pad(rim_back, ((0, 0), (span_len - (TAPS - 1), 0), (0, 0)))
        ).reshape(pair_rows, local_width)
        d_proj = jnp.concatenate([d_mixed * x_part, d_c_part, d_mixed * b_part], axis=1).astype(bf16)
        d_normed = d_normed + times_transposed(d_proj, in_full)
        d_projs.append(d_proj)
    moved = swapped(d_normed[row_count:].astype(bf16), "fsdp", 1)
    d_normed_one = d_normed[:row_count] + moved.astype(f32)
    gain_one_part = jnp.sum(d_normed_one * inputs_f * scale_one, axis=0)
    token_grad = (
        d_hidden
        + scale_one * gain_one * d_normed_one
        - inputs_f
        * scale_one**3
        * jnp.mean(inputs_f * gain_one * d_normed_one, axis=-1, keepdims=True)
    ).astype(bf16)

    mixer_sum = jnp.zeros((), f32)
    for c, d_proj, saved in zip(slices[::-1], d_projs, kept[::-1]):
        grad = mixer_grad(normed_pair, d_mix, d_proj, saved[-1], piece)
        mixer_sum = mixer_sum + (swapped(grad.astype(bf16), "fsdp", c).astype(f32) if c else grad)
    in_grad = mixer_sum[:, : 3 * local_width].reshape(in_weight.shape)
    out_grad = mixer_sum[:, 3 * local_width :].T

    ffn_out = ring_collect(terms, "fsdp")
    block_out = (live_mask * (hidden_one + ffn_out)).astype(bf16)

    taps_sum = tap_parts[-1]
    for c, part in list(zip(slices[::-1], tap_parts))[:-1]:
        taps_sum = taps_sum + swapped(part, "fsdp", c)
    taps_grad = total_all(taps_sum, "dp")
    gain_grads = total_blocks(
        jnp.concatenate(
            [gain_one_part.reshape(-1, piece), gain_two_part.reshape(-1, piece)], 1
        ),
        "dp",
    )
    gain_grads = total_all(gain_grads, "fsdp").reshape(2, piece)
    return (
        block_out.reshape(tokens.shape),
        token_grad.reshape(tokens.shape),
        gain_grads[0],
        in_grad,
        taps_grad,
        out_grad,
        gain_grads[1],
        gate_grad,
        up_grad,
        down_grad,
    )


def solution(mesh):
    rows = P(None, "fsdp", "dp", None)
    return jax.shard_map(
        shards,
        mesh=mesh,
        in_specs=(
            rows,
            rows,
            P(None, "fsdp", None),
            P("dp"),
            P("dp", None, "fsdp"),
            P(None, "fsdp"),
            P("fsdp", "dp"),
            P("dp"),
            P("dp", "fsdp"),
            P("dp", "fsdp"),
            P("fsdp", "dp"),
        ),
        out_specs=(
            rows,
            rows,
            P("dp"),
            P("dp", None, "fsdp"),
            P(None, "fsdp"),
            P("fsdp", "dp"),
            P("dp"),
            P("dp", "fsdp"),
            P("dp", "fsdp"),
            P("fsdp", "dp"),
        ),
        check_vma=False,
    )
```

```python
import functools

import jax
import jax.numpy as jnp
from jax import lax
from jax.experimental import pallas as pl
from jax.experimental.pallas import tpu as pltpu
from jax.sharding import PartitionSpec as P

SEQ_LEN = 1024
TAPS = 3

norm_eps = 1e-05
f32 = jnp.float32
bf16 = jnp.bfloat16


def passed_along(value, axis, steps):
    count = lax.axis_size(axis)
    first, last = (max(0, -steps), min(count, count - steps))
    return lax.ppermute(value, axis, [(source, source + steps) for source in range(first, last)])


def passed_round(value, axis):
    count = lax.axis_size(axis)
    return lax.ppermute(value, axis, [(source, (source + 1) % count) for source in range(count)])


def ring_gather(value, axis):
    chunks = [value]
    for _ in range(lax.axis_size(axis) - 1):
        chunks.append(passed_round(chunks[-1], axis))
    return chunks


def ring_collect(terms, axis):
    count = lax.axis_size(axis)
    total = terms[1 % count]
    for step in range(1, count):
        moved = passed_round(total.astype(bf16), axis)
        total = wide(moved, terms[(step + 1) % count])
    return total


def rms_scale(values):
    return lax.rsqrt(jnp.mean(values * values, axis=-1, keepdims=True) + norm_eps)


def times(left, right):
    return jnp.dot(left, right, preferred_element_type=f32)


def times_transposed(left, right):
    return lax.dot_general(left, right, (((1,), (1,)), ((), ())), preferred_element_type=f32)


def contract_rows(left, right):
    return lax.dot_general(left, right, (((0,), (0,)), ((), ())), preferred_element_type=f32)


def ffn_kernel(a_ref, e_ref, gate_ref, up_ref, down_ref, *refs):
    m_ref, dg_ref, du_ref, term_ref, da_ref, out_ref = refs[-6:]

    @pl.when(pl.program_id(0) == 0)
    def _():
        out_ref[...] = jnp.zeros_like(out_ref)
        da_ref[...] = jnp.zeros_like(da_ref)

    rows, sens = a_ref[...], e_ref[...]
    gate_pre = times(rows, gate_ref[...])
    up_pre = times(rows, up_ref[...])
    d_inner = times(sens, down_ref[...])
    sigmoid_gate = 1.0 / (1.0 + jnp.exp(-gate_pre))
    silu_gate = gate_pre * sigmoid_gate
    inner = (silu_gate * up_pre).astype(bf16)
    d_gate = (d_inner * up_pre * (sigmoid_gate * (1.0 + gate_pre * (1.0 - sigmoid_gate)))).astype(bf16)
    d_up = (d_inner * silu_gate).astype(bf16)
    m_ref[...] = inner
    dg_ref[...] = d_gate
    du_ref[...] = d_up
    out_ref[...] += times_transposed(inner, down_ref[...])
    da_ref[...] += times_transposed(d_gate, gate_ref[...]) + times_transposed(d_up, up_ref[...])

    @pl.when(pl.program_id(0) == pl.num_programs(0) - 1)
    def _():
        term_ref[...] = out_ref[...].astype(bf16)


def ffn_chunk(normed, sens, gate_full, up_full, down_back, saved, step, steps, tile=512):
    rows, width = normed.shape
    hidden = gate_full.shape[1]
    whole = pl.BlockSpec((rows, width), lambda i: (0, 0))
    weight = pl.BlockSpec((width, tile), lambda i: (0, i))
    part = pl.BlockSpec((rows, tile), lambda i: (step, i))
    act = jax.ShapeDtypeStruct((steps * rows, hidden), bf16)
    total = jax.ShapeDtypeStruct((rows, width), f32)
    return pl.pallas_call(
        ffn_kernel,
        grid=(hidden // tile,),
        in_specs=[whole, whole, weight, weight, weight]
        + [pl.BlockSpec(memory_space=pl.ANY)] * len(saved),
        out_specs=[part, part, part, whole, whole],
        out_shape=[act, act, act, jax.ShapeDtypeStruct((rows, width), bf16), total],
        scratch_shapes=[pltpu.VMEM((rows, width), f32)],
        input_output_aliases={5 + i: i for i in range(len(saved))},
        compiler_params=pltpu.CompilerParams(vmem_limit_bytes=48 * 2**20),
        cost_estimate=pl.CostEstimate(
            flops=12 * rows * width * hidden,
            bytes_accessed=6 * width * hidden + 12 * rows * width + 6 * rows * hidden,
            transcendentals=rows * hidden,
        ),
    )(normed, sens, gate_full, up_full, down_back, *saved)


def swapped(value, axis, offset):
    count = lax.axis_size(axis)
    return lax.ppermute(value, axis, [(source, source ^ offset) for source in range(count)])


CORE, XLINK, YLINK = 1, 2, 4


def gather_cube(shard, widths, after):
    if after:
        shard = lax.optimization_barrier((shard, *after))[0]
    if lax.axis_size("dp") != 8:
        full = lax.all_gather(shard, "dp", axis=0, tiled=True)
        ends = [sum(widths[: i + 1]) for i in range(len(widths))]
        return [full[:, end - width : end] for end, width in zip(ends, widths)], ()
    rows = shard.shape[0]
    half = rows // 2
    over_x = swapped(shard, "dp", XLINK)
    over_y = swapped(shard, "dp", YLINK)
    diag_top = swapped(over_x[:half], "dp", YLINK)
    diag_low = swapped(over_y[half:], "dp", XLINK)
    pieces = [
        (shard, 0, 0),
        (over_x, XLINK, 0),
        (over_y, YLINK, 0),
        (diag_top, XLINK | YLINK, 0),
        (diag_low, XLINK | YLINK, half),
    ]
    pieces += [(swapped(v, "dp", CORE), offset ^ CORE, at) for v, offset, at in pieces]

    count = len(pieces)

    def kernel(*refs):
        ins, outs = refs[:count], refs[count : count + len(widths)]
        held, in_sems, out_sems = refs[count + len(widths) :]
        me = lax.axis_index("dp")
        copies = []
        for i, (value, offset, at) in enumerate(pieces):
            start = pl.multiple_of(lax.bitwise_xor(me, offset) * rows + at, half)
            copies.append(
                pltpu.make_async_copy(
                    ins[i], held.at[pl.ds(start, value.shape[0]), :], in_sems.at[i]
                )
            )
        for copy in copies:
            copy.start()
        for copy in copies:
            copy.wait()
        copies, first = [], 0
        for j, width in enumerate(widths):
            copies.append(
                pltpu.make_async_copy(held.at[:, pl.ds(first, width)], outs[j], out_sems.at[j])
            )
            first += width
        for copy in copies:
            copy.start()
        for copy in copies:
            copy.wait()

    spec = pl.BlockSpec(memory_space=pl.ANY)
    full = pl.pallas_call(
        kernel,
        in_specs=[spec] * count,
        out_specs=[spec] * len(widths),
        out_shape=[jax.ShapeDtypeStruct((8 * rows, width), shard.dtype) for width in widths],
        scratch_shapes=[
            pltpu.VMEM((8 * rows, sum(widths)), shard.dtype),
            pltpu.SemaphoreType.DMA((count,)),
            pltpu.SemaphoreType.DMA((len(widths),)),
        ],
        cost_estimate=pl.CostEstimate(
            flops=0, bytes_accessed=32 * rows * sum(widths), transcendentals=0
        ),
    )(*[value for value, _, _ in pieces])
    return full, (over_x, over_y)


def pick(value, axis, index):
    return lax.dynamic_index_in_dim(value, index, axis, keepdims=False)


def grad_kernel(pairs, chunks, order_ref, *refs):
    keep_ref, send_ref = refs[-2:]
    for out_ref, at in ((keep_ref, 0), (send_ref, 1)):
        first = 0
        for pair in range(pairs):
            base = pair * (2 * chunks + 1)
            left = [refs[base + at * chunks + i][...] for i in range(chunks)]
            left = left[0] if chunks == 1 else jnp.concatenate(left, 0)
            right = refs[base + 2 * chunks]
            width = right.shape[1]
            out_ref[0, :, first : first + width] = contract_rows(left, right[...]).astype(bf16)
            first += width


def weight_grad(pairs, piece):
    chunks = len(pairs[0][0])
    width = sum(right.shape[1] for _, right in pairs)
    rows = pairs[0][1].shape[0]
    if lax.axis_size("dp") != 8:
        return (
            jnp.concatenate(
                [contract_rows(jnp.concatenate(left, 0), right).astype(bf16) for left, right in pairs], 1
            ),
        )
    me = lax.axis_index("dp")
    order = jnp.stack([me % 2, me // 2]).astype(jnp.int32)
    out = pl.BlockSpec((1, piece, width), lambda i, o: (i, 0, 0))
    chip = jax.ShapeDtypeStruct((4, piece, width), bf16)
    specs, values = [], []
    for left, right in pairs:
        lead = (left[0].shape[0], piece)
        specs += [pl.BlockSpec(lead, lambda i, o: (0, 2 * (i ^ o[1]) + o[0]))] * chunks
        specs += [pl.BlockSpec(lead, lambda i, o: (0, 2 * (i ^ o[1]) + 1 - o[0]))] * chunks
        specs += [pl.BlockSpec(right.shape, lambda i, o: (0, 0))]
        values += list(left) + list(left) + [right]
    return pl.pallas_call(
        functools.partial(grad_kernel, len(pairs), chunks),
        grid_spec=pltpu.PrefetchScalarGridSpec(
            num_scalar_prefetch=1, grid=(4,), in_specs=specs, out_specs=[out, out]
        ),
        out_shape=[chip, chip],
        compiler_params=pltpu.CompilerParams(vmem_limit_bytes=48 * 2**20),
        cost_estimate=pl.CostEstimate(
            flops=16 * rows * piece * width,
            bytes_accessed=16 * piece * width + 16 * rows * piece + 2 * rows * width,
            transcendentals=0,
        ),
    )(order, *values)


def wide(*values):
    total = values[0].astype(f32)
    for value in values[1:]:
        total = total + value.astype(f32)
    return total


class CubeSum:
    def __init__(self, parts):
        if len(parts) == 1:
            self.whole = lax.psum_scatter(parts[0], "dp", scatter_dimension=0, tiled=True).astype(f32)
            return
        self.whole = None
        self.keep = parts[0]
        self.moved = swapped(parts[1], "dp", CORE)

    def diagonal(self, *after):
        if self.whole is not None:
            return after
        half = self.keep.shape[1] // 2
        diag, *after = lax.optimization_barrier(
            (wide(self.keep[3], self.moved[3]).astype(bf16), *after)
        )
        self.top = swapped(diag[:half], "dp", XLINK)
        self.low = swapped(diag[half:], "dp", YLINK)
        return after

    def sides(self, *after):
        if self.whole is not None:
            return after
        half = self.keep.shape[1] // 2
        over_x = jnp.concatenate(
            [
                wide(self.keep[1, :half], self.moved[1, :half]).astype(bf16),
                wide(self.keep[1, half:], self.moved[1, half:], self.low).astype(bf16),
            ],
            0,
        )
        over_y = jnp.concatenate(
            [
                wide(self.keep[2, :half], self.moved[2, :half], self.top).astype(bf16),
                wide(self.keep[2, half:], self.moved[2, half:]).astype(bf16),
            ],
            0,
        )
        over_x, over_y, *after = lax.optimization_barrier((over_x, over_y, *after))
        self.from_x = swapped(over_x, "dp", XLINK)
        self.from_y = swapped(over_y, "dp", YLINK)
        return after

    def total(self):
        if self.whole is not None:
            return self.whole
        return wide(self.keep[0], self.moved[0], self.from_x, self.from_y)


MESH = pl.DeviceIdType.MESH
ROWS = 16


class Wires:
    def __init__(self, sends, recvs):
        self.sends, self.recvs, self.used = sends, recvs, 0

    def to(self, source, target, **device):
        copy = pltpu.make_async_remote_copy(
            src_ref=source,
            dst_ref=target,
            send_sem=self.sends.at[self.used],
            recv_sem=self.recvs.at[self.used],
            device_id=device,
            device_id_type=MESH,
        )
        self.used += 1
        copy.start()
        return copy


def greet(my_dp, my_line):
    barrier = pltpu.get_barrier_semaphore()
    for offset in range(1, 8):
        pl.semaphore_signal(
            barrier, inc=1, device_id={"dp": lax.bitwise_xor(my_dp, offset)}, device_id_type=MESH
        )
    for offset in range(1, 4):
        pl.semaphore_signal(
            barrier, inc=1, device_id={"fsdp": lax.bitwise_xor(my_line, offset)}, device_id_type=MESH
        )
    pl.semaphore_wait(barrier, 10)


def by_rows(count, body):
    def step(i, carry):
        body(pl.ds(pl.multiple_of(i * ROWS, ROWS), ROWS))
        return carry

    lax.fori_loop(0, count // ROWS, step, 0)


class CubeWires:
    def __init__(self, wires, my_dp, keep, send, moved, top, low, from_x, from_y):
        self.wires, self.keep, self.send, self.moved = wires, keep, send, moved
        self.top, self.low, self.from_x, self.from_y = top, low, from_x, from_y
        self.core = {"dp": lax.bitwise_xor(my_dp, CORE)}
        self.x = {"dp": lax.bitwise_xor(my_dp, XLINK)}
        self.y = {"dp": lax.bitwise_xor(my_dp, YLINK)}
        self.rows = keep.shape[1]
        self.sent = []

    def start(self):
        self.swap = {
            block: self.wires.to(self.send.at[block], self.moved.at[block], **self.core)
            for block in (3, 1, 2, 0)
        }

    def chip(self, block):
        self.swap[block].wait_recv()

        def add(at):
            self.moved[block, at] = wide(self.keep[block, at], self.moved[block, at]).astype(bf16)

        by_rows(self.rows, add)

    def diagonal(self):
        half = self.rows // 2
        self.chip(3)
        self.tops = self.wires.to(self.moved.at[3, pl.ds(0, half)], self.top, **self.x)
        self.lows = self.wires.to(self.moved.at[3, pl.ds(half, half)], self.low, **self.y)

    def sides(self):
        half = self.rows // 2
        self.chip(1)
        self.chip(2)
        self.tops.wait_recv()
        self.lows.wait_recv()

        def add(at):
            below = pl.ds(pl.multiple_of(at.start + half, ROWS), ROWS)
            self.moved[2, at] = wide(self.moved[2, at], self.top[at]).astype(bf16)
            self.moved[1, below] = wide(self.moved[1, below], self.low[at]).astype(bf16)

        by_rows(half, add)
        self.xs = self.wires.to(self.moved.at[1], self.from_x, **self.x)
        self.ys = self.wires.to(self.moved.at[2], self.from_y, **self.y)

    def total(self, store):
        self.swap[0].wait_recv()
        self.xs.wait_recv()
        self.ys.wait_recv()

        def add(at):
            store(at, wide(self.keep[0, at], self.moved[0, at], self.from_x[at], self.from_y[at]))

        by_rows(self.rows, add)

    def close(self):
        for copy in (*self.swap.values(), self.tops, self.lows, self.xs, self.ys):
            copy.wait_send()


def tail_kernel(
    keep_far, send_far, keep_own, send_own, back, term0, term1, term2, term3, hidden, d_hidden,
    inputs, scale, live, gain, gain_two, taps_own, taps_far,
    mixer_out, block_out, token_out, gain_out, taps_out,
    moved_far, moved_own, tops, lows, from_x, from_y, far_out, far_in, back_out, back_in, ring_in,
    gain_cut, gain_in, gain_line, gain_lines, taps_pair, taps_sum, taps_in,
    sends, recvs,
):
    my_dp, my_line = lax.axis_index("dp"), lax.axis_index("fsdp")
    right = {"fsdp": lax.rem(my_line + 1, 4)}
    pair = {"fsdp": lax.bitwise_xor(my_line, 1)}
    far = {"fsdp": lax.bitwise_xor(my_line, 2)}
    wires = Wires(sends, recvs)
    rows = inputs.shape[0]
    piece = gain_out.shape[1]
    greet(my_dp, my_line)

    taps_move = wires.to(taps_far, taps_pair, **far)
    cubes = [
        CubeWires(wires, my_dp, keep_far, send_far, moved_far, tops.at[0], lows.at[0], from_x.at[0], from_y.at[0]),
        CubeWires(wires, my_dp, keep_own, send_own, moved_own, tops.at[1], lows.at[1], from_x.at[1], from_y.at[1]),
    ]
    for cube in cubes:
        cube.start()

    def shorten(at):
        back_out[at] = back[pl.ds(pl.multiple_of(at.start + rows, ROWS), ROWS)].astype(bf16)

    by_rows(rows, shorten)
    back_move = wires.to(back_out, back_in, **pair)
    hops = [wires.to(term1, ring_in.at[0], **right)]
    for cube in cubes:
        cube.diagonal()
    taps_move.wait_recv()
    taps_sum[...] = taps_own[...] + taps_pair[...]
    taps_moves = [
        wires.to(taps_sum, taps_in.at[my_dp], dp=lax.bitwise_xor(my_dp, offset)) for offset in range(1, 8)
    ]
    for cube in cubes:
        cube.sides()

    def add_hop(step, term):
        hops[step].wait_recv()

        def add(at):
            ring_in[step, at] = wide(ring_in[step, at], term[at]).astype(bf16)

        by_rows(rows, add)
        hops.append(wires.to(ring_in.at[step], ring_in.at[step + 1], **right))

    add_hop(0, term2)
    back_move.wait_recv()
    gain_row = gain[...]
    gain_cut[...] = jnp.zeros_like(gain_cut)

    def finish(i, total):
        at = pl.ds(pl.multiple_of(i * ROWS, ROWS), ROWS)
        grad = wide(back[at], back_in[at])
        values = inputs[at].astype(f32)
        r = scale[at]
        along = values * grad
        mean = jnp.mean(along * gain_row, axis=-1, keepdims=True)
        token_out[at] = (d_hidden[at] + r * gain_row * grad - values * (r * r * r) * mean).astype(bf16)
        return total + jnp.sum((along * r).reshape(ROWS // 8, 8, -1), axis=0)

    total = lax.fori_loop(0, rows // ROWS, finish, jnp.zeros((8, inputs.shape[1]), f32))
    total = jnp.sum(total, axis=0, keepdims=True)
    for block in range(8):
        gain_cut[block, 0:1] = total[:, block * piece : (block + 1) * piece]
        gain_cut[block, 1:2] = gain_two[:, block * piece : (block + 1) * piece]
    gain_moves = []
    for offset in range(1, 8):
        peer = lax.bitwise_xor(my_dp, offset)
        gain_moves.append(wires.to(gain_cut.at[peer], gain_in.at[my_dp], dp=peer))
    gain_in[my_dp] = gain_cut[my_dp]

    def keep_low(at, value):
        far_out[at] = value.astype(bf16)

    cubes[0].total(keep_low)
    far_move = wires.to(far_out, far_in, **far)
    add_hop(1, term3)
    for move in gain_moves:
        move.wait_recv()
    gain_line[...] = jnp.sum(gain_in[...], axis=0)
    line_moves = [
        wires.to(gain_line, gain_lines.at[my_line], fsdp=lax.bitwise_xor(my_line, offset))
        for offset in range(1, 4)
    ]
    for move in taps_moves:
        move.wait_recv()
    taps_in[my_dp] = taps_sum[...]
    taps_out[...] = jnp.sum(taps_in[...], axis=0)

    def keep_wide(at, value):
        mixer_out[at] = value

    cubes[1].total(keep_wide)
    hops[2].wait_recv()

    def close_rows(at):
        block_out[at] = (live[at] * wide(hidden[at], ring_in[2, at], term0[at])).astype(bf16)

    by_rows(rows, close_rows)
    for move in line_moves:
        move.wait_recv()
    gain_lines[my_line] = gain_line[...]
    gain_out[...] = jnp.sum(gain_lines[...], axis=0)
    far_move.wait_recv()

    def add_far(at):
        mixer_out[at] = wide(mixer_out[at], far_in[at])

    by_rows(mixer_out.shape[0], add_far)
    for cube in cubes:
        cube.close()
    for move in (taps_move, back_move, far_move, *hops, *taps_moves, *gain_moves, *line_moves):
        move.wait_send()


def tail_call(parts_far, parts_own, back, terms, hidden, d_hidden, inputs, scale, live, gain, gain_two, taps_own, taps_far):
    rows, width = inputs.shape
    piece = parts_own[0].shape[1]
    grad_width = parts_own[0].shape[2]
    pad = ((0, 8 - TAPS), (0, 0))
    taps_own, taps_far = jnp.pad(taps_own, pad), jnp.pad(taps_far, pad)
    taps_width = taps_own.shape[1]
    vmem = pl.BlockSpec(memory_space=pltpu.VMEM)
    anywhere = pl.BlockSpec(memory_space=pl.ANY)
    low = lambda *shape: pltpu.VMEM(shape, bf16)
    full = lambda *shape: pltpu.VMEM(shape, f32)
    copies = 64
    return pl.pallas_call(
        tail_kernel,
        in_specs=[vmem, anywhere, vmem, anywhere] + [vmem] * 14,
        out_specs=[vmem] * 5,
        out_shape=[
            jax.ShapeDtypeStruct((piece, grad_width), f32),
            jax.ShapeDtypeStruct((rows, width), bf16),
            jax.ShapeDtypeStruct((rows, width), bf16),
            jax.ShapeDtypeStruct((8, piece), f32),
            jax.ShapeDtypeStruct((8, taps_width), f32),
        ],
        scratch_shapes=[
            low(4, piece, grad_width),
            low(4, piece, grad_width),
            low(2, piece // 2, grad_width),
            low(2, piece // 2, grad_width),
            low(2, piece, grad_width),
            low(2, piece, grad_width),
            low(piece, grad_width),
            low(piece, grad_width),
            low(rows, width),
            low(rows, width),
            low(3, rows, width),
            full(8, 8, piece),
            full(8, 8, piece),
            full(8, piece),
            full(4, 8, piece),
            full(8, taps_width),
            full(8, taps_width),
            full(8, 8, taps_width),
            pltpu.SemaphoreType.DMA((copies,)),
            pltpu.SemaphoreType.DMA((copies,)),
        ],
        compiler_params=pltpu.CompilerParams(
            collective_id=1, has_side_effects=True, vmem_limit_bytes=60 * 2**20
        ),
        cost_estimate=pl.CostEstimate(flops=10**8, bytes_accessed=3 * 10**8, transcendentals=0),
    )(
        parts_far[0], parts_far[1], parts_own[0], parts_own[1], back, *terms, hidden, d_hidden,
        inputs, scale, live, gain, gain_two, taps_own, taps_far,
    )


def total_all(value, axis):
    count = lax.axis_size(axis)
    offset = 1
    while offset < count:
        value = value + swapped(value, axis, offset)
        offset *= 2
    return value


def total_blocks(value, axis):
    count = lax.axis_size(axis)
    me = lax.axis_index(axis)
    offset = count // 2
    while offset:
        mine = me // offset % 2
        value = value.reshape((2, -1) + value.shape[1:])
        value = pick(value, 0, mine) + swapped(pick(value, 0, 1 - mine), axis, offset)
        offset //= 2
    return value[0]


def shards(
    tokens,
    cotangent,
    lengths,
    norm1_gain,
    in_weight,
    conv_taps,
    out_weight,
    norm2_gain,
    gate_weight,
    up_weight,
    down_weight,
):
    micro_count, group_count, span_len, model_width = tokens.shape
    line_count = micro_count * group_count
    row_count = line_count * span_len
    local_width = conv_taps.shape[1]
    piece = in_weight.shape[0]
    ring = lax.axis_size("fsdp")
    slices = range(0, ring, 2)
    cube = ring == 4 and lax.axis_size("dp") == 8
    my_line = lax.axis_index("fsdp")
    my_span = lax.axis_index("dp")
    slot_index = my_span * span_len + jnp.arange(span_len, dtype=jnp.int32)
    position = slot_index % SEQ_LEN
    seq_count = lengths.shape[2]
    seq_pick = (
        slot_index[:, None] // SEQ_LEN == jnp.arange(seq_count, dtype=jnp.int32)[None, :]
    ).astype(jnp.int32)
    valid_taps = [(position >= tap).astype(f32)[None, :, None] for tap in range(TAPS)]

    def from_owners(value):
        return lax.all_gather(value, "dp", axis=0, tiled=True)

    def to_owners(value):
        return lax.psum_scatter(value, "dp", scatter_dimension=0, tiled=True).astype(f32)

    gains = from_owners(jnp.stack([norm1_gain, norm2_gain], 1)).astype(f32)
    gain_one, gain_two = gains[:, 0], gains[:, 1]
    mixer_shard = jnp.concatenate([in_weight.reshape(piece, -1), out_weight.T], 1)
    gain_one, mixer_shard, gate_weight, up_weight, down_weight = lax.optimization_barrier(
        (gain_one, mixer_shard, gate_weight, up_weight, down_weight)
    )
    shards_of = [mixer_shard] + [swapped(mixer_shard, "fsdp", c) for c in slices[1:]]
    taps_of = [conv_taps] + [swapped(conv_taps, "fsdp", c) for c in slices[1:]]
    mixer_widths = (3 * local_width, local_width)
    mixers, sent = [None], ()
    mixers[0], sent = gather_cube(mixer_shard, mixer_widths, sent)
    for shard in shards_of[1:]:
        mixer, sent = gather_cube(shard, mixer_widths, sent)
        mixers.append(mixer)
    gate_full = from_owners(gate_weight)
    up_full = from_owners(up_weight)
    down_back = from_owners(down_weight.T)

    inputs_f = tokens.reshape(row_count, model_width).astype(f32)
    lens = lengths.reshape(line_count, seq_count)
    seq_lens = jnp.sum(seq_pick[None, :, :] * lens[:, None, :], axis=2)
    live_mask = (position[None, :] < seq_lens).astype(f32).reshape(row_count, 1)
    scale_one = rms_scale(inputs_f)
    sens_own = live_mask * cotangent.reshape(row_count, model_width).astype(f32)

    normed_own = (inputs_f * scale_one * gain_one).astype(bf16)
    normed_pair = jnp.concatenate([normed_own, swapped(normed_own, "fsdp", 1)], 0)
    sens_low, _ = lax.optimization_barrier((sens_own.astype(bf16), shards_of[-1]))
    sens_all = ring_gather(sens_low, "fsdp")

    pair_lines, pair_rows = 2 * line_count, 2 * row_count
    kept = []
    mixed = jnp.zeros((pair_rows, model_width), f32)
    for (in_full, out_back), taps in zip(mixers, taps_of):
        taps_f = taps.astype(f32)
        early = ring // 2 if not kept else ring - 1
        normed_pair, sens_all[early] = lax.optimization_barrier((normed_pair, sens_all[early]))
        projected = times(normed_pair, in_full)
        b_part = projected[:, :local_width]
        c_part = projected[:, local_width : 2 * local_width]
        x_part = projected[:, 2 * local_width :]
        mixed_in = (b_part * x_part).reshape(pair_lines, span_len, local_width)
        rim_in = passed_along(mixed_in[:, span_len - (TAPS - 1) :], "dp", 1)
        padded = jnp.concatenate([rim_in, mixed_in], 1)
        convolved = jnp.zeros_like(mixed_in)
        for tap in range(TAPS):
            convolved = (
                convolved
                + taps_f[tap][None, None, :]
                * padded[:, TAPS - 1 - tap : TAPS - 1 - tap + span_len]
                * valid_taps[tap]
            )
        convolved = convolved.reshape(pair_rows, local_width)
        gated = (c_part * convolved).astype(bf16)
        kept.append((in_full, out_back, taps_f, b_part, c_part, x_part, padded, convolved, gated))
        mixed = mixed + times_transposed(gated, out_back)
    moved = swapped(mixed[row_count:].astype(bf16), "fsdp", 1)
    hidden_one = inputs_f + mixed[:row_count] + moved.astype(f32)
    scale_two = rms_scale(hidden_one)
    normed = (hidden_one * scale_two * gain_two).astype(bf16)

    normed_two, terms, back_terms, saved, back_sum = [], [], [], (), None
    for step, sens in enumerate(sens_all):
        normed_two.append(normed)
        coming = passed_round(normed, "fsdp") if step < ring - 1 else None
        *saved, term, back_term = ffn_chunk(
            normed, sens, gate_full, up_full, down_back, saved, step, ring
        )
        terms.append(term)
        back_terms.append(back_term)
        if step == 0:
            normed, back_terms[0] = lax.optimization_barrier((coming, back_term))
        elif step == 1:
            back_sum = passed_round(back_term.astype(bf16), "fsdp")
            normed = coming
        elif step < ring - 1:
            back_sum, normed = lax.optimization_barrier(
                (wide(back_sum, back_term).astype(bf16), coming)
            )
            back_sum = passed_round(back_sum, "fsdp")
    back_sum, *saved = lax.optimization_barrier((back_sum, *saved))
    inner, d_gates, d_ups = saved
    back_sum = passed_round(wide(back_sum, back_terms[-1]).astype(bf16), "fsdp")
    sens_rows = jnp.concatenate(sens_all, 0)
    normed_rows = jnp.concatenate(normed_two, 0)
    down_part = contract_rows(sens_rows, inner).astype(bf16)
    gate_part = contract_rows(normed_rows, d_gates).astype(bf16)
    up_part = contract_rows(normed_rows, d_ups).astype(bf16)
    back_terms[0], down_part, gate_part = lax.optimization_barrier(
        (back_terms[0], down_part, gate_part)
    )
    d_normed_two = wide(back_sum, back_terms[0])

    gain_two_part = jnp.sum(d_normed_two * hidden_one * scale_two, axis=0)
    d_hidden = (
        sens_own
        + scale_two * gain_two * d_normed_two
        - hidden_one
        * scale_two**3
        * jnp.mean(hidden_one * gain_two * d_normed_two, axis=-1, keepdims=True)
    )
    d_hidden_low, up_part = lax.optimization_barrier((d_hidden.astype(bf16), up_part))
    down_grad = to_owners(down_part)
    gate_grad = to_owners(gate_part)
    up_grad = to_owners(up_part)
    d_mix = jnp.concatenate([d_hidden_low, swapped(d_hidden_low, "fsdp", 1)], 0)
    if not cube:
        d_mix, terms[1] = lax.optimization_barrier((d_mix, terms[1]))

    tap_parts, sums = [], []
    d_normed = jnp.zeros((pair_rows, model_width), f32)
    for in_full, out_back, taps_f, b_part, c_part, x_part, padded, convolved, gated in kept[::-1]:
        d_gated = times(d_mix, out_back)
        d_c_part = d_gated * convolved
        d_conv = (d_gated * c_part).reshape(pair_lines, span_len, local_width)
        d_padded = jnp.zeros_like(padded)
        tap_rows = []
        for tap in range(TAPS):
            weighted = d_conv * valid_taps[tap]
            d_padded = d_padded + jnp.pad(
                taps_f[tap][None, None, :] * weighted,
                ((0, 0), (TAPS - 1 - tap, tap), (0, 0)),
            )
            tap_rows.append(
                jnp.sum(weighted * padded[:, TAPS - 1 - tap : TAPS - 1 - tap + span_len], axis=(0, 1))
            )
        tap_parts.append(jnp.stack(tap_rows, 0))
        rim_back = passed_along(d_padded[:, : TAPS - 1], "dp", -1)
        d_mixed = (
            d_padded[:, TAPS - 1 :]
            + jnp.pad(rim_back, ((0, 0), (span_len - (TAPS - 1), 0), (0, 0)))
        ).reshape(pair_rows, local_width)
        d_proj = jnp.concatenate([d_mixed * x_part, d_c_part, d_mixed * b_part], axis=1).astype(bf16)
        d_normed = d_normed + times_transposed(d_proj, in_full)
        parts = weight_grad([([normed_pair], d_proj), ([d_mix], gated)], piece)
        if cube:
            sums.append(parts)
            continue
        d_mix, d_normed, *parts = lax.optimization_barrier((d_mix, d_normed, *parts))
        sums.append(CubeSum(parts))
    if cube:
        mixer_sum, block_out, token_grad, gain_grads, taps_grad = tail_call(
            sums[0],
            sums[1],
            d_normed,
            terms,
            hidden_one,
            d_hidden,
            tokens.reshape(row_count, model_width),
            scale_one,
            live_mask,
            gain_one[None],
            gain_two_part[None],
            tap_parts[1],
            tap_parts[0],
        )
        return (
            block_out.reshape(tokens.shape),
            token_grad.reshape(tokens.shape),
            gain_grads[0],
            mixer_sum[:, : 3 * local_width].reshape(in_weight.shape),
            taps_grad[:TAPS],
            mixer_sum[:, 3 * local_width :].T,
            gain_grads[1],
            gate_grad,
            up_grad,
            down_grad.T,
        )
    moved = swapped(d_normed[row_count:].astype(bf16), "fsdp", 1)
    for step in sums[:-1]:
        (moved,) = step.diagonal(moved)
    for step in sums[:-1]:
        (moved,) = step.sides(moved)
    (moved,) = sums[-1].diagonal(moved)
    (moved,) = sums[-1].sides(moved)
    d_normed_one = d_normed[:row_count] + moved.astype(f32)
    gain_one_part = jnp.sum(d_normed_one * inputs_f * scale_one, axis=0)
    token_grad = (
        d_hidden
        + scale_one * gain_one * d_normed_one
        - inputs_f
        * scale_one**3
        * jnp.mean(inputs_f * gain_one * d_normed_one, axis=-1, keepdims=True)
    ).astype(bf16)

    mixer_sum = sums[-1].total()
    for c, step in list(zip(slices[::-1], sums))[:-1]:
        mixer_sum = mixer_sum + swapped(step.total().astype(bf16), "fsdp", c).astype(f32)
    in_grad = mixer_sum[:, : 3 * local_width].reshape(in_weight.shape)
    out_grad = mixer_sum[:, 3 * local_width :].T

    ffn_out = ring_collect(terms, "fsdp")
    block_out = (live_mask * (hidden_one + ffn_out)).astype(bf16)

    taps_sum = tap_parts[-1]
    for c, part in list(zip(slices[::-1], tap_parts))[:-1]:
        taps_sum = taps_sum + swapped(part, "fsdp", c)
    taps_grad = total_all(taps_sum, "dp")
    gain_grads = total_blocks(
        jnp.concatenate(
            [gain_one_part.reshape(-1, piece), gain_two_part.reshape(-1, piece)], 1
        ),
        "dp",
    )
    gain_grads = total_all(gain_grads, "fsdp").reshape(2, piece)
    return (
        block_out.reshape(tokens.shape),
        token_grad.reshape(tokens.shape),
        gain_grads[0],
        in_grad,
        taps_grad,
        out_grad,
        gain_grads[1],
        gate_grad,
        up_grad,
        down_grad.T,
    )


def solution(mesh):
    rows = P(None, "fsdp", "dp", None)
    return jax.shard_map(
        shards,
        mesh=mesh,
        in_specs=(
            rows,
            rows,
            P(None, "fsdp", None),
            P("dp"),
            P("dp", None, "fsdp"),
            P(None, "fsdp"),
            P("fsdp", "dp"),
            P("dp"),
            P("dp", "fsdp"),
            P("dp", "fsdp"),
            P("fsdp", "dp"),
        ),
        out_specs=(
            rows,
            rows,
            P("dp"),
            P("dp", None, "fsdp"),
            P(None, "fsdp"),
            P("fsdp", "dp"),
            P("dp"),
            P("dp", "fsdp"),
            P("dp", "fsdp"),
            P("fsdp", "dp"),
        ),
        check_vma=False,
    )
```

```python
import functools

import jax
import jax.numpy as jnp
from jax import lax
from jax.experimental import pallas as pl
from jax.experimental.pallas import tpu as pltpu
from jax.sharding import PartitionSpec as P

SEQ_LEN = 1024
TAPS = 3

norm_eps = 1e-05
f32 = jnp.float32
bf16 = jnp.bfloat16


def passed_along(value, axis, steps):
    count = lax.axis_size(axis)
    first, last = (max(0, -steps), min(count, count - steps))
    return lax.ppermute(value, axis, [(source, source + steps) for source in range(first, last)])


def passed_round(value, axis):
    count = lax.axis_size(axis)
    return lax.ppermute(value, axis, [(source, (source + 1) % count) for source in range(count)])


def ring_gather(value, axis):
    chunks = [value]
    for _ in range(lax.axis_size(axis) - 1):
        chunks.append(passed_round(chunks[-1], axis))
    return chunks


def ring_collect(terms, axis):
    count = lax.axis_size(axis)
    total = terms[1 % count]
    for step in range(1, count):
        moved = passed_round(total.astype(bf16), axis)
        total = wide(moved, terms[(step + 1) % count])
    return total


def rms_scale(values):
    return lax.rsqrt(jnp.mean(values * values, axis=-1, keepdims=True) + norm_eps)


def times(left, right):
    return jnp.dot(left, right, preferred_element_type=f32)


def times_transposed(left, right):
    return lax.dot_general(left, right, (((1,), (1,)), ((), ())), preferred_element_type=f32)


def contract_rows(left, right):
    return lax.dot_general(left, right, (((0,), (0,)), ((), ())), preferred_element_type=f32)


def ffn_kernel(a_ref, e_ref, gate_ref, up_ref, down_ref, *refs):
    m_ref, dg_ref, du_ref, term_ref, back_ref, out_ref, da_ref = refs[-7:]

    @pl.when(pl.program_id(0) == 0)
    def _():
        out_ref[...] = jnp.zeros_like(out_ref)
        da_ref[...] = jnp.zeros_like(da_ref)

    rows, sens = a_ref[...], e_ref[...]
    gate_pre = times(rows, gate_ref[...])
    up_pre = times(rows, up_ref[...])
    d_inner = times(sens, down_ref[...])
    sigmoid_gate = 1.0 / (1.0 + jnp.exp(-gate_pre))
    silu_gate = gate_pre * sigmoid_gate
    inner = (silu_gate * up_pre).astype(bf16)
    d_gate = (d_inner * up_pre * (sigmoid_gate * (1.0 + gate_pre * (1.0 - sigmoid_gate)))).astype(bf16)
    d_up = (d_inner * silu_gate).astype(bf16)
    m_ref[...] = inner
    dg_ref[...] = d_gate
    du_ref[...] = d_up
    out_ref[...] += times_transposed(inner, down_ref[...])
    da_ref[...] += times_transposed(d_gate, gate_ref[...]) + times_transposed(d_up, up_ref[...])

    @pl.when(pl.program_id(0) == pl.num_programs(0) - 1)
    def _():
        term_ref[...] = out_ref[...].astype(bf16)
        back_ref[...] = da_ref[...].astype(bf16)


def ffn_chunk(normed, sens, gate_full, up_full, down_back, saved, step, steps, tile=512):
    rows, width = normed.shape
    hidden = gate_full.shape[1]
    whole = pl.BlockSpec((rows, width), lambda i: (0, 0))
    weight = pl.BlockSpec((width, tile), lambda i: (0, i))
    part = pl.BlockSpec((rows, tile), lambda i: (step, i))
    act = jax.ShapeDtypeStruct((steps * rows, hidden), bf16)
    total = jax.ShapeDtypeStruct((rows, width), bf16)
    return pl.pallas_call(
        ffn_kernel,
        grid=(hidden // tile,),
        in_specs=[whole, whole, weight, weight, weight]
        + [pl.BlockSpec(memory_space=pl.ANY)] * len(saved),
        out_specs=[part, part, part, whole, whole],
        out_shape=[act, act, act, total, total],
        scratch_shapes=[pltpu.VMEM((rows, width), f32)] * 2,
        input_output_aliases={5 + i: i for i in range(len(saved))},
        compiler_params=pltpu.CompilerParams(vmem_limit_bytes=48 * 2**20),
        cost_estimate=pl.CostEstimate(
            flops=12 * rows * width * hidden,
            bytes_accessed=6 * width * hidden + 12 * rows * width + 6 * rows * hidden,
            transcendentals=rows * hidden,
        ),
    )(normed, sens, gate_full, up_full, down_back, *saved)


def swapped(value, axis, offset):
    count = lax.axis_size(axis)
    return lax.ppermute(value, axis, [(source, source ^ offset) for source in range(count)])


CORE, XLINK, YLINK = 1, 2, 4


def gather_cube(shard, widths, after):
    if after:
        shard = lax.optimization_barrier((shard, *after))[0]
    if lax.axis_size("dp") != 8:
        full = lax.all_gather(shard, "dp", axis=0, tiled=True)
        ends = [sum(widths[: i + 1]) for i in range(len(widths))]
        return [full[:, end - width : end] for end, width in zip(ends, widths)], ()
    rows = shard.shape[0]
    half = rows // 2
    over_x = swapped(shard, "dp", XLINK)
    over_y = swapped(shard, "dp", YLINK)
    diag_top = swapped(over_x[:half], "dp", YLINK)
    diag_low = swapped(over_y[half:], "dp", XLINK)
    pieces = [
        (shard, 0, 0),
        (over_x, XLINK, 0),
        (over_y, YLINK, 0),
        (diag_top, XLINK | YLINK, 0),
        (diag_low, XLINK | YLINK, half),
    ]
    pieces += [(swapped(v, "dp", CORE), offset ^ CORE, at) for v, offset, at in pieces]

    count = len(pieces)

    def kernel(*refs):
        ins, outs = refs[:count], refs[count : count + len(widths)]
        held, in_sems, out_sems = refs[count + len(widths) :]
        me = lax.axis_index("dp")
        copies = []
        for i, (value, offset, at) in enumerate(pieces):
            start = pl.multiple_of(lax.bitwise_xor(me, offset) * rows + at, half)
            copies.append(
                pltpu.make_async_copy(
                    ins[i], held.at[pl.ds(start, value.shape[0]), :], in_sems.at[i]
                )
            )
        for copy in copies:
            copy.start()
        for copy in copies:
            copy.wait()
        copies, first = [], 0
        for j, width in enumerate(widths):
            copies.append(
                pltpu.make_async_copy(held.at[:, pl.ds(first, width)], outs[j], out_sems.at[j])
            )
            first += width
        for copy in copies:
            copy.start()
        for copy in copies:
            copy.wait()

    spec = pl.BlockSpec(memory_space=pl.ANY)
    full = pl.pallas_call(
        kernel,
        in_specs=[spec] * count,
        out_specs=[spec] * len(widths),
        out_shape=[jax.ShapeDtypeStruct((8 * rows, width), shard.dtype) for width in widths],
        scratch_shapes=[
            pltpu.VMEM((8 * rows, sum(widths)), shard.dtype),
            pltpu.SemaphoreType.DMA((count,)),
            pltpu.SemaphoreType.DMA((len(widths),)),
        ],
        cost_estimate=pl.CostEstimate(
            flops=0, bytes_accessed=32 * rows * sum(widths), transcendentals=0
        ),
    )(*[value for value, _, _ in pieces])
    return full, (over_x, over_y)


def pick(value, axis, index):
    return lax.dynamic_index_in_dim(value, index, axis, keepdims=False)


def grad_kernel(pairs, chunks, order_ref, *refs):
    keep_ref, send_ref = refs[-2:]
    for out_ref, at in ((keep_ref, 0), (send_ref, 1)):
        first = 0
        for pair in range(pairs):
            base = pair * (2 * chunks + 1)
            left = [refs[base + at * chunks + i][...] for i in range(chunks)]
            left = left[0] if chunks == 1 else jnp.concatenate(left, 0)
            right = refs[base + 2 * chunks]
            width = right.shape[1]
            out_ref[0, :, first : first + width] = contract_rows(left, right[...]).astype(bf16)
            first += width


def weight_grad(pairs, piece):
    chunks = len(pairs[0][0])
    width = sum(right.shape[1] for _, right in pairs)
    rows = pairs[0][1].shape[0]
    if lax.axis_size("dp") != 8:
        return (
            jnp.concatenate(
                [contract_rows(jnp.concatenate(left, 0), right).astype(bf16) for left, right in pairs], 1
            ),
        )
    me = lax.axis_index("dp")
    order = jnp.stack([me % 2, me // 2]).astype(jnp.int32)
    out = pl.BlockSpec((1, piece, width), lambda i, o: (i, 0, 0))
    chip = jax.ShapeDtypeStruct((4, piece, width), bf16)
    specs, values = [], []
    for left, right in pairs:
        lead = (left[0].shape[0], piece)
        specs += [pl.BlockSpec(lead, lambda i, o: (0, 2 * (i ^ o[1]) + o[0]))] * chunks
        specs += [pl.BlockSpec(lead, lambda i, o: (0, 2 * (i ^ o[1]) + 1 - o[0]))] * chunks
        specs += [pl.BlockSpec(right.shape, lambda i, o: (0, 0))]
        values += list(left) + list(left) + [right]
    return pl.pallas_call(
        functools.partial(grad_kernel, len(pairs), chunks),
        grid_spec=pltpu.PrefetchScalarGridSpec(
            num_scalar_prefetch=1, grid=(4,), in_specs=specs, out_specs=[out, out]
        ),
        out_shape=[chip, chip],
        compiler_params=pltpu.CompilerParams(vmem_limit_bytes=48 * 2**20),
        cost_estimate=pl.CostEstimate(
            flops=16 * rows * piece * width,
            bytes_accessed=16 * piece * width + 16 * rows * piece + 2 * rows * width,
            transcendentals=0,
        ),
    )(order, *values)


def wide(*values):
    total = values[0].astype(f32)
    for value in values[1:]:
        total = total + value.astype(f32)
    return total


class CubeSum:
    def __init__(self, parts):
        if len(parts) == 1:
            self.whole = lax.psum_scatter(parts[0], "dp", scatter_dimension=0, tiled=True).astype(f32)
            return
        self.whole = None
        self.keep = parts[0]
        self.moved = swapped(parts[1], "dp", CORE)

    def diagonal(self, *after):
        if self.whole is not None:
            return after
        half = self.keep.shape[1] // 2
        diag, *after = lax.optimization_barrier(
            (wide(self.keep[3], self.moved[3]).astype(bf16), *after)
        )
        self.top = swapped(diag[:half], "dp", XLINK)
        self.low = swapped(diag[half:], "dp", YLINK)
        return after

    def sides(self, *after):
        if self.whole is not None:
            return after
        half = self.keep.shape[1] // 2
        over_x = jnp.concatenate(
            [
                wide(self.keep[1, :half], self.moved[1, :half]).astype(bf16),
                wide(self.keep[1, half:], self.moved[1, half:], self.low).astype(bf16),
            ],
            0,
        )
        over_y = jnp.concatenate(
            [
                wide(self.keep[2, :half], self.moved[2, :half], self.top).astype(bf16),
                wide(self.keep[2, half:], self.moved[2, half:]).astype(bf16),
            ],
            0,
        )
        over_x, over_y, *after = lax.optimization_barrier((over_x, over_y, *after))
        self.from_x = swapped(over_x, "dp", XLINK)
        self.from_y = swapped(over_y, "dp", YLINK)
        return after

    def total(self):
        if self.whole is not None:
            return self.whole
        return wide(self.keep[0], self.moved[0], self.from_x, self.from_y)


MESH = pl.DeviceIdType.MESH
ROWS = 16


class Wires:
    def __init__(self, sends, recvs):
        self.sends, self.recvs, self.used = sends, recvs, 0

    def to(self, source, target, **device):
        copy = pltpu.make_async_remote_copy(
            src_ref=source,
            dst_ref=target,
            send_sem=self.sends.at[self.used],
            recv_sem=self.recvs.at[self.used],
            device_id=device,
            device_id_type=MESH,
        )
        self.used += 1
        copy.start()
        return copy


def greet(my_dp, my_line):
    barrier = pltpu.get_barrier_semaphore()
    for offset in range(1, 8):
        pl.semaphore_signal(
            barrier, inc=1, device_id={"dp": lax.bitwise_xor(my_dp, offset)}, device_id_type=MESH
        )
    for offset in range(1, 4):
        pl.semaphore_signal(
            barrier, inc=1, device_id={"fsdp": lax.bitwise_xor(my_line, offset)}, device_id_type=MESH
        )
    pl.semaphore_wait(barrier, 10)


def by_rows(count, body):
    def step(i, carry):
        body(pl.ds(pl.multiple_of(i * ROWS, ROWS), ROWS))
        return carry

    lax.fori_loop(0, count // ROWS, step, 0)


class CubeWires:
    def __init__(self, wires, my_dp, keep, send, moved, top, low, from_x, from_y):
        self.wires, self.keep, self.send, self.moved = wires, keep, send, moved
        self.top, self.low, self.from_x, self.from_y = top, low, from_x, from_y
        self.core = {"dp": lax.bitwise_xor(my_dp, CORE)}
        self.x = {"dp": lax.bitwise_xor(my_dp, XLINK)}
        self.y = {"dp": lax.bitwise_xor(my_dp, YLINK)}
        self.rows = keep.shape[1]
        self.sent = []

    def start(self):
        self.swap = {
            block: self.wires.to(self.send.at[block], self.moved.at[block], **self.core)
            for block in (3, 1, 2, 0)
        }

    def chip(self, block):
        self.swap[block].wait_recv()

        def add(at):
            self.moved[block, at] = wide(self.keep[block, at], self.moved[block, at]).astype(bf16)

        by_rows(self.rows, add)

    def diagonal(self):
        half = self.rows // 2
        self.chip(3)
        self.tops = self.wires.to(self.moved.at[3, pl.ds(0, half)], self.top, **self.x)
        self.lows = self.wires.to(self.moved.at[3, pl.ds(half, half)], self.low, **self.y)
        self.chip(1)
        self.chip(2)
        self.sides = [self.side(1, 0), self.side(2, half)]

    def side(self, block, first):
        at = pl.ds(first, self.rows // 2)
        target, device = ((self.from_x, self.x), (self.from_y, self.y))[block - 1]
        return self.wires.to(self.moved.at[block, at], target.at[at], **device)

    def others(self):
        half = self.rows // 2
        self.tops.wait_recv()

        def add_top(at):
            self.moved[2, at] = wide(self.moved[2, at], self.top[at]).astype(bf16)

        by_rows(half, add_top)
        self.sides.append(self.side(2, 0))
        self.lows.wait_recv()

        def add_low(at):
            below = pl.ds(pl.multiple_of(at.start + half, ROWS), ROWS)
            self.moved[1, below] = wide(self.moved[1, below], self.low[at]).astype(bf16)

        by_rows(half, add_low)
        self.sides.append(self.side(1, half))

    def total(self, store):
        self.swap[0].wait_recv()
        for side in self.sides:
            side.wait_recv()

        def add(at):
            store(at, wide(self.keep[0, at], self.moved[0, at], self.from_x[at], self.from_y[at]))

        by_rows(self.rows, add)

    def close(self):
        for copy in (*self.swap.values(), self.tops, self.lows, *self.sides):
            copy.wait_send()


class Spread:
    def __init__(self, wires, my_dp, shard, full, own_sem):
        self.wires, self.my_dp, self.shard, self.full, self.own_sem = wires, my_dp, shard, full, own_sem
        self.rows = shard.shape[0]
        self.core = {"dp": lax.bitwise_xor(my_dp, CORE)}
        self.x = {"dp": lax.bitwise_xor(my_dp, XLINK)}
        self.y = {"dp": lax.bitwise_xor(my_dp, YLINK)}

    def block(self, offset, first=0, count=None):
        half = self.rows // 2
        start = lax.bitwise_xor(self.my_dp, offset) * self.rows + first
        return self.full.at[pl.ds(pl.multiple_of(start, half), count or self.rows)]

    def start(self):
        own = self.block(0)
        self.own = pltpu.make_async_copy(self.shard, own, self.own_sem)
        self.own.start()
        self.over_x = self.wires.to(self.shard, own, **self.x)
        self.over_y = self.wires.to(self.shard, own, **self.y)
        self.cores = [self.wires.to(self.shard, own, **self.core)]

    def pass_on(self, block, **device):
        return self.wires.to(block, block, **device)

    def relay(self):
        half = self.rows // 2
        self.over_x.wait_recv()
        self.top = self.pass_on(self.block(XLINK, 0, half), **self.y)
        self.over_y.wait_recv()
        self.low = self.pass_on(self.block(YLINK, half, half), **self.x)
        self.cores += [self.pass_on(self.block(offset), **self.core) for offset in (XLINK, YLINK)]

    def finish(self):
        half = self.rows // 2
        for move, first in ((self.top, 0), (self.low, half)):
            move.wait_recv()
            self.cores.append(self.pass_on(self.block(XLINK | YLINK, first, half), **self.core))

    def complete(self):
        self.own.wait()
        for move in self.cores:
            move.wait_recv()

    def close(self):
        for move in (self.over_x, self.over_y, self.top, self.low, *self.cores):
            move.wait_send()


def head_kernel(
    span, mixer, gate, up, down, sens, inputs, gains, taps,
    in_own, in_far, back_own, back_far, gate_full, up_full, down_full, sens1, sens2, sens3,
    normed, proj_own, proj_far, conv_own, conv_far, gated_own, gated_far, rim_own, rim_far,
    hidden, normed_two, normed_next, scale_one, scale_two, gain_one, gain_two,
    full_own, full_far, mixer_far, taps_far, total, lines_own, lines_far, mix_out, mix_in, gains_in,
    own_sems, out_sems, sends, recvs,
):
    my_dp, my_line = lax.axis_index("dp"), lax.axis_index("fsdp")
    right = {"fsdp": lax.rem(my_line + 1, 4)}
    pair = {"fsdp": lax.bitwise_xor(my_line, 1)}
    far = {"fsdp": lax.bitwise_xor(my_line, 2)}
    wires = Wires(sends, recvs)
    rows, width = inputs.shape
    piece = gains.shape[1]
    local = taps.shape[1]
    line_count = 2 * rows // span
    greet(my_dp, my_line)

    gain_moves = [
        wires.to(gains, gains_in.at[my_dp], dp=lax.bitwise_xor(my_dp, offset)) for offset in range(1, 8)
    ]
    taps_move = wires.to(taps, taps_far, **far)
    spreads = [
        Spread(wires, my_dp, shard, full, own_sems.at[i])
        for i, (shard, full) in enumerate(
            ((mixer, full_own), (mixer_far, full_far), (gate, gate_full), (up, up_full), (down, down_full))
        )
    ]
    one, two, gates, ups, downs = spreads
    one.start()
    mixer_move = wires.to(mixer, mixer_far, **far)
    gains_in[my_dp] = gains[...]
    for move in gain_moves:
        move.wait_recv()
    for block in range(8):
        gain_one[:, block * piece : (block + 1) * piece] = gains_in[block, 0:1]
        gain_two[:, block * piece : (block + 1) * piece] = gains_in[block, 1:2]
    gain_row, gain_next = gain_one[...], gain_two[...]

    def first_norm(at):
        values = inputs[at].astype(f32)
        r = lax.rsqrt(jnp.mean(values * values, axis=-1, keepdims=True) + norm_eps)
        scale_one[at] = r
        normed[at] = (values * r * gain_row).astype(bf16)

    by_rows(rows, first_norm)
    normed_move = wires.to(normed.at[pl.ds(0, rows)], normed.at[pl.ds(rows, rows)], **pair)

    def mix(full, proj, conv, gated, rim, lines, taps_ref, first):
        def project(j, carry):
            columns = pl.ds(pl.multiple_of(j * local, local), local)
            proj[:, columns] = times(normed[...], full[:, columns])
            return carry

        lax.fori_loop(0, 3, project, 0)

        @pl.when(my_dp == 0)
        def _():
            lines[:, 0:8] = jnp.zeros((line_count, 8, local), f32)

        def gate_in(i, carry):
            at = pl.ds(pl.multiple_of(i * span, span), span)
            lines[i, 8 : 8 + span] = proj[at, 0:local] * proj[at, 2 * local : 3 * local]
            return carry

        lax.fori_loop(0, line_count, gate_in, 0)
        rim_move = pltpu.make_async_remote_copy(
            src_ref=lines.at[:, pl.ds(span, 8)],
            dst_ref=lines.at[:, pl.ds(0, 8)],
            send_sem=sends.at[wires.used],
            recv_sem=recvs.at[wires.used],
            device_id={"dp": jnp.minimum(my_dp + 1, 7)},
            device_id_type=MESH,
        )
        wires.used += 1

        @pl.when(my_dp < 7)
        def _():
            rim_move.start()

        @pl.when(my_dp > 0)
        def _():
            rim_move.wait_recv()

        rim[...] = lines[:, 0:8]
        tap_rows = [taps_ref[tap : tap + 1] for tap in range(TAPS)]

        def convolve(i, carry):
            for base in range(0, span, ROWS):
                at = pl.ds(pl.multiple_of(i * span + base, ROWS), ROWS)
                spot = my_dp * span + base + lax.broadcasted_iota(jnp.int32, (ROWS, 1), 0)
                position = lax.rem(spot, SEQ_LEN)
                value = tap_rows[0] * lines[i, 8 + base : 8 + base + ROWS]
                for tap in range(1, TAPS):
                    before = tap_rows[tap] * lines[i, 8 + base - tap : 8 + base - tap + ROWS]
                    value = value + jnp.where(position >= tap, before, 0.0)
                conv[at] = value
                gated[at] = (proj[at, local : 2 * local] * value).astype(bf16)
            return carry

        lax.fori_loop(0, line_count, convolve, 0)

        def back(j, carry):
            columns = pl.ds(pl.multiple_of(j * local, local), local)
            value = times_transposed(gated[...], full[columns, 3 * local : 4 * local])
            total[:, columns] = value if first else total[:, columns] + value
            return carry

        lax.fori_loop(0, width // local, back, 0)
        return rim_move

    def write_out(full, in_ref, back_ref, i):
        copies = [
            pltpu.make_async_copy(full.at[:, pl.ds(0, 3 * local)], in_ref, out_sems.at[2 * i]),
            pltpu.make_async_copy(full.at[:, pl.ds(3 * local, local)], back_ref, out_sems.at[2 * i + 1]),
        ]
        for copy in copies:
            copy.start()
        return copies

    one.relay()
    gates.start()
    taps_move.wait_recv()
    mixer_move.wait_recv()
    sens_moves = [wires.to(sens, sens1, **right)]
    two.start()
    one.finish()
    normed_move.wait_recv()
    one.complete()
    rims = [mix(full_own, proj_own, conv_own, gated_own, rim_own, lines_own, taps, True)]
    outs = write_out(full_own, in_own, back_own, 0)
    gates.relay()
    ups.start()
    sens_moves[0].wait_recv()
    sens_moves.append(wires.to(sens1, sens2, **right))
    two.relay()
    gates.finish()
    sens_moves[1].wait_recv()
    sens_moves.append(wires.to(sens2, sens3, **right))
    two.finish()
    two.complete()
    rims.append(mix(full_far, proj_far, conv_far, gated_far, rim_far, lines_far, taps_far, False))

    def shorten(at):
        mix_out[at] = total[pl.ds(pl.multiple_of(at.start + rows, ROWS), ROWS)].astype(bf16)

    by_rows(rows, shorten)
    mix_move = wires.to(mix_out, mix_in, **pair)
    outs += write_out(full_far, in_far, back_far, 1)
    ups.relay()
    downs.start()
    mix_move.wait_recv()

    def second_norm(at):
        values = wide(inputs[at], total[at], mix_in[at])
        hidden[at] = values
        r = lax.rsqrt(jnp.mean(values * values, axis=-1, keepdims=True) + norm_eps)
        scale_two[at] = r
        normed_two[at] = (values * r * gain_next).astype(bf16)

    by_rows(rows, second_norm)
    next_move = wires.to(normed_two, normed_next, **right)
    ups.finish()
    downs.relay()
    downs.finish()
    sens_moves[2].wait_recv()
    for spread in (gates, ups, downs):
        spread.complete()
    next_move.wait_recv()
    for copy in outs:
        copy.wait()
    for spread in spreads:
        spread.close()

    @pl.when(my_dp < 7)
    def _():
        for move in rims:
            move.wait_send()

    for move in (taps_move, mixer_move, normed_move, mix_move, next_move, *gain_moves, *sens_moves):
        move.wait_send()


def head_call(mixer, gate, up, down, sens, inputs, gains, taps, span):
    rows, width = inputs.shape
    piece = mixer.shape[0]
    local = taps.shape[1]
    hidden = gate.shape[1]
    lines = 2 * rows // span
    vmem = pl.BlockSpec(memory_space=pltpu.VMEM)
    anywhere = pl.BlockSpec(memory_space=pl.ANY)
    low = lambda *shape: pltpu.VMEM(shape, bf16)
    full = lambda *shape: pltpu.VMEM(shape, f32)
    out = lambda kind, *shape: jax.ShapeDtypeStruct(shape, kind)
    copies = 80
    return pl.pallas_call(
        functools.partial(head_kernel, span),
        in_specs=[anywhere] * 5 + [vmem] * 3,
        out_specs=[anywhere] * 10 + [vmem] * 16,
        out_shape=[
            out(bf16, width, 3 * local),
            out(bf16, width, 3 * local),
            out(bf16, width, local),
            out(bf16, width, local),
            out(bf16, width, hidden),
            out(bf16, width, hidden),
            out(bf16, width, hidden),
            out(bf16, rows, width),
            out(bf16, rows, width),
            out(bf16, rows, width),
            out(bf16, 2 * rows, width),
            out(f32, 2 * rows, 3 * local),
            out(f32, 2 * rows, 3 * local),
            out(f32, 2 * rows, local),
            out(f32, 2 * rows, local),
            out(bf16, 2 * rows, local),
            out(bf16, 2 * rows, local),
            out(f32, lines, 8, local),
            out(f32, lines, 8, local),
            out(f32, rows, width),
            out(bf16, rows, width),
            out(bf16, rows, width),
            out(f32, rows, 1),
            out(f32, rows, 1),
            out(f32, 1, width),
            out(f32, 1, width),
        ],
        scratch_shapes=[
            low(width, 4 * local),
            low(width, 4 * local),
            low(piece, 4 * local),
            full(*taps.shape),
            full(2 * rows, width),
            full(lines, 8 + span, local),
            full(lines, 8 + span, local),
            low(rows, width),
            low(rows, width),
            full(8, 8, piece),
            pltpu.SemaphoreType.DMA((5,)),
            pltpu.SemaphoreType.DMA((4,)),
            pltpu.SemaphoreType.DMA((copies,)),
            pltpu.SemaphoreType.DMA((copies,)),
        ],
        compiler_params=pltpu.CompilerParams(
            collective_id=3, has_side_effects=True, vmem_limit_bytes=60 * 2**20
        ),
        cost_estimate=pl.CostEstimate(
            flops=32 * rows * width * local, bytes_accessed=2 * 10**8, transcendentals=0
        ),
    )(mixer, gate, up, down, sens, inputs, gains, taps)


def tail_kernel(
    keep_far, send_far, keep_own, send_own, back, d_hidden, inputs, scale, gain, gain_two, taps_own, taps_far,
    mixer_out, token_out, gain_out, taps_out,
    moved_far, moved_own, tops, lows, from_x, from_y, far_out, far_in, back_out, back_in,
    gain_cut, gain_in, gain_line, gain_lines, taps_pair, taps_sum, taps_in,
    sends, recvs,
):
    my_dp, my_line = lax.axis_index("dp"), lax.axis_index("fsdp")
    pair = {"fsdp": lax.bitwise_xor(my_line, 1)}
    far = {"fsdp": lax.bitwise_xor(my_line, 2)}
    wires = Wires(sends, recvs)
    rows = inputs.shape[0]
    piece = gain_out.shape[1]
    greet(my_dp, my_line)

    taps_move = wires.to(taps_far, taps_pair, **far)
    far_cube = CubeWires(
        wires, my_dp, keep_far, send_far, moved_far, tops.at[0], lows.at[0], from_x.at[0], from_y.at[0]
    )
    own_cube = CubeWires(
        wires, my_dp, keep_own, send_own, moved_own, tops.at[1], lows.at[1], from_x.at[1], from_y.at[1]
    )
    far_cube.start()
    own_cube.start()

    def shorten(at):
        back_out[at] = back[pl.ds(pl.multiple_of(at.start + rows, ROWS), ROWS)].astype(bf16)

    by_rows(rows, shorten)
    back_move = wires.to(back_out, back_in, **pair)
    far_cube.diagonal()
    taps_move.wait_recv()
    taps_sum[...] = taps_own[...] + taps_pair[...]
    taps_moves = [
        wires.to(taps_sum, taps_in.at[my_dp], dp=lax.bitwise_xor(my_dp, offset)) for offset in range(1, 8)
    ]
    far_cube.others()
    own_cube.diagonal()
    back_move.wait_recv()
    gain_row = gain[...]
    gain_cut[...] = jnp.zeros_like(gain_cut)

    def finish(i, total):
        at = pl.ds(pl.multiple_of(i * ROWS, ROWS), ROWS)
        grad = wide(back[at], back_in[at])
        values = inputs[at].astype(f32)
        r = scale[at]
        along = values * grad
        mean = jnp.mean(along * gain_row, axis=-1, keepdims=True)
        token_out[at] = (d_hidden[at] + r * gain_row * grad - values * (r * r * r) * mean).astype(bf16)
        return total + jnp.sum((along * r).reshape(ROWS // 8, 8, -1), axis=0)

    total = lax.fori_loop(0, rows // ROWS, finish, jnp.zeros((8, inputs.shape[1]), f32))
    total = jnp.sum(total, axis=0, keepdims=True)
    for block in range(8):
        gain_cut[block, 0:1] = total[:, block * piece : (block + 1) * piece]
        gain_cut[block, 1:2] = gain_two[:, block * piece : (block + 1) * piece]
    gain_moves = []
    for offset in range(1, 8):
        peer = lax.bitwise_xor(my_dp, offset)
        gain_moves.append(wires.to(gain_cut.at[peer], gain_in.at[my_dp], dp=peer))
    gain_in[my_dp] = gain_cut[my_dp]

    def keep_low(at, value):
        far_out[at] = value.astype(bf16)

    far_cube.total(keep_low)
    far_move = wires.to(far_out, far_in, **far)
    own_cube.others()
    for move in gain_moves:
        move.wait_recv()
    gain_line[...] = jnp.sum(gain_in[...], axis=0)
    line_moves = [
        wires.to(gain_line, gain_lines.at[my_line], fsdp=lax.bitwise_xor(my_line, offset))
        for offset in range(1, 4)
    ]
    for move in taps_moves:
        move.wait_recv()
    taps_in[my_dp] = taps_sum[...]
    taps_out[...] = jnp.sum(taps_in[...], axis=0)

    def keep_wide(at, value):
        mixer_out[at] = value

    own_cube.total(keep_wide)
    for move in line_moves:
        move.wait_recv()
    gain_lines[my_line] = gain_line[...]
    gain_out[...] = jnp.sum(gain_lines[...], axis=0)
    far_move.wait_recv()

    def add_far(at):
        mixer_out[at] = wide(mixer_out[at], far_in[at])

    by_rows(mixer_out.shape[0], add_far)
    far_cube.close()
    own_cube.close()
    for move in (taps_move, back_move, far_move, *taps_moves, *gain_moves, *line_moves):
        move.wait_send()


def tail_call(parts_far, parts_own, back, d_hidden, inputs, scale, gain, gain_two, taps_own, taps_far):
    rows, width = inputs.shape
    piece = parts_own[0].shape[1]
    grad_width = parts_own[0].shape[2]
    pad = ((0, 8 - TAPS), (0, 0))
    taps_own, taps_far = jnp.pad(taps_own, pad), jnp.pad(taps_far, pad)
    taps_width = taps_own.shape[1]
    vmem = pl.BlockSpec(memory_space=pltpu.VMEM)
    anywhere = pl.BlockSpec(memory_space=pl.ANY)
    low = lambda *shape: pltpu.VMEM(shape, bf16)
    full = lambda *shape: pltpu.VMEM(shape, f32)
    copies = 48
    return pl.pallas_call(
        tail_kernel,
        in_specs=[vmem, anywhere, vmem, anywhere] + [vmem] * 8,
        out_specs=[vmem] * 4,
        out_shape=[
            jax.ShapeDtypeStruct((piece, grad_width), f32),
            jax.ShapeDtypeStruct((rows, width), bf16),
            jax.ShapeDtypeStruct((8, piece), f32),
            jax.ShapeDtypeStruct((8, taps_width), f32),
        ],
        scratch_shapes=[
            low(4, piece, grad_width),
            low(4, piece, grad_width),
            low(2, piece // 2, grad_width),
            low(2, piece // 2, grad_width),
            low(2, piece, grad_width),
            low(2, piece, grad_width),
            low(piece, grad_width),
            low(piece, grad_width),
            low(rows, width),
            low(rows, width),
            full(8, 8, piece),
            full(8, 8, piece),
            full(8, piece),
            full(4, 8, piece),
            full(8, taps_width),
            full(8, taps_width),
            full(8, 8, taps_width),
            pltpu.SemaphoreType.DMA((copies,)),
            pltpu.SemaphoreType.DMA((copies,)),
        ],
        compiler_params=pltpu.CompilerParams(
            collective_id=1, has_side_effects=True, vmem_limit_bytes=60 * 2**20
        ),
        cost_estimate=pl.CostEstimate(flops=10**8, bytes_accessed=3 * 10**8, transcendentals=0),
    )(
        parts_far[0], parts_far[1], parts_own[0], parts_own[1], back, d_hidden,
        inputs, scale, gain, gain_two, taps_own, taps_far,
    )


def turn_kernel(
    eb0, eb1, eb2, eb3, an0, an1, an2, an3, inner, d_gates, d_ups, hop_in, term0, term2, term3,
    hidden, scale, gain,
    down_out, gate_out, up_own, up_x, up_y, d_hidden, d_mix, gain_part,
    sens, normed, right_a, right_b, send_stage, moved, tops, lows, from_x, from_y, ring_in,
    load_sems, store_sems, swap_sends, swap_recvs, sends, recvs,
):
    my_dp, my_line = lax.axis_index("dp"), lax.axis_index("fsdp")
    my_chip, my_core = my_dp // 2, lax.rem(my_dp, 2)
    core = {"dp": lax.bitwise_xor(my_dp, CORE)}
    over_x = {"dp": lax.bitwise_xor(my_dp, XLINK)}
    over_y = {"dp": lax.bitwise_xor(my_dp, YLINK)}
    right = {"fsdp": lax.rem(my_line + 1, 4)}
    pair = {"fsdp": lax.bitwise_xor(my_line, 1)}
    rows = hidden.shape[0]
    piece = moved.shape[2]
    half = piece // 2

    loads = [0]

    def load(source, target):
        copy = pltpu.make_async_copy(source, target, load_sems.at[loads[0]])
        loads[0] += 1
        copy.start()
        return copy

    def load_rows(chunks, target):
        return [load(chunk, target.at[pl.ds(i * rows, rows)]) for i, chunk in enumerate(chunks)]

    first = load_rows((eb0, eb1, eb2, eb3), sens) + [load(inner, right_a)]
    second = load_rows((an0, an1, an2, an3), normed) + [load(d_gates, right_b)]
    greet(my_dp, my_line)
    wires = Wires(sends, recvs)

    def add_hop(source, term, step):
        def add(at):
            ring_in[step, at] = wide(source[at], term[at]).astype(bf16)

        by_rows(rows, add)
        return wires.to(ring_in.at[step], ring_in.at[step + 1], **right)

    hop2 = add_hop(hop_in, term2, 0)

    def swap(w, block):
        return pltpu.make_async_remote_copy(
            src_ref=send_stage.at[block],
            dst_ref=moved.at[w, block],
            send_sem=swap_sends.at[w, block],
            recv_sem=swap_recvs.at[w, block],
            device_id=core,
            device_id_type=MESH,
        )

    def across(w, side):
        source, target, device = (
            (moved.at[w, 3, pl.ds(0, half)], tops.at[w], over_x),
            (moved.at[w, 3, pl.ds(half, half)], lows.at[w], over_y),
        )[side]
        return pltpu.make_async_remote_copy(
            src_ref=source,
            dst_ref=target,
            send_sem=swap_sends.at[w, 4 + side],
            recv_sem=swap_recvs.at[w, 4 + side],
            device_id=device,
            device_id_type=MESH,
        )

    def weigh(w, left, right_ref, own):
        def product(block, side):
            place = 2 * lax.bitwise_xor(block, my_chip) + side
            columns = pl.ds(pl.multiple_of(place * piece, piece), piece)
            return contract_rows(left[:, columns], right_ref[...])

        def order(i):
            return jnp.where((i == 0) | (i == 3), 3 - i, i)

        if w:
            for block in range(4):
                swap(w - 1, block).wait_send()

        def give(i, carry):
            block = order(i)
            send_stage[block] = product(block, 1 - my_core).astype(bf16)
            swap(w, block).start()
            return carry

        def keep(i, carry):
            block = order(i)
            swap(w, block).wait_recv()
            value = product(block, my_core) + moved[w, block].astype(f32)
            moved[w, block] = value.astype(bf16)

            @pl.when(i == 0)
            def _():
                across(w, 0).start()
                across(w, 1).start()

            @pl.when(i == 3)
            def _():
                own[...] = value.astype(own.dtype)

            return carry

        lax.fori_loop(0, 4, give, 0)
        lax.fori_loop(0, 4, keep, 0)

    def sides(w):
        across(w, 0).wait_recv()
        across(w, 1).wait_recv()

        def add(at):
            below = pl.ds(pl.multiple_of(at.start + half, ROWS), ROWS)
            moved[w, 2, at] = wide(moved[w, 2, at], tops[w, at]).astype(bf16)
            moved[w, 1, below] = wide(moved[w, 1, below], lows[w, at]).astype(bf16)

        by_rows(half, add)

    for copy in first:
        copy.wait()
    weigh(0, sens, right_a, down_out)
    third = load(d_ups, right_a)
    for copy in second:
        copy.wait()
    weigh(1, normed, right_b, gate_out)
    sides(0)

    def sides_move(w):
        return [
            wires.to(moved.at[w, 1], from_x.at[w], **over_x),
            wires.to(moved.at[w, 2], from_y.at[w], **over_y),
        ]

    down_moves = sides_move(0)
    hop2.wait_recv()
    hop3 = add_hop(ring_in.at[1], term3, 1)
    third.wait()
    weigh(2, normed, right_a, up_own)
    sides(1)
    gate_moves = sides_move(1)
    hop3.wait_recv()
    gain_row = gain[...]

    def finish(i, total):
        at = pl.ds(pl.multiple_of(i * ROWS, ROWS), ROWS)
        grad = wide(ring_in[2, at], term0[at])
        values = hidden[at]
        r = scale[at]
        along = values * grad
        mean = jnp.mean(along * gain_row, axis=-1, keepdims=True)
        value = sens[at].astype(f32) + r * gain_row * grad - values * (r * r * r) * mean
        d_hidden[at] = value
        d_mix[at] = value.astype(bf16)
        return total + jnp.sum((along * r).reshape(ROWS // 8, 8, -1), axis=0)

    total = lax.fori_loop(0, rows // ROWS, finish, jnp.zeros((8, hidden.shape[1]), f32))
    pair_move = wires.to(d_mix.at[pl.ds(0, rows)], d_mix.at[pl.ds(rows, rows)], **pair)
    gain_part[...] = jnp.sum(total, axis=0, keepdims=True)
    sides(2)
    more = [
        pltpu.make_async_copy(moved.at[2, 1], up_x, store_sems.at[0]),
        pltpu.make_async_copy(moved.at[2, 2], up_y, store_sems.at[1]),
    ]
    for copy in more:
        copy.start()
    for w, moves, out in ((0, down_moves, down_out), (1, gate_moves, gate_out)):
        for move in moves:
            move.wait_recv()

        def add_sides(at):
            out[at] = wide(out[at], from_x[w, at], from_y[w, at])

        by_rows(piece, add_sides)
    pair_move.wait_recv()
    for copy in more:
        copy.wait()
    for block in range(4):
        swap(2, block).wait_send()
    for w in range(3):
        across(w, 0).wait_send()
        across(w, 1).wait_send()
    for move in (hop2, hop3, pair_move, *down_moves, *gate_moves):
        move.wait_send()


def turn_call(sens_all, normed_two, saved, hop_in, terms, hidden, scale, gain, piece):
    rows, width = hidden.shape
    inner_width = saved[0].shape[1]
    vmem = pl.BlockSpec(memory_space=pltpu.VMEM)
    anywhere = pl.BlockSpec(memory_space=pl.ANY)
    low = lambda *shape: pltpu.VMEM(shape, bf16)
    grad = jax.ShapeDtypeStruct((piece, inner_width), f32)
    side = jax.ShapeDtypeStruct((piece, inner_width), bf16)
    return pl.pallas_call(
        turn_kernel,
        in_specs=[anywhere] * 11 + [vmem] * 7,
        out_specs=[vmem] * 3 + [anywhere] * 2 + [vmem] * 3,
        out_shape=[
            grad,
            grad,
            side,
            side,
            side,
            jax.ShapeDtypeStruct((rows, width), f32),
            jax.ShapeDtypeStruct((2 * rows, width), bf16),
            jax.ShapeDtypeStruct((1, width), f32),
        ],
        scratch_shapes=[
            low(4 * rows, width),
            low(4 * rows, width),
            low(4 * rows, inner_width),
            low(4 * rows, inner_width),
            low(4, piece, inner_width),
            low(3, 4, piece, inner_width),
            low(3, piece // 2, inner_width),
            low(3, piece // 2, inner_width),
            low(2, piece, inner_width),
            low(2, piece, inner_width),
            low(3, rows, width),
            pltpu.SemaphoreType.DMA((12,)),
            pltpu.SemaphoreType.DMA((2,)),
            pltpu.SemaphoreType.DMA((3, 6)),
            pltpu.SemaphoreType.DMA((3, 6)),
            pltpu.SemaphoreType.DMA((8,)),
            pltpu.SemaphoreType.DMA((8,)),
        ],
        compiler_params=pltpu.CompilerParams(
            collective_id=2, has_side_effects=True, vmem_limit_bytes=60 * 2**20
        ),
        cost_estimate=pl.CostEstimate(
            flops=24 * rows * width * inner_width, bytes_accessed=2 * 10**8, transcendentals=0
        ),
    )(*sens_all, *normed_two, *saved, hop_in, *terms, hidden, scale, gain)


def total_all(value, axis):
    count = lax.axis_size(axis)
    offset = 1
    while offset < count:
        value = value + swapped(value, axis, offset)
        offset *= 2
    return value


def total_blocks(value, axis):
    count = lax.axis_size(axis)
    me = lax.axis_index(axis)
    offset = count // 2
    while offset:
        mine = me // offset % 2
        value = value.reshape((2, -1) + value.shape[1:])
        value = pick(value, 0, mine) + swapped(pick(value, 0, 1 - mine), axis, offset)
        offset //= 2
    return value[0]


def shards(
    tokens,
    cotangent,
    lengths,
    norm1_gain,
    in_weight,
    conv_taps,
    out_weight,
    norm2_gain,
    gate_weight,
    up_weight,
    down_weight,
):
    micro_count, group_count, span_len, model_width = tokens.shape
    line_count = micro_count * group_count
    row_count = line_count * span_len
    local_width = conv_taps.shape[1]
    piece = in_weight.shape[0]
    ring = lax.axis_size("fsdp")
    slices = range(0, ring, 2)
    cube = ring == 4 and lax.axis_size("dp") == 8
    my_line = lax.axis_index("fsdp")
    my_span = lax.axis_index("dp")
    slot_index = my_span * span_len + jnp.arange(span_len, dtype=jnp.int32)
    position = slot_index % SEQ_LEN
    seq_count = lengths.shape[2]
    seq_pick = (
        slot_index[:, None] // SEQ_LEN == jnp.arange(seq_count, dtype=jnp.int32)[None, :]
    ).astype(jnp.int32)
    valid_taps = [(position >= tap).astype(f32)[None, :, None] for tap in range(TAPS)]

    def from_owners(value):
        return lax.all_gather(value, "dp", axis=0, tiled=True)

    def to_owners(value):
        return lax.psum_scatter(value, "dp", scatter_dimension=0, tiled=True).astype(f32)

    inputs_f = tokens.reshape(row_count, model_width).astype(f32)
    lens = lengths.reshape(line_count, seq_count)
    seq_lens = jnp.sum(seq_pick[None, :, :] * lens[:, None, :], axis=2)
    live_mask = (position[None, :] < seq_lens).astype(f32).reshape(row_count, 1)
    sens_own = live_mask * cotangent.reshape(row_count, model_width).astype(f32)

    mixer_shard = jnp.concatenate([in_weight.reshape(piece, -1), out_weight.T], 1)
    pair_lines, pair_rows = 2 * line_count, 2 * row_count
    if cube:
        sens_low = sens_own.astype(bf16)
        pad = ((0, 8 - TAPS), (0, 0))
        (
            in_own, in_far, back_own, back_far, gate_full, up_full, down_back, sens1, sens2, sens3,
            normed_pair, proj_own, proj_far, conv_own, conv_far, gated_own, gated_far, rim_own, rim_far,
            hidden_one, normed, coming, scale_one, scale_two, gain_one, gain_two,
        ) = head_call(
            mixer_shard,
            gate_weight,
            up_weight,
            down_weight.T,
            sens_low,
            tokens.reshape(row_count, model_width),
            jnp.pad(jnp.stack([norm1_gain, norm2_gain]).astype(f32), ((0, 6), (0, 0))),
            jnp.pad(conv_taps.astype(f32), pad),
            span_len,
        )
        gain_one, gain_two = gain_one[0], gain_two[0]
        sens_all = [sens_low, sens1, sens2, sens3]
        kept = []
        for in_full, out_back, proj, conv, gated, rim, taps in (
            (in_own, back_own, proj_own, conv_own, gated_own, rim_own, conv_taps),
            (in_far, back_far, proj_far, conv_far, gated_far, rim_far, swapped(conv_taps, "fsdp", 2)),
        ):
            b_part = proj[:, :local_width]
            c_part = proj[:, local_width : 2 * local_width]
            x_part = proj[:, 2 * local_width :]
            padded = jnp.concatenate(
                [rim[:, 8 - (TAPS - 1) :], (b_part * x_part).reshape(pair_lines, span_len, local_width)], 1
            )
            kept.append(
                (in_full, out_back, taps.astype(f32), b_part, c_part, x_part, padded, conv, gated)
            )
    else:
        gains = from_owners(jnp.stack([norm1_gain, norm2_gain], 1)).astype(f32)
        gain_one, gain_two = gains[:, 0], gains[:, 1]
        gain_one, mixer_shard, gate_weight, up_weight, down_weight = lax.optimization_barrier(
            (gain_one, mixer_shard, gate_weight, up_weight, down_weight)
        )
        shards_of = [mixer_shard] + [swapped(mixer_shard, "fsdp", c) for c in slices[1:]]
        taps_of = [conv_taps] + [swapped(conv_taps, "fsdp", c) for c in slices[1:]]
        mixer_widths = (3 * local_width, local_width)
        mixers, sent = [None], ()
        mixers[0], sent = gather_cube(mixer_shard, mixer_widths, sent)
        for shard in shards_of[1:]:
            mixer, sent = gather_cube(shard, mixer_widths, sent)
            mixers.append(mixer)
        gate_full = from_owners(gate_weight)
        up_full = from_owners(up_weight)
        down_back = from_owners(down_weight.T)

        scale_one = rms_scale(inputs_f)
        normed_own = (inputs_f * scale_one * gain_one).astype(bf16)
        normed_pair = jnp.concatenate([normed_own, swapped(normed_own, "fsdp", 1)], 0)
        sens_low, _ = lax.optimization_barrier((sens_own.astype(bf16), shards_of[-1]))
        sens_all = ring_gather(sens_low, "fsdp")

        kept = []
        mixed = jnp.zeros((pair_rows, model_width), f32)
        for (in_full, out_back), taps in zip(mixers, taps_of):
            taps_f = taps.astype(f32)
            early = ring // 2 if not kept else ring - 1
            normed_pair, sens_all[early] = lax.optimization_barrier((normed_pair, sens_all[early]))
            projected = times(normed_pair, in_full)
            b_part = projected[:, :local_width]
            c_part = projected[:, local_width : 2 * local_width]
            x_part = projected[:, 2 * local_width :]
            mixed_in = (b_part * x_part).reshape(pair_lines, span_len, local_width)
            rim_in = passed_along(mixed_in[:, span_len - (TAPS - 1) :], "dp", 1)
            padded = jnp.concatenate([rim_in, mixed_in], 1)
            convolved = jnp.zeros_like(mixed_in)
            for tap in range(TAPS):
                convolved = (
                    convolved
                    + taps_f[tap][None, None, :]
                    * padded[:, TAPS - 1 - tap : TAPS - 1 - tap + span_len]
                    * valid_taps[tap]
                )
            convolved = convolved.reshape(pair_rows, local_width)
            gated = (c_part * convolved).astype(bf16)
            kept.append((in_full, out_back, taps_f, b_part, c_part, x_part, padded, convolved, gated))
            mixed = mixed + times_transposed(gated, out_back)
        moved = swapped(mixed[row_count:].astype(bf16), "fsdp", 1)
        hidden_one = inputs_f + mixed[:row_count] + moved.astype(f32)
        scale_two = rms_scale(hidden_one)
        normed = (hidden_one * scale_two * gain_two).astype(bf16)

    normed_two, terms, back_terms, saved = [], [], [], ()
    for step, sens in enumerate(sens_all):
        normed_two.append(normed)
        if step < ring - 1 and not (cube and step == 0):
            coming = passed_round(normed, "fsdp")
        *saved, term, back_term = ffn_chunk(
            normed, sens, gate_full, up_full, down_back, saved, step, ring
        )
        terms.append(term)
        back_terms.append(back_term)
        if step == ring - 1:
            break
        normed, back_terms[0] = lax.optimization_barrier((coming, back_terms[0])) if step == 0 else (coming, back_terms[0])
        if cube and step == 2:
            back_terms[1], normed = lax.optimization_barrier((back_terms[1], normed))
            hop_in = passed_round(back_terms[1], "fsdp")
    if cube:
        (
            down_grad, gate_grad, up_own, up_x, up_y, d_hidden, d_mix, gain_two_part,
        ) = turn_call(
            sens_all,
            normed_two,
            saved,
            hop_in,
            (back_terms[0], back_terms[2], back_terms[3]),
            hidden_one,
            scale_two,
            gain_two[None],
            piece,
        )
        d_mix, terms[1] = lax.optimization_barrier((d_mix, terms[1]))
        hop = passed_round(terms[1], "fsdp")
        up_from = (swapped(up_x, "dp", XLINK), swapped(up_y, "dp", YLINK))
    else:
        d_normed_two = ring_collect([term.astype(f32) for term in back_terms], "fsdp")
        inner, d_gates, d_ups = saved
        sens_rows = jnp.concatenate(sens_all, 0)
        normed_rows = jnp.concatenate(normed_two, 0)
        down_grad = to_owners(contract_rows(sens_rows, inner).astype(bf16))
        gate_grad = to_owners(contract_rows(normed_rows, d_gates).astype(bf16))
        up_grad = to_owners(contract_rows(normed_rows, d_ups).astype(bf16))
        gain_two_part = jnp.sum(d_normed_two * hidden_one * scale_two, axis=0)
        d_hidden = (
            sens_own
            + scale_two * gain_two * d_normed_two
            - hidden_one
            * scale_two**3
            * jnp.mean(hidden_one * gain_two * d_normed_two, axis=-1, keepdims=True)
        )
        d_hidden_low = d_hidden.astype(bf16)
        d_mix = jnp.concatenate([d_hidden_low, swapped(d_hidden_low, "fsdp", 1)], 0)

    tap_parts, sums = [], []
    d_normed = jnp.zeros((pair_rows, model_width), f32)
    for in_full, out_back, taps_f, b_part, c_part, x_part, padded, convolved, gated in kept[::-1]:
        d_gated = times(d_mix, out_back)
        d_c_part = d_gated * convolved
        d_conv = (d_gated * c_part).reshape(pair_lines, span_len, local_width)
        d_padded = jnp.zeros_like(padded)
        tap_rows = []
        for tap in range(TAPS):
            weighted = d_conv * valid_taps[tap]
            d_padded = d_padded + jnp.pad(
                taps_f[tap][None, None, :] * weighted,
                ((0, 0), (TAPS - 1 - tap, tap), (0, 0)),
            )
            tap_rows.append(
                jnp.sum(weighted * padded[:, TAPS - 1 - tap : TAPS - 1 - tap + span_len], axis=(0, 1))
            )
        tap_parts.append(jnp.stack(tap_rows, 0))
        rim_back = passed_along(d_padded[:, : TAPS - 1], "dp", -1)
        d_mixed = (
            d_padded[:, TAPS - 1 :]
            + jnp.pad(rim_back, ((0, 0), (span_len - (TAPS - 1), 0), (0, 0)))
        ).reshape(pair_rows, local_width)
        d_proj = jnp.concatenate([d_mixed * x_part, d_c_part, d_mixed * b_part], axis=1).astype(bf16)
        d_normed = d_normed + times_transposed(d_proj, in_full)
        parts = weight_grad([([normed_pair], d_proj), ([d_mix], gated)], piece)
        if cube:
            step = len(sums) + 2
            d_mix, d_normed, hop, *parts = lax.optimization_barrier((d_mix, d_normed, hop, *parts))
            hop = passed_round(wide(hop, terms[step]).astype(bf16), "fsdp")
            sums.append(parts)
            continue
        d_mix, d_normed, *parts = lax.optimization_barrier((d_mix, d_normed, *parts))
        sums.append(CubeSum(parts))
    if cube:
        mixer_sum, token_grad, gain_grads, taps_grad = tail_call(
            sums[0],
            sums[1],
            d_normed,
            d_hidden,
            tokens.reshape(row_count, model_width),
            scale_one,
            gain_one[None],
            gain_two_part,
            tap_parts[1],
            tap_parts[0],
        )
        block_out = (live_mask * wide(hidden_one, hop, terms[0])).astype(bf16)
        up_grad = wide(up_own, *up_from)
        return (
            block_out.reshape(tokens.shape),
            token_grad.reshape(tokens.shape),
            gain_grads[0],
            mixer_sum[:, : 3 * local_width].reshape(in_weight.shape),
            taps_grad[:TAPS],
            mixer_sum[:, 3 * local_width :].T,
            gain_grads[1],
            gate_grad,
            up_grad,
            down_grad.T,
        )
    moved = swapped(d_normed[row_count:].astype(bf16), "fsdp", 1)
    for step in sums[:-1]:
        (moved,) = step.diagonal(moved)
    for step in sums[:-1]:
        (moved,) = step.sides(moved)
    (moved,) = sums[-1].diagonal(moved)
    (moved,) = sums[-1].sides(moved)
    d_normed_one = d_normed[:row_count] + moved.astype(f32)
    gain_one_part = jnp.sum(d_normed_one * inputs_f * scale_one, axis=0)
    token_grad = (
        d_hidden
        + scale_one * gain_one * d_normed_one
        - inputs_f
        * scale_one**3
        * jnp.mean(inputs_f * gain_one * d_normed_one, axis=-1, keepdims=True)
    ).astype(bf16)

    mixer_sum = sums[-1].total()
    for c, step in list(zip(slices[::-1], sums))[:-1]:
        mixer_sum = mixer_sum + swapped(step.total().astype(bf16), "fsdp", c).astype(f32)
    in_grad = mixer_sum[:, : 3 * local_width].reshape(in_weight.shape)
    out_grad = mixer_sum[:, 3 * local_width :].T

    ffn_out = ring_collect([term.astype(f32) for term in terms], "fsdp")
    block_out = (live_mask * (hidden_one + ffn_out)).astype(bf16)

    taps_sum = tap_parts[-1]
    for c, part in list(zip(slices[::-1], tap_parts))[:-1]:
        taps_sum = taps_sum + swapped(part, "fsdp", c)
    taps_grad = total_all(taps_sum, "dp")
    gain_grads = total_blocks(
        jnp.concatenate(
            [gain_one_part.reshape(-1, piece), gain_two_part.reshape(-1, piece)], 1
        ),
        "dp",
    )
    gain_grads = total_all(gain_grads, "fsdp").reshape(2, piece)
    return (
        block_out.reshape(tokens.shape),
        token_grad.reshape(tokens.shape),
        gain_grads[0],
        in_grad,
        taps_grad,
        out_grad,
        gain_grads[1],
        gate_grad,
        up_grad,
        down_grad.T,
    )


def solution(mesh):
    rows = P(None, "fsdp", "dp", None)
    return jax.shard_map(
        shards,
        mesh=mesh,
        in_specs=(
            rows,
            rows,
            P(None, "fsdp", None),
            P("dp"),
            P("dp", None, "fsdp"),
            P(None, "fsdp"),
            P("fsdp", "dp"),
            P("dp"),
            P("dp", "fsdp"),
            P("dp", "fsdp"),
            P("fsdp", "dp"),
        ),
        out_specs=(
            rows,
            rows,
            P("dp"),
            P("dp", None, "fsdp"),
            P(None, "fsdp"),
            P("fsdp", "dp"),
            P("dp"),
            P("dp", "fsdp"),
            P("dp", "fsdp"),
            P("fsdp", "dp"),
        ),
        check_vma=False,
    )
```

```python
import functools

import jax
import jax.numpy as jnp
from jax import lax
from jax.experimental import pallas as pl
from jax.experimental.pallas import tpu as pltpu
from jax.sharding import PartitionSpec as P

SEQ_LEN = 1024
TAPS = 3

norm_eps = 1e-05
f32 = jnp.float32
bf16 = jnp.bfloat16


def passed_along(value, axis, steps):
    count = lax.axis_size(axis)
    first, last = (max(0, -steps), min(count, count - steps))
    return lax.ppermute(value, axis, [(source, source + steps) for source in range(first, last)])


def passed_round(value, axis):
    count = lax.axis_size(axis)
    return lax.ppermute(value, axis, [(source, (source + 1) % count) for source in range(count)])


def ring_gather(value, axis):
    chunks = [value]
    for _ in range(lax.axis_size(axis) - 1):
        chunks.append(passed_round(chunks[-1], axis))
    return chunks


def ring_collect(terms, axis):
    count = lax.axis_size(axis)
    total = terms[1 % count]
    for step in range(1, count):
        moved = passed_round(total.astype(bf16), axis)
        total = wide(moved, terms[(step + 1) % count])
    return total


def rms_scale(values):
    return lax.rsqrt(jnp.mean(values * values, axis=-1, keepdims=True) + norm_eps)


def times(left, right):
    return jnp.dot(left, right, preferred_element_type=f32)


def times_transposed(left, right):
    return lax.dot_general(left, right, (((1,), (1,)), ((), ())), preferred_element_type=f32)


def contract_rows(left, right):
    return lax.dot_general(left, right, (((0,), (0,)), ((), ())), preferred_element_type=f32)


def ffn_kernel(a_ref, e_ref, gate_ref, up_ref, down_ref, *refs):
    m_ref, dg_ref, du_ref, term_ref, back_ref, out_ref, da_ref = refs[-7:]

    @pl.when(pl.program_id(0) == 0)
    def _():
        out_ref[...] = jnp.zeros_like(out_ref)
        da_ref[...] = jnp.zeros_like(da_ref)

    rows, sens = a_ref[...], e_ref[...]
    gate_pre = times(rows, gate_ref[...])
    up_pre = times(rows, up_ref[...])
    d_inner = times(sens, down_ref[...])
    sigmoid_gate = 1.0 / (1.0 + jnp.exp(-gate_pre))
    silu_gate = gate_pre * sigmoid_gate
    inner = (silu_gate * up_pre).astype(bf16)
    d_gate = (d_inner * up_pre * (sigmoid_gate * (1.0 + gate_pre * (1.0 - sigmoid_gate)))).astype(bf16)
    d_up = (d_inner * silu_gate).astype(bf16)
    m_ref[...] = inner
    dg_ref[...] = d_gate
    du_ref[...] = d_up
    out_ref[...] += times_transposed(inner, down_ref[...])
    da_ref[...] += times_transposed(d_gate, gate_ref[...]) + times_transposed(d_up, up_ref[...])

    @pl.when(pl.program_id(0) == pl.num_programs(0) - 1)
    def _():
        term_ref[...] = out_ref[...].astype(bf16)
        back_ref[...] = da_ref[...].astype(bf16)


def ffn_chunk(normed, sens, gate_full, up_full, down_back, saved, step, steps, tile=512):
    rows, width = normed.shape
    hidden = gate_full.shape[1]
    whole = pl.BlockSpec((rows, width), lambda i: (0, 0))
    weight = pl.BlockSpec((width, tile), lambda i: (0, i))
    part = pl.BlockSpec((rows, tile), lambda i: (step, i))
    act = jax.ShapeDtypeStruct((steps * rows, hidden), bf16)
    total = jax.ShapeDtypeStruct((rows, width), bf16)
    return pl.pallas_call(
        ffn_kernel,
        grid=(hidden // tile,),
        in_specs=[whole, whole, weight, weight, weight]
        + [pl.BlockSpec(memory_space=pl.ANY)] * len(saved),
        out_specs=[part, part, part, whole, whole],
        out_shape=[act, act, act, total, total],
        scratch_shapes=[pltpu.VMEM((rows, width), f32)] * 2,
        input_output_aliases={5 + i: i for i in range(len(saved))},
        compiler_params=pltpu.CompilerParams(vmem_limit_bytes=48 * 2**20),
        cost_estimate=pl.CostEstimate(
            flops=12 * rows * width * hidden,
            bytes_accessed=6 * width * hidden + 12 * rows * width + 6 * rows * hidden,
            transcendentals=rows * hidden,
        ),
    )(normed, sens, gate_full, up_full, down_back, *saved)


def swapped(value, axis, offset):
    count = lax.axis_size(axis)
    return lax.ppermute(value, axis, [(source, source ^ offset) for source in range(count)])


CORE, XLINK, YLINK = 1, 2, 4


def gather_cube(shard, widths, after):
    if after:
        shard = lax.optimization_barrier((shard, *after))[0]
    if lax.axis_size("dp") != 8:
        full = lax.all_gather(shard, "dp", axis=0, tiled=True)
        ends = [sum(widths[: i + 1]) for i in range(len(widths))]
        return [full[:, end - width : end] for end, width in zip(ends, widths)], ()
    rows = shard.shape[0]
    half = rows // 2
    over_x = swapped(shard, "dp", XLINK)
    over_y = swapped(shard, "dp", YLINK)
    diag_top = swapped(over_x[:half], "dp", YLINK)
    diag_low = swapped(over_y[half:], "dp", XLINK)
    pieces = [
        (shard, 0, 0),
        (over_x, XLINK, 0),
        (over_y, YLINK, 0),
        (diag_top, XLINK | YLINK, 0),
        (diag_low, XLINK | YLINK, half),
    ]
    pieces += [(swapped(v, "dp", CORE), offset ^ CORE, at) for v, offset, at in pieces]

    count = len(pieces)

    def kernel(*refs):
        ins, outs = refs[:count], refs[count : count + len(widths)]
        held, in_sems, out_sems = refs[count + len(widths) :]
        me = lax.axis_index("dp")
        copies = []
        for i, (value, offset, at) in enumerate(pieces):
            start = pl.multiple_of(lax.bitwise_xor(me, offset) * rows + at, half)
            copies.append(
                pltpu.make_async_copy(
                    ins[i], held.at[pl.ds(start, value.shape[0]), :], in_sems.at[i]
                )
            )
        for copy in copies:
            copy.start()
        for copy in copies:
            copy.wait()
        copies, first = [], 0
        for j, width in enumerate(widths):
            copies.append(
                pltpu.make_async_copy(held.at[:, pl.ds(first, width)], outs[j], out_sems.at[j])
            )
            first += width
        for copy in copies:
            copy.start()
        for copy in copies:
            copy.wait()

    spec = pl.BlockSpec(memory_space=pl.ANY)
    full = pl.pallas_call(
        kernel,
        in_specs=[spec] * count,
        out_specs=[spec] * len(widths),
        out_shape=[jax.ShapeDtypeStruct((8 * rows, width), shard.dtype) for width in widths],
        scratch_shapes=[
            pltpu.VMEM((8 * rows, sum(widths)), shard.dtype),
            pltpu.SemaphoreType.DMA((count,)),
            pltpu.SemaphoreType.DMA((len(widths),)),
        ],
        cost_estimate=pl.CostEstimate(
            flops=0, bytes_accessed=32 * rows * sum(widths), transcendentals=0
        ),
    )(*[value for value, _, _ in pieces])
    return full, (over_x, over_y)


def pick(value, axis, index):
    return lax.dynamic_index_in_dim(value, index, axis, keepdims=False)


def grad_kernel(pairs, chunks, order_ref, *refs):
    keep_ref, send_ref = refs[-2:]
    for out_ref, at in ((keep_ref, 0), (send_ref, 1)):
        first = 0
        for pair in range(pairs):
            base = pair * (2 * chunks + 1)
            left = [refs[base + at * chunks + i][...] for i in range(chunks)]
            left = left[0] if chunks == 1 else jnp.concatenate(left, 0)
            right = refs[base + 2 * chunks]
            width = right.shape[1]
            out_ref[0, :, first : first + width] = contract_rows(left, right[...]).astype(bf16)
            first += width


def weight_grad(pairs, piece):
    chunks = len(pairs[0][0])
    width = sum(right.shape[1] for _, right in pairs)
    rows = pairs[0][1].shape[0]
    if lax.axis_size("dp") != 8:
        return (
            jnp.concatenate(
                [contract_rows(jnp.concatenate(left, 0), right).astype(bf16) for left, right in pairs], 1
            ),
        )
    me = lax.axis_index("dp")
    order = jnp.stack([me % 2, me // 2]).astype(jnp.int32)
    out = pl.BlockSpec((1, piece, width), lambda i, o: (i, 0, 0))
    chip = jax.ShapeDtypeStruct((4, piece, width), bf16)
    specs, values = [], []
    for left, right in pairs:
        lead = (left[0].shape[0], piece)
        specs += [pl.BlockSpec(lead, lambda i, o: (0, 2 * (i ^ o[1]) + o[0]))] * chunks
        specs += [pl.BlockSpec(lead, lambda i, o: (0, 2 * (i ^ o[1]) + 1 - o[0]))] * chunks
        specs += [pl.BlockSpec(right.shape, lambda i, o: (0, 0))]
        values += list(left) + list(left) + [right]
    return pl.pallas_call(
        functools.partial(grad_kernel, len(pairs), chunks),
        grid_spec=pltpu.PrefetchScalarGridSpec(
            num_scalar_prefetch=1, grid=(4,), in_specs=specs, out_specs=[out, out]
        ),
        out_shape=[chip, chip],
        compiler_params=pltpu.CompilerParams(vmem_limit_bytes=48 * 2**20),
        cost_estimate=pl.CostEstimate(
            flops=16 * rows * piece * width,
            bytes_accessed=16 * piece * width + 16 * rows * piece + 2 * rows * width,
            transcendentals=0,
        ),
    )(order, *values)


def wide(*values):
    total = values[0].astype(f32)
    for value in values[1:]:
        total = total + value.astype(f32)
    return total


class CubeSum:
    def __init__(self, parts):
        if len(parts) == 1:
            self.whole = lax.psum_scatter(parts[0], "dp", scatter_dimension=0, tiled=True).astype(f32)
            return
        self.whole = None
        self.keep = parts[0]
        self.moved = swapped(parts[1], "dp", CORE)

    def diagonal(self, *after):
        if self.whole is not None:
            return after
        half = self.keep.shape[1] // 2
        diag, *after = lax.optimization_barrier(
            (wide(self.keep[3], self.moved[3]).astype(bf16), *after)
        )
        self.top = swapped(diag[:half], "dp", XLINK)
        self.low = swapped(diag[half:], "dp", YLINK)
        return after

    def sides(self, *after):
        if self.whole is not None:
            return after
        half = self.keep.shape[1] // 2
        over_x = jnp.concatenate(
            [
                wide(self.keep[1, :half], self.moved[1, :half]).astype(bf16),
                wide(self.keep[1, half:], self.moved[1, half:], self.low).astype(bf16),
            ],
            0,
        )
        over_y = jnp.concatenate(
            [
                wide(self.keep[2, :half], self.moved[2, :half], self.top).astype(bf16),
                wide(self.keep[2, half:], self.moved[2, half:]).astype(bf16),
            ],
            0,
        )
        over_x, over_y, *after = lax.optimization_barrier((over_x, over_y, *after))
        self.from_x = swapped(over_x, "dp", XLINK)
        self.from_y = swapped(over_y, "dp", YLINK)
        return after

    def total(self):
        if self.whole is not None:
            return self.whole
        return wide(self.keep[0], self.moved[0], self.from_x, self.from_y)


MESH = pl.DeviceIdType.MESH
ROWS = 16


class Wires:
    def __init__(self, sends, recvs):
        self.sends, self.recvs, self.used = sends, recvs, 0

    def to(self, source, target, **device):
        copy = pltpu.make_async_remote_copy(
            src_ref=source,
            dst_ref=target,
            send_sem=self.sends.at[self.used],
            recv_sem=self.recvs.at[self.used],
            device_id=device,
            device_id_type=MESH,
        )
        self.used += 1
        copy.start()
        return copy


def greet(my_dp, my_line):
    barrier = pltpu.get_barrier_semaphore()
    for offset in range(1, 8):
        pl.semaphore_signal(
            barrier, inc=1, device_id={"dp": lax.bitwise_xor(my_dp, offset)}, device_id_type=MESH
        )
    for offset in range(1, 4):
        pl.semaphore_signal(
            barrier, inc=1, device_id={"fsdp": lax.bitwise_xor(my_line, offset)}, device_id_type=MESH
        )
    pl.semaphore_wait(barrier, 10)


def by_rows(count, body):
    def step(i, carry):
        body(pl.ds(pl.multiple_of(i * ROWS, ROWS), ROWS))
        return carry

    lax.fori_loop(0, count // ROWS, step, 0)


class CubeWires:
    def __init__(self, my_dp, product, stage, moved, top, low, from_x, from_y, own, sends, recvs):
        self.product, self.stage, self.moved, self.own = product, stage, moved, own
        self.top, self.low, self.from_x, self.from_y = top, low, from_x, from_y
        self.sends, self.recvs = sends, recvs
        self.my_core = lax.rem(my_dp, 2)
        self.core = {"dp": lax.bitwise_xor(my_dp, CORE)}
        self.x = {"dp": lax.bitwise_xor(my_dp, XLINK)}
        self.y = {"dp": lax.bitwise_xor(my_dp, YLINK)}
        self.rows = moved.shape[1]
        self.half = moved.shape[1] // 2

    def copy(self, i, source, target, device):
        return pltpu.make_async_remote_copy(
            src_ref=source,
            dst_ref=target,
            send_sem=self.sends.at[i],
            recv_sem=self.recvs.at[i],
            device_id=device,
            device_id_type=MESH,
        )

    def swap(self, block):
        return self.copy(block, self.stage.at[block], self.moved.at[block], self.core)

    def corner(self, i):
        if i == 0:
            return self.copy(4, self.moved.at[3, pl.ds(0, self.half)], self.top, self.x)
        return self.copy(5, self.moved.at[3, pl.ds(self.half, self.half)], self.low, self.y)

    def side(self, block, part):
        at = pl.ds(part * self.half, self.half)
        target, device = ((self.from_x, self.x), (self.from_y, self.y))[block - 1]
        return self.copy(4 + 2 * block + part, self.moved.at[block, at], target.at[at], device)

    def give(self):
        def step(i, carry):
            block = jnp.where((i == 0) | (i == 3), 3 - i, i)
            self.stage[block] = self.product(block, 1 - self.my_core)
            self.swap(block).start()
            return carry

        lax.fori_loop(0, 4, step, 0)

    def keep(self):
        def step(i, carry):
            block = jnp.where((i == 0) | (i == 3), 3 - i, i)
            self.swap(block).wait_recv()
            value = wide(self.product(block, self.my_core), self.moved[block])
            self.moved[block] = value.astype(bf16)

            @pl.when(i == 0)
            def _():
                self.corner(0).start()
                self.corner(1).start()

            @pl.when(i == 1)
            def _():
                self.side(1, 0).start()

            @pl.when(i == 2)
            def _():
                self.side(2, 1).start()

            if self.own is not None:

                @pl.when(i == 3)
                def _():
                    self.own[...] = value

            return carry

        lax.fori_loop(0, 4, step, 0)

    def others(self):
        self.corner(0).wait_recv()

        def add_top(at):
            self.moved[2, at] = wide(self.moved[2, at], self.top[at]).astype(bf16)

        by_rows(self.half, add_top)
        self.side(2, 0).start()
        self.corner(1).wait_recv()

        def add_low(at):
            below = pl.ds(pl.multiple_of(at.start + self.half, ROWS), ROWS)
            self.moved[1, below] = wide(self.moved[1, below], self.low[at]).astype(bf16)

        by_rows(self.half, add_low)
        self.side(1, 1).start()

    def total(self, store):
        for block in (1, 2):
            for part in range(2):
                self.side(block, part).wait_recv()

        own = self.moved.at[0] if self.own is None else self.own

        def add(at):
            store(at, wide(own[at], self.from_x[at], self.from_y[at]))

        by_rows(self.rows, add)

    def close_stage(self):
        for block in range(4):
            self.swap(block).wait_send()

    def close(self):
        for i in range(2):
            self.corner(i).wait_send()
        for block in (1, 2):
            for part in range(2):
                self.side(block, part).wait_send()


class Spread:
    def __init__(self, wires, my_dp, shard, full, own_sem):
        self.wires, self.my_dp, self.shard, self.full, self.own_sem = wires, my_dp, shard, full, own_sem
        self.rows = shard.shape[0]
        self.core = {"dp": lax.bitwise_xor(my_dp, CORE)}
        self.x = {"dp": lax.bitwise_xor(my_dp, XLINK)}
        self.y = {"dp": lax.bitwise_xor(my_dp, YLINK)}

    def block(self, offset, first=0, count=None):
        half = self.rows // 2
        start = lax.bitwise_xor(self.my_dp, offset) * self.rows + first
        return self.full.at[pl.ds(pl.multiple_of(start, half), count or self.rows)]

    def start(self):
        own = self.block(0)
        self.own = pltpu.make_async_copy(self.shard, own, self.own_sem)
        self.own.start()
        self.over_x = self.wires.to(self.shard, own, **self.x)
        self.over_y = self.wires.to(self.shard, own, **self.y)
        self.cores = [self.wires.to(self.shard, own, **self.core)]

    def pass_on(self, block, **device):
        return self.wires.to(block, block, **device)

    def relay(self):
        half = self.rows // 2
        self.over_x.wait_recv()
        self.top = self.pass_on(self.block(XLINK, 0, half), **self.y)
        self.over_y.wait_recv()
        self.low = self.pass_on(self.block(YLINK, half, half), **self.x)
        self.cores += [self.pass_on(self.block(offset), **self.core) for offset in (XLINK, YLINK)]

    def finish(self):
        half = self.rows // 2
        for move, first in ((self.top, 0), (self.low, half)):
            move.wait_recv()
            self.cores.append(self.pass_on(self.block(XLINK | YLINK, first, half), **self.core))

    def complete(self):
        self.own.wait()
        for move in self.cores:
            move.wait_recv()

    def close(self):
        for move in (self.over_x, self.over_y, self.top, self.low, *self.cores):
            move.wait_send()


def head_kernel(
    span, mixer, gate, up, down, sens, inputs, gains, taps,
    in_own, in_far, back_own, back_far, gate_full, up_full, down_full, sens1, sens2, sens3,
    normed, proj_own, proj_far, conv_own, conv_far, gated_own, gated_far, rim_own, rim_far,
    hidden, normed_two, normed_next, scale_one, scale_two, gain_one, gain_two,
    full_own, full_far, mixer_far, taps_far, total, lines_own, lines_far, mix_out, mix_in, gains_in,
    own_sems, out_sems, sends, recvs,
):
    my_dp, my_line = lax.axis_index("dp"), lax.axis_index("fsdp")
    right = {"fsdp": lax.rem(my_line + 1, 4)}
    pair = {"fsdp": lax.bitwise_xor(my_line, 1)}
    far = {"fsdp": lax.bitwise_xor(my_line, 2)}
    wires = Wires(sends, recvs)
    rows, width = inputs.shape
    piece = gains.shape[1]
    local = taps.shape[1]
    line_count = 2 * rows // span
    greet(my_dp, my_line)

    gain_moves = [
        wires.to(gains, gains_in.at[my_dp], dp=lax.bitwise_xor(my_dp, offset)) for offset in range(1, 8)
    ]
    taps_move = wires.to(taps, taps_far, **far)
    spreads = [
        Spread(wires, my_dp, shard, full, own_sems.at[i])
        for i, (shard, full) in enumerate(
            ((mixer, full_own), (mixer_far, full_far), (gate, gate_full), (up, up_full), (down, down_full))
        )
    ]
    one, two, gates, ups, downs = spreads
    one.start()
    mixer_move = wires.to(mixer, mixer_far, **far)
    gains_in[my_dp] = gains[...]
    for move in gain_moves:
        move.wait_recv()
    for block in range(8):
        gain_one[:, block * piece : (block + 1) * piece] = gains_in[block, 0:1]
        gain_two[:, block * piece : (block + 1) * piece] = gains_in[block, 1:2]
    gain_row, gain_next = gain_one[...], gain_two[...]

    def first_norm(at):
        values = inputs[at].astype(f32)
        r = lax.rsqrt(jnp.mean(values * values, axis=-1, keepdims=True) + norm_eps)
        scale_one[at] = r
        normed[at] = (values * r * gain_row).astype(bf16)

    by_rows(rows, first_norm)
    normed_move = wires.to(normed.at[pl.ds(0, rows)], normed.at[pl.ds(rows, rows)], **pair)

    def mix(full, proj, conv, gated, rim, lines, taps_ref, first):
        def project(j, carry):
            columns = pl.ds(pl.multiple_of(j * local, local), local)
            proj[:, columns] = times(normed[...], full[:, columns])
            return carry

        lax.fori_loop(0, 3, project, 0)

        @pl.when(my_dp == 0)
        def _():
            lines[:, 0:8] = jnp.zeros((line_count, 8, local), f32)

        def gate_in(i, carry):
            at = pl.ds(pl.multiple_of(i * span, span), span)
            lines[i, 8 : 8 + span] = proj[at, 0:local] * proj[at, 2 * local : 3 * local]
            return carry

        lax.fori_loop(0, line_count, gate_in, 0)
        rim_move = pltpu.make_async_remote_copy(
            src_ref=lines.at[:, pl.ds(span, 8)],
            dst_ref=lines.at[:, pl.ds(0, 8)],
            send_sem=sends.at[wires.used],
            recv_sem=recvs.at[wires.used],
            device_id={"dp": jnp.minimum(my_dp + 1, 7)},
            device_id_type=MESH,
        )
        wires.used += 1

        @pl.when(my_dp < 7)
        def _():
            rim_move.start()

        @pl.when(my_dp > 0)
        def _():
            rim_move.wait_recv()

        rim[...] = lines[:, 0:8]
        tap_rows = [taps_ref[tap : tap + 1] for tap in range(TAPS)]

        def convolve(i, carry):
            for base in range(0, span, ROWS):
                at = pl.ds(pl.multiple_of(i * span + base, ROWS), ROWS)
                spot = my_dp * span + base + lax.broadcasted_iota(jnp.int32, (ROWS, 1), 0)
                position = lax.rem(spot, SEQ_LEN)
                value = tap_rows[0] * lines[i, 8 + base : 8 + base + ROWS]
                for tap in range(1, TAPS):
                    before = tap_rows[tap] * lines[i, 8 + base - tap : 8 + base - tap + ROWS]
                    value = value + jnp.where(position >= tap, before, 0.0)
                conv[at] = value
                gated[at] = (proj[at, local : 2 * local] * value).astype(bf16)
            return carry

        lax.fori_loop(0, line_count, convolve, 0)

        def back(j, carry):
            columns = pl.ds(pl.multiple_of(j * local, local), local)
            value = times_transposed(gated[...], full[columns, 3 * local : 4 * local])
            total[:, columns] = value if first else total[:, columns] + value
            return carry

        lax.fori_loop(0, width // local, back, 0)
        return rim_move

    def write_out(full, in_ref, back_ref, i):
        copies = [
            pltpu.make_async_copy(full.at[:, pl.ds(0, 3 * local)], in_ref, out_sems.at[2 * i]),
            pltpu.make_async_copy(full.at[:, pl.ds(3 * local, local)], back_ref, out_sems.at[2 * i + 1]),
        ]
        for copy in copies:
            copy.start()
        return copies

    one.relay()
    gates.start()
    taps_move.wait_recv()
    mixer_move.wait_recv()
    sens_moves = [wires.to(sens, sens1, **right)]
    two.start()
    one.finish()
    normed_move.wait_recv()
    one.complete()
    rims = [mix(full_own, proj_own, conv_own, gated_own, rim_own, lines_own, taps, True)]
    outs = write_out(full_own, in_own, back_own, 0)
    gates.relay()
    ups.start()
    sens_moves[0].wait_recv()
    sens_moves.append(wires.to(sens1, sens2, **right))
    two.relay()
    gates.finish()
    sens_moves[1].wait_recv()
    sens_moves.append(wires.to(sens2, sens3, **right))
    two.finish()
    two.complete()
    rims.append(mix(full_far, proj_far, conv_far, gated_far, rim_far, lines_far, taps_far, False))

    def shorten(at):
        mix_out[at] = total[pl.ds(pl.multiple_of(at.start + rows, ROWS), ROWS)].astype(bf16)

    by_rows(rows, shorten)
    mix_move = wires.to(mix_out, mix_in, **pair)
    outs += write_out(full_far, in_far, back_far, 1)
    ups.relay()
    downs.start()
    mix_move.wait_recv()

    def second_norm(at):
        values = wide(inputs[at], total[at], mix_in[at])
        hidden[at] = values
        r = lax.rsqrt(jnp.mean(values * values, axis=-1, keepdims=True) + norm_eps)
        scale_two[at] = r
        normed_two[at] = (values * r * gain_next).astype(bf16)

    by_rows(rows, second_norm)
    next_move = wires.to(normed_two, normed_next, **right)
    ups.finish()
    downs.relay()
    downs.finish()
    sens_moves[2].wait_recv()
    for spread in (gates, ups, downs):
        spread.complete()
    next_move.wait_recv()
    for copy in outs:
        copy.wait()
    for spread in spreads:
        spread.close()

    @pl.when(my_dp < 7)
    def _():
        for move in rims:
            move.wait_send()

    for move in (taps_move, mixer_move, normed_move, mix_move, next_move, *gain_moves, *sens_moves):
        move.wait_send()


def head_call(mixer, gate, up, down, sens, inputs, gains, taps, span):
    rows, width = inputs.shape
    piece = mixer.shape[0]
    local = taps.shape[1]
    hidden = gate.shape[1]
    lines = 2 * rows // span
    vmem = pl.BlockSpec(memory_space=pltpu.VMEM)
    anywhere = pl.BlockSpec(memory_space=pl.ANY)
    low = lambda *shape: pltpu.VMEM(shape, bf16)
    full = lambda *shape: pltpu.VMEM(shape, f32)
    out = lambda kind, *shape: jax.ShapeDtypeStruct(shape, kind)
    copies = 80
    return pl.pallas_call(
        functools.partial(head_kernel, span),
        in_specs=[anywhere] * 5 + [vmem] * 3,
        out_specs=[anywhere] * 10 + [vmem] * 16,
        out_shape=[
            out(bf16, width, 3 * local),
            out(bf16, width, 3 * local),
            out(bf16, width, local),
            out(bf16, width, local),
            out(bf16, width, hidden),
            out(bf16, width, hidden),
            out(bf16, width, hidden),
            out(bf16, rows, width),
            out(bf16, rows, width),
            out(bf16, rows, width),
            out(bf16, 2 * rows, width),
            out(f32, 2 * rows, 3 * local),
            out(f32, 2 * rows, 3 * local),
            out(f32, 2 * rows, local),
            out(f32, 2 * rows, local),
            out(bf16, 2 * rows, local),
            out(bf16, 2 * rows, local),
            out(f32, lines, 8, local),
            out(f32, lines, 8, local),
            out(f32, rows, width),
            out(bf16, rows, width),
            out(bf16, rows, width),
            out(f32, rows, 1),
            out(f32, rows, 1),
            out(f32, 1, width),
            out(f32, 1, width),
        ],
        scratch_shapes=[
            low(width, 4 * local),
            low(width, 4 * local),
            low(piece, 4 * local),
            full(*taps.shape),
            full(2 * rows, width),
            full(lines, 8 + span, local),
            full(lines, 8 + span, local),
            low(rows, width),
            low(rows, width),
            full(8, 8, piece),
            pltpu.SemaphoreType.DMA((5,)),
            pltpu.SemaphoreType.DMA((4,)),
            pltpu.SemaphoreType.DMA((copies,)),
            pltpu.SemaphoreType.DMA((copies,)),
        ],
        compiler_params=pltpu.CompilerParams(
            collective_id=3, has_side_effects=True, vmem_limit_bytes=60 * 2**20
        ),
        cost_estimate=pl.CostEstimate(
            flops=32 * rows * width * local, bytes_accessed=2 * 10**8, transcendentals=0
        ),
    )(mixer, gate, up, down, sens, inputs, gains, taps)


def rear_kernel(
    span, up_x, up_y, in_far, in_own, back_far, back_own, proj_far, proj_own, conv_far, conv_own, hop_in, term,
    normed, d_mix, d_hidden, gated_far, gated_own, rim_far, rim_own, inputs, scale, gain, gain_two, taps_own,
    mixer_out, token_out, gain_out, taps_out, up_from_x, up_from_y, hop_out,
    in_full, backs, parts, lines_far, lines_own, line, d_far, d_own, stage, moved_far, moved_own,
    tops, lows, from_x, from_y, far_in, total, back_in, hop_mid, hop_term,
    gain_cut, gain_in, gain_line, gain_lines, taps_given, taps_got, taps_part, taps_pair, taps_sum, taps_in,
    loads, cube_sends, cube_recvs, sends, recvs,
):
    my_dp, my_line = lax.axis_index("dp"), lax.axis_index("fsdp")
    my_chip = my_dp // 2
    pair = {"fsdp": lax.bitwise_xor(my_line, 1)}
    far = {"fsdp": lax.bitwise_xor(my_line, 2)}
    wires = Wires(sends, recvs)
    rows = inputs.shape[0]
    width = inputs.shape[1]
    piece = gain_out.shape[1]
    local = taps_own.shape[1]
    line_count = 2 * rows // span
    loaded = [0]

    def load(source, target):
        copy = pltpu.make_async_copy(source, target, loads.at[loaded[0]])
        loaded[0] += 1
        copy.start()
        return copy

    def column(proj, part):
        return proj.at[:, pl.ds(part * local, local)]

    early_far = [
        load(back_far, backs.at[0]), load(column(proj_far, 1), parts.at[0]), load(conv_far, parts.at[1])
    ]
    early_own = [
        load(back_own, backs.at[1]), load(column(proj_own, 1), parts.at[2]), load(conv_own, parts.at[3])
    ]
    in_load = load(in_far, in_full)
    term_load = load(term, hop_term)
    greet(my_dp, my_line)
    right = {"fsdp": lax.rem(my_line + 1, 4)}
    taps_move = wires.to(taps_own, taps_got, **far)
    hops = [wires.to(hop_in, hop_mid, **right)]

    def open_slice(i, early, lines, d_proj):
        for copy in early:
            copy.wait()

        def spread_rows(j, carry):
            at = pl.ds(pl.multiple_of(j * span, span), span)
            lines[j, 8 : 8 + span] = times(d_mix[at], backs[i])
            return carry

        lax.fori_loop(0, line_count, spread_rows, 0)

        @pl.when(my_dp == 7)
        def _():
            lines[:, 8 + span : 16 + span] = jnp.zeros((line_count, 8, local), f32)

        def share(j, carry):
            for base in range(0, span, ROWS):
                at = pl.ds(pl.multiple_of(j * span + base, ROWS), ROWS)
                d_gated = lines[j, 8 + base : 8 + base + ROWS]
                d_proj[at, local : 2 * local] = (d_gated * parts[2 * i + 1, at]).astype(bf16)
                lines[j, 8 + base : 8 + base + ROWS] = d_gated * parts[2 * i, at]
            return carry

        lax.fori_loop(0, line_count, share, 0)
        move = pltpu.make_async_remote_copy(
            src_ref=lines.at[:, pl.ds(8, 8)],
            dst_ref=lines.at[:, pl.ds(8 + span, 8)],
            send_sem=sends.at[wires.used],
            recv_sem=recvs.at[wires.used],
            device_id={"dp": jnp.maximum(my_dp - 1, 0)},
            device_id_type=MESH,
        )
        wires.used += 1

        @pl.when(my_dp > 0)
        def _():
            move.start()

        return move

    def close_slice(i, late, rim_move, lines, rim, d_proj, taps_ref):
        for copy in late:
            copy.wait()

        @pl.when(my_dp < 7)
        def _():
            rim_move.wait_recv()

        tap_rows = [taps_ref[tap : tap + 1] for tap in range(TAPS)]

        def convolve(j, sums):
            line[0:8] = rim[j]
            for base in range(0, span, ROWS):
                at = pl.ds(pl.multiple_of(j * span + base, ROWS), ROWS)
                line[8 + base : 8 + base + ROWS] = parts[2 * i, at] * parts[2 * i + 1, at]
            sums = list(sums)
            for base in range(0, span, ROWS):
                at = pl.ds(pl.multiple_of(j * span + base, ROWS), ROWS)
                spot = my_dp * span + base + lax.broadcasted_iota(jnp.int32, (ROWS, 1), 0)
                here = lines[j, 8 + base : 8 + base + ROWS]
                value = tap_rows[0] * here
                for tap in range(TAPS):
                    before = line[8 + base - tap : 8 + base - tap + ROWS]
                    valid = lax.rem(spot, SEQ_LEN) >= tap
                    grad = jnp.where(valid, here * before, 0.0)
                    sums[tap] = sums[tap] + jnp.sum(grad.reshape(ROWS // 8, 8, local), axis=0)
                for tap in range(1, TAPS):
                    after = tap_rows[tap] * lines[j, 8 + base + tap : 8 + base + tap + ROWS]
                    valid = lax.rem(spot + tap, SEQ_LEN) >= tap
                    value = value + jnp.where(valid, after, 0.0)
                d_proj[at, 0:local] = (value * parts[2 * i, at]).astype(bf16)
                d_proj[at, 2 * local : 3 * local] = (value * parts[2 * i + 1, at]).astype(bf16)
            return tuple(sums)

        sums = lax.fori_loop(0, line_count, convolve, (jnp.zeros((8, local), f32),) * TAPS)
        for tap in range(TAPS):
            taps_part[i, tap : tap + 1] = jnp.sum(sums[tap], axis=0, keepdims=True)

    def late_loads(i, proj):
        return [load(column(proj, 2), parts.at[2 * i]), load(column(proj, 0), parts.at[2 * i + 1])]

    def weigher(d_proj, gated):
        def product(block, side):
            place = 2 * lax.bitwise_xor(block, my_chip) + side
            columns = pl.ds(pl.multiple_of(place * piece, piece), piece)
            return jnp.concatenate(
                [
                    contract_rows(normed[:, columns], d_proj[...]).astype(bf16),
                    contract_rows(d_mix[:, columns], gated[...]).astype(bf16),
                ],
                1,
            )

        return product

    def back_rows(d_proj, first):
        def step(j, carry):
            columns = pl.ds(pl.multiple_of(j * local, local), local)
            value = times_transposed(d_proj[...], in_full[columns, :])
            total[:, columns] = value if first else total[:, columns] + value
            return carry

        lax.fori_loop(0, width // local, step, 0)

    rims = [open_slice(0, early_far, lines_far, d_far)]
    late_far = late_loads(0, proj_far)
    rims.append(open_slice(1, early_own, lines_own, d_own))
    late_own = late_loads(1, proj_own)
    taps_part[...] = jnp.zeros_like(taps_part)
    taps_move.wait_recv()
    close_slice(0, late_far, rims[0], lines_far, rim_far, d_far, taps_got)
    far_cube = CubeWires(
        my_dp, weigher(d_far, gated_far), stage, moved_far, tops.at[0], lows.at[0],
        from_x.at[0], from_y.at[0], None, cube_sends.at[0], cube_recvs.at[0],
    )
    own_cube = CubeWires(
        my_dp, weigher(d_own, gated_own), stage, moved_own, tops.at[1], lows.at[1],
        from_x.at[1], from_y.at[1], mixer_out, cube_sends.at[1], cube_recvs.at[1],
    )
    far_cube.give()
    far_cube.keep()
    close_slice(1, late_own, rims[1], lines_own, rim_own, d_own, taps_own)
    taps_given[...] = taps_part[0]
    taps_back = wires.to(taps_given, taps_pair, **far)
    in_load.wait()
    back_rows(d_far, True)
    in_load = load(in_own, in_full)
    term_load.wait()
    hops[0].wait_recv()

    def add_hop(at):
        hop_mid[at] = wide(hop_mid[at], hop_term[at]).astype(bf16)

    by_rows(rows, add_hop)
    hops.append(wires.to(hop_mid, hop_out, **right))
    far_cube.others()
    up_moves = [
        wires.to(up_x, up_from_x, dp=lax.bitwise_xor(my_dp, XLINK)),
        wires.to(up_y, up_from_y, dp=lax.bitwise_xor(my_dp, YLINK)),
    ]
    far_cube.close_stage()
    own_cube.give()
    own_cube.keep()
    in_load.wait()
    back_rows(d_own, False)

    own_cube.close_stage()

    def shorten(at):
        stage[0, at] = total[pl.ds(pl.multiple_of(at.start + rows, ROWS), ROWS)].astype(bf16)

    by_rows(rows, shorten)
    back_move = wires.to(stage.at[0], back_in, **pair)
    taps_back.wait_recv()
    taps_sum[...] = taps_part[1] + taps_pair[...]
    taps_moves = [
        wires.to(taps_sum, taps_in.at[my_dp], dp=lax.bitwise_xor(my_dp, offset)) for offset in range(1, 8)
    ]

    def keep_low(at, value):
        stage[1, at] = value.astype(bf16)

    far_cube.total(keep_low)
    far_move = wires.to(stage.at[1], far_in, **far)
    own_cube.others()
    back_move.wait_recv()
    gain_row = gain[...]
    gain_cut[...] = jnp.zeros_like(gain_cut)

    def finish(i, part):
        at = pl.ds(pl.multiple_of(i * ROWS, ROWS), ROWS)
        grad = wide(total[at], back_in[at])
        values = inputs[at].astype(f32)
        r = scale[at]
        along = values * grad
        mean = jnp.mean(along * gain_row, axis=-1, keepdims=True)
        token_out[at] = (d_hidden[at] + r * gain_row * grad - values * (r * r * r) * mean).astype(bf16)
        return part + jnp.sum((along * r).reshape(ROWS // 8, 8, -1), axis=0)

    part = lax.fori_loop(0, rows // ROWS, finish, jnp.zeros((8, width), f32))
    part = jnp.sum(part, axis=0, keepdims=True)
    for block in range(8):
        gain_cut[block, 0:1] = part[:, block * piece : (block + 1) * piece]
        gain_cut[block, 1:2] = gain_two[:, block * piece : (block + 1) * piece]
    gain_moves = []
    for offset in range(1, 8):
        peer = lax.bitwise_xor(my_dp, offset)
        gain_moves.append(wires.to(gain_cut.at[peer], gain_in.at[my_dp], dp=peer))
    gain_in[my_dp] = gain_cut[my_dp]
    for move in gain_moves:
        move.wait_recv()
    gain_line[...] = jnp.sum(gain_in[...], axis=0)
    line_moves = [
        wires.to(gain_line, gain_lines.at[my_line], fsdp=lax.bitwise_xor(my_line, offset))
        for offset in range(1, 4)
    ]
    for move in taps_moves:
        move.wait_recv()
    taps_in[my_dp] = taps_sum[...]
    taps_out[...] = jnp.sum(taps_in[...], axis=0)

    def keep_wide(at, value):
        mixer_out[at] = value

    own_cube.total(keep_wide)
    for move in line_moves:
        move.wait_recv()
    gain_lines[my_line] = gain_line[...]
    gain_out[...] = jnp.sum(gain_lines[...], axis=0)
    far_move.wait_recv()

    def add_far(at):
        mixer_out[at] = wide(mixer_out[at], far_in[at])

    by_rows(piece, add_far)
    for move in (*up_moves, hops[1]):
        move.wait_recv()
    far_cube.close()
    own_cube.close()

    @pl.when(my_dp > 0)
    def _():
        for move in rims:
            move.wait_send()

    for move in (taps_move, taps_back, back_move, far_move, *hops, *up_moves, *taps_moves, *gain_moves, *line_moves):
        move.wait_send()


def rear_call(up_sides, ins, backs, projs, convs, hop_in, term, normed, d_mix, d_hidden, gated, rims, inputs, scale, gain, gain_two, taps, span):
    rows, width = inputs.shape
    piece = up_sides[0].shape[0]
    local = taps.shape[1]
    grad_width = 4 * local
    lines = 2 * rows // span
    vmem = pl.BlockSpec(memory_space=pltpu.VMEM)
    anywhere = pl.BlockSpec(memory_space=pl.ANY)
    low = lambda *shape: pltpu.VMEM(shape, bf16)
    full = lambda *shape: pltpu.VMEM(shape, f32)
    out = lambda kind, *shape: jax.ShapeDtypeStruct(shape, kind)
    copies = 48
    return pl.pallas_call(
        functools.partial(rear_kernel, span),
        in_specs=[anywhere] * 12 + [vmem] * 12,
        out_specs=[vmem] * 4 + [anywhere] * 3,
        out_shape=[
            out(f32, piece, grad_width),
            out(bf16, rows, width),
            out(f32, 8, piece),
            out(f32, 8, local),
            out(bf16, *up_sides[0].shape),
            out(bf16, *up_sides[1].shape),
            out(bf16, rows, width),
        ],
        scratch_shapes=[
            low(width, 3 * local),
            low(2, width, local),
            full(4, 2 * rows, local),
            full(lines, span + 16, local),
            full(lines, span + 16, local),
            full(span + 8, local),
            low(2 * rows, 3 * local),
            low(2 * rows, 3 * local),
            low(4, piece, grad_width),
            low(4, piece, grad_width),
            low(4, piece, grad_width),
            low(2, piece // 2, grad_width),
            low(2, piece // 2, grad_width),
            low(2, piece, grad_width),
            low(2, piece, grad_width),
            low(piece, grad_width),
            full(2 * rows, width),
            low(rows, width),
            low(rows, width),
            low(rows, width),
            full(8, 8, piece),
            full(8, 8, piece),
            full(8, piece),
            full(4, 8, piece),
            full(8, local),
            full(8, local),
            full(2, 8, local),
            full(8, local),
            full(8, local),
            full(8, 8, local),
            pltpu.SemaphoreType.DMA((16,)),
            pltpu.SemaphoreType.DMA((2, 10)),
            pltpu.SemaphoreType.DMA((2, 10)),
            pltpu.SemaphoreType.DMA((copies,)),
            pltpu.SemaphoreType.DMA((copies,)),
        ],
        compiler_params=pltpu.CompilerParams(
            collective_id=1, has_side_effects=True, vmem_limit_bytes=60 * 2**20
        ),
        cost_estimate=pl.CostEstimate(
            flops=64 * rows * width * local, bytes_accessed=10**8, transcendentals=0
        ),
    )(
        *up_sides, *ins, *backs, *projs, *convs, hop_in, term, normed, d_mix, d_hidden, *gated, *rims,
        inputs, scale, gain, gain_two, taps,
    )


def turn_kernel(
    eb0, eb1, eb2, eb3, an0, an1, an2, an3, inner, d_gates, d_ups, hop_in, term0, term2, term3,
    hidden, scale, gain,
    down_out, gate_out, up_own, up_x, up_y, d_hidden, d_mix, gain_part,
    sens, normed, right_a, right_b, send_stage, moved, tops, lows, from_x, from_y, ring_in,
    load_sems, store_sems, swap_sends, swap_recvs, sends, recvs,
):
    my_dp, my_line = lax.axis_index("dp"), lax.axis_index("fsdp")
    my_chip, my_core = my_dp // 2, lax.rem(my_dp, 2)
    core = {"dp": lax.bitwise_xor(my_dp, CORE)}
    over_x = {"dp": lax.bitwise_xor(my_dp, XLINK)}
    over_y = {"dp": lax.bitwise_xor(my_dp, YLINK)}
    right = {"fsdp": lax.rem(my_line + 1, 4)}
    pair = {"fsdp": lax.bitwise_xor(my_line, 1)}
    rows = hidden.shape[0]
    piece = moved.shape[2]
    half = piece // 2

    loads = [0]

    def load(source, target):
        copy = pltpu.make_async_copy(source, target, load_sems.at[loads[0]])
        loads[0] += 1
        copy.start()
        return copy

    def load_rows(chunks, target):
        return [load(chunk, target.at[pl.ds(i * rows, rows)]) for i, chunk in enumerate(chunks)]

    first = load_rows((eb0, eb1, eb2, eb3), sens) + [load(inner, right_a)]
    second = load_rows((an0, an1, an2, an3), normed) + [load(d_gates, right_b)]
    greet(my_dp, my_line)
    wires = Wires(sends, recvs)

    def add_hop(source, term, step):
        def add(at):
            ring_in[step, at] = wide(source[at], term[at]).astype(bf16)

        by_rows(rows, add)
        return wires.to(ring_in.at[step], ring_in.at[step + 1], **right)

    hop2 = add_hop(hop_in, term2, 0)

    def swap(w, block):
        return pltpu.make_async_remote_copy(
            src_ref=send_stage.at[block],
            dst_ref=moved.at[w, block],
            send_sem=swap_sends.at[w, block],
            recv_sem=swap_recvs.at[w, block],
            device_id=core,
            device_id_type=MESH,
        )

    def across(w, side):
        source, target, device = (
            (moved.at[w, 3, pl.ds(0, half)], tops.at[w], over_x),
            (moved.at[w, 3, pl.ds(half, half)], lows.at[w], over_y),
        )[side]
        return pltpu.make_async_remote_copy(
            src_ref=source,
            dst_ref=target,
            send_sem=swap_sends.at[w, 4 + side],
            recv_sem=swap_recvs.at[w, 4 + side],
            device_id=device,
            device_id_type=MESH,
        )

    def weigh(w, left, right_ref, own):
        def product(block, side):
            place = 2 * lax.bitwise_xor(block, my_chip) + side
            columns = pl.ds(pl.multiple_of(place * piece, piece), piece)
            return contract_rows(left[:, columns], right_ref[...])

        def order(i):
            return jnp.where((i == 0) | (i == 3), 3 - i, i)

        if w:
            for block in range(4):
                swap(w - 1, block).wait_send()

        def give(i, carry):
            block = order(i)
            send_stage[block] = product(block, 1 - my_core).astype(bf16)
            swap(w, block).start()
            return carry

        def keep(i, carry):
            block = order(i)
            swap(w, block).wait_recv()
            value = product(block, my_core) + moved[w, block].astype(f32)
            moved[w, block] = value.astype(bf16)

            @pl.when(i == 0)
            def _():
                across(w, 0).start()
                across(w, 1).start()

            @pl.when(i == 3)
            def _():
                own[...] = value.astype(own.dtype)

            return carry

        lax.fori_loop(0, 4, give, 0)
        lax.fori_loop(0, 4, keep, 0)

    def sides(w):
        across(w, 0).wait_recv()
        across(w, 1).wait_recv()

        def add(at):
            below = pl.ds(pl.multiple_of(at.start + half, ROWS), ROWS)
            moved[w, 2, at] = wide(moved[w, 2, at], tops[w, at]).astype(bf16)
            moved[w, 1, below] = wide(moved[w, 1, below], lows[w, at]).astype(bf16)

        by_rows(half, add)

    for copy in first:
        copy.wait()
    weigh(0, sens, right_a, down_out)
    third = load(d_ups, right_a)
    for copy in second:
        copy.wait()
    weigh(1, normed, right_b, gate_out)
    sides(0)

    def sides_move(w):
        return [
            wires.to(moved.at[w, 1], from_x.at[w], **over_x),
            wires.to(moved.at[w, 2], from_y.at[w], **over_y),
        ]

    down_moves = sides_move(0)
    hop2.wait_recv()
    hop3 = add_hop(ring_in.at[1], term3, 1)
    third.wait()
    weigh(2, normed, right_a, up_own)
    sides(1)
    gate_moves = sides_move(1)
    hop3.wait_recv()
    gain_row = gain[...]

    def finish(i, total):
        at = pl.ds(pl.multiple_of(i * ROWS, ROWS), ROWS)
        grad = wide(ring_in[2, at], term0[at])
        values = hidden[at]
        r = scale[at]
        along = values * grad
        mean = jnp.mean(along * gain_row, axis=-1, keepdims=True)
        value = sens[at].astype(f32) + r * gain_row * grad - values * (r * r * r) * mean
        d_hidden[at] = value
        d_mix[at] = value.astype(bf16)
        return total + jnp.sum((along * r).reshape(ROWS // 8, 8, -1), axis=0)

    total = lax.fori_loop(0, rows // ROWS, finish, jnp.zeros((8, hidden.shape[1]), f32))
    pair_move = wires.to(d_mix.at[pl.ds(0, rows)], d_mix.at[pl.ds(rows, rows)], **pair)
    gain_part[...] = jnp.sum(total, axis=0, keepdims=True)
    sides(2)
    more = [
        pltpu.make_async_copy(moved.at[2, 1], up_x, store_sems.at[0]),
        pltpu.make_async_copy(moved.at[2, 2], up_y, store_sems.at[1]),
    ]
    for copy in more:
        copy.start()
    for w, moves, out in ((0, down_moves, down_out), (1, gate_moves, gate_out)):
        for move in moves:
            move.wait_recv()

        def add_sides(at):
            out[at] = wide(out[at], from_x[w, at], from_y[w, at])

        by_rows(piece, add_sides)
    pair_move.wait_recv()
    for copy in more:
        copy.wait()
    for block in range(4):
        swap(2, block).wait_send()
    for w in range(3):
        across(w, 0).wait_send()
        across(w, 1).wait_send()
    for move in (hop2, hop3, pair_move, *down_moves, *gate_moves):
        move.wait_send()


def turn_call(sens_all, normed_two, saved, hop_in, terms, hidden, scale, gain, piece):
    rows, width = hidden.shape
    inner_width = saved[0].shape[1]
    vmem = pl.BlockSpec(memory_space=pltpu.VMEM)
    anywhere = pl.BlockSpec(memory_space=pl.ANY)
    low = lambda *shape: pltpu.VMEM(shape, bf16)
    grad = jax.ShapeDtypeStruct((piece, inner_width), f32)
    side = jax.ShapeDtypeStruct((piece, inner_width), bf16)
    return pl.pallas_call(
        turn_kernel,
        in_specs=[anywhere] * 11 + [vmem] * 7,
        out_specs=[vmem] * 3 + [anywhere] * 2 + [vmem] * 3,
        out_shape=[
            grad,
            grad,
            side,
            side,
            side,
            jax.ShapeDtypeStruct((rows, width), f32),
            jax.ShapeDtypeStruct((2 * rows, width), bf16),
            jax.ShapeDtypeStruct((1, width), f32),
        ],
        scratch_shapes=[
            low(4 * rows, width),
            low(4 * rows, width),
            low(4 * rows, inner_width),
            low(4 * rows, inner_width),
            low(4, piece, inner_width),
            low(3, 4, piece, inner_width),
            low(3, piece // 2, inner_width),
            low(3, piece // 2, inner_width),
            low(2, piece, inner_width),
            low(2, piece, inner_width),
            low(3, rows, width),
            pltpu.SemaphoreType.DMA((12,)),
            pltpu.SemaphoreType.DMA((2,)),
            pltpu.SemaphoreType.DMA((3, 6)),
            pltpu.SemaphoreType.DMA((3, 6)),
            pltpu.SemaphoreType.DMA((8,)),
            pltpu.SemaphoreType.DMA((8,)),
        ],
        compiler_params=pltpu.CompilerParams(
            collective_id=2, has_side_effects=True, vmem_limit_bytes=60 * 2**20
        ),
        cost_estimate=pl.CostEstimate(
            flops=24 * rows * width * inner_width, bytes_accessed=2 * 10**8, transcendentals=0
        ),
    )(*sens_all, *normed_two, *saved, hop_in, *terms, hidden, scale, gain)


def total_all(value, axis):
    count = lax.axis_size(axis)
    offset = 1
    while offset < count:
        value = value + swapped(value, axis, offset)
        offset *= 2
    return value


def total_blocks(value, axis):
    count = lax.axis_size(axis)
    me = lax.axis_index(axis)
    offset = count // 2
    while offset:
        mine = me // offset % 2
        value = value.reshape((2, -1) + value.shape[1:])
        value = pick(value, 0, mine) + swapped(pick(value, 0, 1 - mine), axis, offset)
        offset //= 2
    return value[0]


def shards(
    tokens,
    cotangent,
    lengths,
    norm1_gain,
    in_weight,
    conv_taps,
    out_weight,
    norm2_gain,
    gate_weight,
    up_weight,
    down_weight,
):
    micro_count, group_count, span_len, model_width = tokens.shape
    line_count = micro_count * group_count
    row_count = line_count * span_len
    local_width = conv_taps.shape[1]
    piece = in_weight.shape[0]
    ring = lax.axis_size("fsdp")
    slices = range(0, ring, 2)
    cube = ring == 4 and lax.axis_size("dp") == 8 and row_count == piece
    my_line = lax.axis_index("fsdp")
    my_span = lax.axis_index("dp")
    slot_index = my_span * span_len + jnp.arange(span_len, dtype=jnp.int32)
    position = slot_index % SEQ_LEN
    seq_count = lengths.shape[2]
    seq_pick = (
        slot_index[:, None] // SEQ_LEN == jnp.arange(seq_count, dtype=jnp.int32)[None, :]
    ).astype(jnp.int32)
    valid_taps = [(position >= tap).astype(f32)[None, :, None] for tap in range(TAPS)]

    def from_owners(value):
        return lax.all_gather(value, "dp", axis=0, tiled=True)

    def to_owners(value):
        return lax.psum_scatter(value, "dp", scatter_dimension=0, tiled=True).astype(f32)

    inputs_f = tokens.reshape(row_count, model_width).astype(f32)
    lens = lengths.reshape(line_count, seq_count)
    seq_lens = jnp.sum(seq_pick[None, :, :] * lens[:, None, :], axis=2)
    live_mask = (position[None, :] < seq_lens).astype(f32).reshape(row_count, 1)
    sens_own = live_mask * cotangent.reshape(row_count, model_width).astype(f32)

    mixer_shard = jnp.concatenate([in_weight.reshape(piece, -1), out_weight.T], 1)
    pair_lines, pair_rows = 2 * line_count, 2 * row_count
    if cube:
        sens_low = sens_own.astype(bf16)
        taps_low = jnp.pad(conv_taps.astype(f32), ((0, 8 - TAPS), (0, 0)))
        (
            in_own, in_far, back_own, back_far, gate_full, up_full, down_back, sens1, sens2, sens3,
            normed_pair, proj_own, proj_far, conv_own, conv_far, gated_own, gated_far, rim_own, rim_far,
            hidden_one, normed, coming, scale_one, scale_two, gain_one, gain_two,
        ) = head_call(
            mixer_shard,
            gate_weight,
            up_weight,
            down_weight.T,
            sens_low,
            tokens.reshape(row_count, model_width),
            jnp.pad(jnp.stack([norm1_gain, norm2_gain]).astype(f32), ((0, 6), (0, 0))),
            taps_low,
            span_len,
        )
        gain_one, gain_two = gain_one[0], gain_two[0]
        sens_all = [sens_low, sens1, sens2, sens3]
    else:
        gains = from_owners(jnp.stack([norm1_gain, norm2_gain], 1)).astype(f32)
        gain_one, gain_two = gains[:, 0], gains[:, 1]
        gain_one, mixer_shard, gate_weight, up_weight, down_weight = lax.optimization_barrier(
            (gain_one, mixer_shard, gate_weight, up_weight, down_weight)
        )
        shards_of = [mixer_shard] + [swapped(mixer_shard, "fsdp", c) for c in slices[1:]]
        taps_of = [conv_taps] + [swapped(conv_taps, "fsdp", c) for c in slices[1:]]
        mixer_widths = (3 * local_width, local_width)
        mixers, sent = [None], ()
        mixers[0], sent = gather_cube(mixer_shard, mixer_widths, sent)
        for shard in shards_of[1:]:
            mixer, sent = gather_cube(shard, mixer_widths, sent)
            mixers.append(mixer)
        gate_full = from_owners(gate_weight)
        up_full = from_owners(up_weight)
        down_back = from_owners(down_weight.T)

        scale_one = rms_scale(inputs_f)
        normed_own = (inputs_f * scale_one * gain_one).astype(bf16)
        normed_pair = jnp.concatenate([normed_own, swapped(normed_own, "fsdp", 1)], 0)
        sens_low, _ = lax.optimization_barrier((sens_own.astype(bf16), shards_of[-1]))
        sens_all = ring_gather(sens_low, "fsdp")

        kept = []
        mixed = jnp.zeros((pair_rows, model_width), f32)
        for (in_full, out_back), taps in zip(mixers, taps_of):
            taps_f = taps.astype(f32)
            early = ring // 2 if not kept else ring - 1
            normed_pair, sens_all[early] = lax.optimization_barrier((normed_pair, sens_all[early]))
            projected = times(normed_pair, in_full)
            b_part = projected[:, :local_width]
            c_part = projected[:, local_width : 2 * local_width]
            x_part = projected[:, 2 * local_width :]
            mixed_in = (b_part * x_part).reshape(pair_lines, span_len, local_width)
            rim_in = passed_along(mixed_in[:, span_len - (TAPS - 1) :], "dp", 1)
            padded = jnp.concatenate([rim_in, mixed_in], 1)
            convolved = jnp.zeros_like(mixed_in)
            for tap in range(TAPS):
                convolved = (
                    convolved
                    + taps_f[tap][None, None, :]
                    * padded[:, TAPS - 1 - tap : TAPS - 1 - tap + span_len]
                    * valid_taps[tap]
                )
            convolved = convolved.reshape(pair_rows, local_width)
            gated = (c_part * convolved).astype(bf16)
            kept.append((in_full, out_back, taps_f, b_part, c_part, x_part, padded, convolved, gated))
            mixed = mixed + times_transposed(gated, out_back)
        moved = swapped(mixed[row_count:].astype(bf16), "fsdp", 1)
        hidden_one = inputs_f + mixed[:row_count] + moved.astype(f32)
        scale_two = rms_scale(hidden_one)
        normed = (hidden_one * scale_two * gain_two).astype(bf16)

    normed_two, terms, back_terms, saved = [], [], [], ()
    for step, sens in enumerate(sens_all):
        normed_two.append(normed)
        if step < ring - 1 and not (cube and step == 0):
            coming = passed_round(normed, "fsdp")
        *saved, term, back_term = ffn_chunk(
            normed, sens, gate_full, up_full, down_back, saved, step, ring
        )
        terms.append(term)
        back_terms.append(back_term)
        if step == ring - 1:
            break
        normed, back_terms[0] = lax.optimization_barrier((coming, back_terms[0])) if step == 0 else (coming, back_terms[0])
        if cube and step == 2:
            back_terms[1], normed = lax.optimization_barrier((back_terms[1], normed))
            hop_in = passed_round(back_terms[1], "fsdp")
    if cube:
        hop_in, terms[1] = lax.optimization_barrier((hop_in, terms[1]))
        hop = passed_round(terms[1], "fsdp")
        (
            down_grad, gate_grad, up_own, up_x, up_y, d_hidden, d_mix, gain_two_part,
        ) = turn_call(
            sens_all,
            normed_two,
            saved,
            hop_in,
            (back_terms[0], back_terms[2], back_terms[3]),
            hidden_one,
            scale_two,
            gain_two[None],
            piece,
        )
        hop = wide(hop, terms[2]).astype(bf16)
        mixer_sum, token_grad, gain_grads, taps_grad, *up_from, hop = rear_call(
            (up_x, up_y),
            (in_far, in_own),
            (back_far, back_own),
            (proj_far, proj_own),
            (conv_far, conv_own),
            hop,
            terms[3],
            normed_pair,
            d_mix,
            d_hidden,
            (gated_far, gated_own),
            (rim_far, rim_own),
            tokens.reshape(row_count, model_width),
            scale_one,
            gain_one[None],
            gain_two_part,
            taps_low,
            span_len,
        )
        block_out = (live_mask * wide(hidden_one, hop, terms[0])).astype(bf16)
        up_grad = wide(up_own, *up_from)
        return (
            block_out.reshape(tokens.shape),
            token_grad.reshape(tokens.shape),
            gain_grads[0],
            mixer_sum[:, : 3 * local_width].reshape(in_weight.shape),
            taps_grad[:TAPS],
            mixer_sum[:, 3 * local_width :].T,
            gain_grads[1],
            gate_grad,
            up_grad,
            down_grad.T,
        )
    d_normed_two = ring_collect([term.astype(f32) for term in back_terms], "fsdp")
    inner, d_gates, d_ups = saved
    sens_rows = jnp.concatenate(sens_all, 0)
    normed_rows = jnp.concatenate(normed_two, 0)
    down_grad = to_owners(contract_rows(sens_rows, inner).astype(bf16))
    gate_grad = to_owners(contract_rows(normed_rows, d_gates).astype(bf16))
    up_grad = to_owners(contract_rows(normed_rows, d_ups).astype(bf16))
    gain_two_part = jnp.sum(d_normed_two * hidden_one * scale_two, axis=0)
    d_hidden = (
        sens_own
        + scale_two * gain_two * d_normed_two
        - hidden_one
        * scale_two**3
        * jnp.mean(hidden_one * gain_two * d_normed_two, axis=-1, keepdims=True)
    )
    d_hidden_low = d_hidden.astype(bf16)
    d_mix = jnp.concatenate([d_hidden_low, swapped(d_hidden_low, "fsdp", 1)], 0)

    tap_parts, sums = [], []
    d_normed = jnp.zeros((pair_rows, model_width), f32)
    for in_full, out_back, taps_f, b_part, c_part, x_part, padded, convolved, gated in kept[::-1]:
        d_gated = times(d_mix, out_back)
        d_c_part = d_gated * convolved
        d_conv = (d_gated * c_part).reshape(pair_lines, span_len, local_width)
        d_padded = jnp.zeros_like(padded)
        tap_rows = []
        for tap in range(TAPS):
            weighted = d_conv * valid_taps[tap]
            d_padded = d_padded + jnp.pad(
                taps_f[tap][None, None, :] * weighted,
                ((0, 0), (TAPS - 1 - tap, tap), (0, 0)),
            )
            tap_rows.append(
                jnp.sum(weighted * padded[:, TAPS - 1 - tap : TAPS - 1 - tap + span_len], axis=(0, 1))
            )
        tap_parts.append(jnp.stack(tap_rows, 0))
        rim_back = passed_along(d_padded[:, : TAPS - 1], "dp", -1)
        d_mixed = (
            d_padded[:, TAPS - 1 :]
            + jnp.pad(rim_back, ((0, 0), (span_len - (TAPS - 1), 0), (0, 0)))
        ).reshape(pair_rows, local_width)
        d_proj = jnp.concatenate([d_mixed * x_part, d_c_part, d_mixed * b_part], axis=1).astype(bf16)
        d_normed = d_normed + times_transposed(d_proj, in_full)
        parts = weight_grad([([normed_pair], d_proj), ([d_mix], gated)], piece)
        d_mix, d_normed, *parts = lax.optimization_barrier((d_mix, d_normed, *parts))
        sums.append(CubeSum(parts))
    moved = swapped(d_normed[row_count:].astype(bf16), "fsdp", 1)
    for step in sums[:-1]:
        (moved,) = step.diagonal(moved)
    for step in sums[:-1]:
        (moved,) = step.sides(moved)
    (moved,) = sums[-1].diagonal(moved)
    (moved,) = sums[-1].sides(moved)
    d_normed_one = d_normed[:row_count] + moved.astype(f32)
    gain_one_part = jnp.sum(d_normed_one * inputs_f * scale_one, axis=0)
    token_grad = (
        d_hidden
        + scale_one * gain_one * d_normed_one
        - inputs_f
        * scale_one**3
        * jnp.mean(inputs_f * gain_one * d_normed_one, axis=-1, keepdims=True)
    ).astype(bf16)

    mixer_sum = sums[-1].total()
    for c, step in list(zip(slices[::-1], sums))[:-1]:
        mixer_sum = mixer_sum + swapped(step.total().astype(bf16), "fsdp", c).astype(f32)
    in_grad = mixer_sum[:, : 3 * local_width].reshape(in_weight.shape)
    out_grad = mixer_sum[:, 3 * local_width :].T

    ffn_out = ring_collect([term.astype(f32) for term in terms], "fsdp")
    block_out = (live_mask * (hidden_one + ffn_out)).astype(bf16)

    taps_sum = tap_parts[-1]
    for c, part in list(zip(slices[::-1], tap_parts))[:-1]:
        taps_sum = taps_sum + swapped(part, "fsdp", c)
    taps_grad = total_all(taps_sum, "dp")
    gain_grads = total_blocks(
        jnp.concatenate(
            [gain_one_part.reshape(-1, piece), gain_two_part.reshape(-1, piece)], 1
        ),
        "dp",
    )
    gain_grads = total_all(gain_grads, "fsdp").reshape(2, piece)
    return (
        block_out.reshape(tokens.shape),
        token_grad.reshape(tokens.shape),
        gain_grads[0],
        in_grad,
        taps_grad,
        out_grad,
        gain_grads[1],
        gate_grad,
        up_grad,
        down_grad.T,
    )


def solution(mesh):
    rows = P(None, "fsdp", "dp", None)
    return jax.shard_map(
        shards,
        mesh=mesh,
        in_specs=(
            rows,
            rows,
            P(None, "fsdp", None),
            P("dp"),
            P("dp", None, "fsdp"),
            P(None, "fsdp"),
            P("fsdp", "dp"),
            P("dp"),
            P("dp", "fsdp"),
            P("dp", "fsdp"),
            P("fsdp", "dp"),
        ),
        out_specs=(
            rows,
            rows,
            P("dp"),
            P("dp", None, "fsdp"),
            P(None, "fsdp"),
            P("fsdp", "dp"),
            P("dp"),
            P("dp", "fsdp"),
            P("dp", "fsdp"),
            P("fsdp", "dp"),
        ),
        check_vma=False,
    )
```

```python
import functools

import jax
import jax.numpy as jnp
from jax import lax
from jax.experimental import pallas as pl
from jax.experimental.pallas import tpu as pltpu
from jax.sharding import PartitionSpec as P

SEQ_LEN = 1024
TAPS = 3

norm_eps = 1e-05
f32 = jnp.float32
bf16 = jnp.bfloat16


def passed_along(value, axis, steps):
    count = lax.axis_size(axis)
    first, last = (max(0, -steps), min(count, count - steps))
    return lax.ppermute(value, axis, [(source, source + steps) for source in range(first, last)])


def passed_round(value, axis):
    count = lax.axis_size(axis)
    return lax.ppermute(value, axis, [(source, (source + 1) % count) for source in range(count)])


def ring_gather(value, axis):
    chunks = [value]
    for _ in range(lax.axis_size(axis) - 1):
        chunks.append(passed_round(chunks[-1], axis))
    return chunks


def ring_collect(terms, axis):
    count = lax.axis_size(axis)
    total = terms[1 % count]
    for step in range(1, count):
        moved = passed_round(total.astype(bf16), axis)
        total = wide(moved, terms[(step + 1) % count])
    return total


def rms_scale(values):
    return lax.rsqrt(jnp.mean(values * values, axis=-1, keepdims=True) + norm_eps)


def times(left, right):
    return jnp.dot(left, right, preferred_element_type=f32)


def times_transposed(left, right):
    return lax.dot_general(left, right, (((1,), (1,)), ((), ())), preferred_element_type=f32)


def contract_rows(left, right):
    return lax.dot_general(left, right, (((0,), (0,)), ((), ())), preferred_element_type=f32)


def ffn_tile(a_ref, e_ref, gate_ref, up_ref, down_ref, m_ref, dg_ref, du_ref, out_ref, da_ref):
    rows, sens = a_ref[...], e_ref[...]
    gate_pre = times(rows, gate_ref[...])
    up_pre = times(rows, up_ref[...])
    d_inner = times(sens, down_ref[...])
    sigmoid_gate = 1.0 / (1.0 + jnp.exp(-gate_pre))
    silu_gate = gate_pre * sigmoid_gate
    inner = (silu_gate * up_pre).astype(bf16)
    d_gate = (d_inner * up_pre * (sigmoid_gate * (1.0 + gate_pre * (1.0 - sigmoid_gate)))).astype(bf16)
    d_up = (d_inner * silu_gate).astype(bf16)
    m_ref[...] = inner
    dg_ref[...] = d_gate
    du_ref[...] = d_up
    out_ref[...] += times_transposed(inner, down_ref[...])
    da_ref[...] += times_transposed(d_gate, gate_ref[...]) + times_transposed(d_up, up_ref[...])


def ffn_kernel(a_ref, e_ref, gate_ref, up_ref, down_ref, *refs):
    m_ref, dg_ref, du_ref, term_ref, back_ref, out_ref, da_ref = refs[-7:]

    @pl.when(pl.program_id(0) == 0)
    def _():
        out_ref[...] = jnp.zeros_like(out_ref)
        da_ref[...] = jnp.zeros_like(da_ref)

    ffn_tile(a_ref, e_ref, gate_ref, up_ref, down_ref, m_ref, dg_ref, du_ref, out_ref, da_ref)

    @pl.when(pl.program_id(0) == pl.num_programs(0) - 1)
    def _():
        term_ref[...] = out_ref[...].astype(bf16)
        back_ref[...] = da_ref[...].astype(bf16)


def ffn_pair_kernel(a0, a1, e0, e1, gate_ref, up_ref, down_ref, *refs):
    m_ref, dg_ref, du_ref, term0, term1, back0, back1, a_ref, e_ref, out_ref, da_ref = refs[-11:]
    rows = a0.shape[0]

    @pl.when(pl.program_id(0) == 0)
    def _():
        a_ref[:rows] = a0[...]
        a_ref[rows:] = a1[...]
        e_ref[:rows] = e0[...]
        e_ref[rows:] = e1[...]
        out_ref[...] = jnp.zeros_like(out_ref)
        da_ref[...] = jnp.zeros_like(da_ref)

    ffn_tile(a_ref, e_ref, gate_ref, up_ref, down_ref, m_ref, dg_ref, du_ref, out_ref, da_ref)

    @pl.when(pl.program_id(0) == pl.num_programs(0) - 1)
    def _():
        term0[...] = out_ref[:rows].astype(bf16)
        term1[...] = out_ref[rows:].astype(bf16)
        back0[...] = da_ref[:rows].astype(bf16)
        back1[...] = da_ref[rows:].astype(bf16)


def ffn_pair(normed, sens, gate_full, up_full, down_back, saved, step, steps, tile=256):
    rows, width = normed[0].shape
    hidden = gate_full.shape[1]
    whole = pl.BlockSpec((rows, width), lambda i: (0, 0))
    weight = pl.BlockSpec((width, tile), lambda i: (0, i))
    part = pl.BlockSpec((2 * rows, tile), lambda i: (step, i))
    act = jax.ShapeDtypeStruct((2 * steps * rows, hidden), bf16)
    total = jax.ShapeDtypeStruct((rows, width), bf16)
    return pl.pallas_call(
        ffn_pair_kernel,
        grid=(hidden // tile,),
        in_specs=[whole] * 4
        + [weight] * 3
        + [pl.BlockSpec(memory_space=pl.ANY)] * len(saved),
        out_specs=[part] * 3 + [whole] * 4,
        out_shape=[act] * 3 + [total] * 4,
        scratch_shapes=[pltpu.VMEM((2 * rows, width), bf16)] * 2 + [pltpu.VMEM((2 * rows, width), f32)] * 2,
        input_output_aliases={7 + i: i for i in range(len(saved))},
        compiler_params=pltpu.CompilerParams(vmem_limit_bytes=60 * 2**20),
        cost_estimate=pl.CostEstimate(
            flops=24 * rows * width * hidden,
            bytes_accessed=6 * width * hidden + 24 * rows * width + 12 * rows * hidden,
            transcendentals=2 * rows * hidden,
        ),
    )(*normed, *sens, gate_full, up_full, down_back, *saved)


def ffn_chunk(normed, sens, gate_full, up_full, down_back, saved, step, steps, tile=512):
    rows, width = normed.shape
    hidden = gate_full.shape[1]
    whole = pl.BlockSpec((rows, width), lambda i: (0, 0))
    weight = pl.BlockSpec((width, tile), lambda i: (0, i))
    part = pl.BlockSpec((rows, tile), lambda i: (step, i))
    act = jax.ShapeDtypeStruct((steps * rows, hidden), bf16)
    total = jax.ShapeDtypeStruct((rows, width), bf16)
    return pl.pallas_call(
        ffn_kernel,
        grid=(hidden // tile,),
        in_specs=[whole, whole, weight, weight, weight]
        + [pl.BlockSpec(memory_space=pl.ANY)] * len(saved),
        out_specs=[part, part, part, whole, whole],
        out_shape=[act, act, act, total, total],
        scratch_shapes=[pltpu.VMEM((rows, width), f32)] * 2,
        input_output_aliases={5 + i: i for i in range(len(saved))},
        compiler_params=pltpu.CompilerParams(vmem_limit_bytes=48 * 2**20),
        cost_estimate=pl.CostEstimate(
            flops=12 * rows * width * hidden,
            bytes_accessed=6 * width * hidden + 12 * rows * width + 6 * rows * hidden,
            transcendentals=rows * hidden,
        ),
    )(normed, sens, gate_full, up_full, down_back, *saved)


def swapped(value, axis, offset):
    count = lax.axis_size(axis)
    return lax.ppermute(value, axis, [(source, source ^ offset) for source in range(count)])


CORE, XLINK, YLINK = 1, 2, 4


def gather_cube(shard, widths, after):
    if after:
        shard = lax.optimization_barrier((shard, *after))[0]
    if lax.axis_size("dp") != 8:
        full = lax.all_gather(shard, "dp", axis=0, tiled=True)
        ends = [sum(widths[: i + 1]) for i in range(len(widths))]
        return [full[:, end - width : end] for end, width in zip(ends, widths)], ()
    rows = shard.shape[0]
    half = rows // 2
    over_x = swapped(shard, "dp", XLINK)
    over_y = swapped(shard, "dp", YLINK)
    diag_top = swapped(over_x[:half], "dp", YLINK)
    diag_low = swapped(over_y[half:], "dp", XLINK)
    pieces = [
        (shard, 0, 0),
        (over_x, XLINK, 0),
        (over_y, YLINK, 0),
        (diag_top, XLINK | YLINK, 0),
        (diag_low, XLINK | YLINK, half),
    ]
    pieces += [(swapped(v, "dp", CORE), offset ^ CORE, at) for v, offset, at in pieces]

    count = len(pieces)

    def kernel(*refs):
        ins, outs = refs[:count], refs[count : count + len(widths)]
        held, in_sems, out_sems = refs[count + len(widths) :]
        me = lax.axis_index("dp")
        copies = []
        for i, (value, offset, at) in enumerate(pieces):
            start = pl.multiple_of(lax.bitwise_xor(me, offset) * rows + at, half)
            copies.append(
                pltpu.make_async_copy(
                    ins[i], held.at[pl.ds(start, value.shape[0]), :], in_sems.at[i]
                )
            )
        for copy in copies:
            copy.start()
        for copy in copies:
            copy.wait()
        copies, first = [], 0
        for j, width in enumerate(widths):
            copies.append(
                pltpu.make_async_copy(held.at[:, pl.ds(first, width)], outs[j], out_sems.at[j])
            )
            first += width
        for copy in copies:
            copy.start()
        for copy in copies:
            copy.wait()

    spec = pl.BlockSpec(memory_space=pl.ANY)
    full = pl.pallas_call(
        kernel,
        in_specs=[spec] * count,
        out_specs=[spec] * len(widths),
        out_shape=[jax.ShapeDtypeStruct((8 * rows, width), shard.dtype) for width in widths],
        scratch_shapes=[
            pltpu.VMEM((8 * rows, sum(widths)), shard.dtype),
            pltpu.SemaphoreType.DMA((count,)),
            pltpu.SemaphoreType.DMA((len(widths),)),
        ],
        cost_estimate=pl.CostEstimate(
            flops=0, bytes_accessed=32 * rows * sum(widths), transcendentals=0
        ),
    )(*[value for value, _, _ in pieces])
    return full, (over_x, over_y)


def pick(value, axis, index):
    return lax.dynamic_index_in_dim(value, index, axis, keepdims=False)


def grad_kernel(pairs, chunks, order_ref, *refs):
    keep_ref, send_ref = refs[-2:]
    for out_ref, at in ((keep_ref, 0), (send_ref, 1)):
        first = 0
        for pair in range(pairs):
            base = pair * (2 * chunks + 1)
            left = [refs[base + at * chunks + i][...] for i in range(chunks)]
            left = left[0] if chunks == 1 else jnp.concatenate(left, 0)
            right = refs[base + 2 * chunks]
            width = right.shape[1]
            out_ref[0, :, first : first + width] = contract_rows(left, right[...]).astype(bf16)
            first += width


def weight_grad(pairs, piece):
    chunks = len(pairs[0][0])
    width = sum(right.shape[1] for _, right in pairs)
    rows = pairs[0][1].shape[0]
    if lax.axis_size("dp") != 8:
        return (
            jnp.concatenate(
                [contract_rows(jnp.concatenate(left, 0), right).astype(bf16) for left, right in pairs], 1
            ),
        )
    me = lax.axis_index("dp")
    order = jnp.stack([me % 2, me // 2]).astype(jnp.int32)
    out = pl.BlockSpec((1, piece, width), lambda i, o: (i, 0, 0))
    chip = jax.ShapeDtypeStruct((4, piece, width), bf16)
    specs, values = [], []
    for left, right in pairs:
        lead = (left[0].shape[0], piece)
        specs += [pl.BlockSpec(lead, lambda i, o: (0, 2 * (i ^ o[1]) + o[0]))] * chunks
        specs += [pl.BlockSpec(lead, lambda i, o: (0, 2 * (i ^ o[1]) + 1 - o[0]))] * chunks
        specs += [pl.BlockSpec(right.shape, lambda i, o: (0, 0))]
        values += list(left) + list(left) + [right]
    return pl.pallas_call(
        functools.partial(grad_kernel, len(pairs), chunks),
        grid_spec=pltpu.PrefetchScalarGridSpec(
            num_scalar_prefetch=1, grid=(4,), in_specs=specs, out_specs=[out, out]
        ),
        out_shape=[chip, chip],
        compiler_params=pltpu.CompilerParams(vmem_limit_bytes=48 * 2**20),
        cost_estimate=pl.CostEstimate(
            flops=16 * rows * piece * width,
            bytes_accessed=16 * piece * width + 16 * rows * piece + 2 * rows * width,
            transcendentals=0,
        ),
    )(order, *values)


def wide(*values):
    total = values[0].astype(f32)
    for value in values[1:]:
        total = total + value.astype(f32)
    return total


class CubeSum:
    def __init__(self, parts):
        if len(parts) == 1:
            self.whole = lax.psum_scatter(parts[0], "dp", scatter_dimension=0, tiled=True).astype(f32)
            return
        self.whole = None
        self.keep = parts[0]
        self.moved = swapped(parts[1], "dp", CORE)

    def diagonal(self, *after):
        if self.whole is not None:
            return after
        half = self.keep.shape[1] // 2
        diag, *after = lax.optimization_barrier(
            (wide(self.keep[3], self.moved[3]).astype(bf16), *after)
        )
        self.top = swapped(diag[:half], "dp", XLINK)
        self.low = swapped(diag[half:], "dp", YLINK)
        return after

    def sides(self, *after):
        if self.whole is not None:
            return after
        half = self.keep.shape[1] // 2
        over_x = jnp.concatenate(
            [
                wide(self.keep[1, :half], self.moved[1, :half]).astype(bf16),
                wide(self.keep[1, half:], self.moved[1, half:], self.low).astype(bf16),
            ],
            0,
        )
        over_y = jnp.concatenate(
            [
                wide(self.keep[2, :half], self.moved[2, :half], self.top).astype(bf16),
                wide(self.keep[2, half:], self.moved[2, half:]).astype(bf16),
            ],
            0,
        )
        over_x, over_y, *after = lax.optimization_barrier((over_x, over_y, *after))
        self.from_x = swapped(over_x, "dp", XLINK)
        self.from_y = swapped(over_y, "dp", YLINK)
        return after

    def total(self):
        if self.whole is not None:
            return self.whole
        return wide(self.keep[0], self.moved[0], self.from_x, self.from_y)


MESH = pl.DeviceIdType.MESH
ROWS = 16


class Wires:
    def __init__(self, sends, recvs):
        self.sends, self.recvs, self.used = sends, recvs, 0

    def to(self, source, target, **device):
        copy = pltpu.make_async_remote_copy(
            src_ref=source,
            dst_ref=target,
            send_sem=self.sends.at[self.used],
            recv_sem=self.recvs.at[self.used],
            device_id=device,
            device_id_type=MESH,
        )
        self.used += 1
        copy.start()
        return copy


def greet(my_dp, my_line):
    barrier = pltpu.get_barrier_semaphore()
    for offset in range(1, 8):
        pl.semaphore_signal(
            barrier, inc=1, device_id={"dp": lax.bitwise_xor(my_dp, offset)}, device_id_type=MESH
        )
    for offset in range(1, 4):
        pl.semaphore_signal(
            barrier, inc=1, device_id={"fsdp": lax.bitwise_xor(my_line, offset)}, device_id_type=MESH
        )
    pl.semaphore_wait(barrier, 10)


def by_rows(count, body):
    def step(i, carry):
        body(pl.ds(pl.multiple_of(i * ROWS, ROWS), ROWS))
        return carry

    lax.fori_loop(0, count // ROWS, step, 0)


class CubeWires:
    def __init__(self, my_dp, product, stage, moved, top, low, from_x, from_y, own, sends, recvs):
        self.product, self.stage, self.moved, self.own = product, stage, moved, own
        self.top, self.low, self.from_x, self.from_y = top, low, from_x, from_y
        self.sends, self.recvs = sends, recvs
        self.my_core = lax.rem(my_dp, 2)
        self.core = {"dp": lax.bitwise_xor(my_dp, CORE)}
        self.x = {"dp": lax.bitwise_xor(my_dp, XLINK)}
        self.y = {"dp": lax.bitwise_xor(my_dp, YLINK)}
        self.rows = moved.shape[1]
        self.half = moved.shape[1] // 2

    def copy(self, i, source, target, device):
        return pltpu.make_async_remote_copy(
            src_ref=source,
            dst_ref=target,
            send_sem=self.sends.at[i],
            recv_sem=self.recvs.at[i],
            device_id=device,
            device_id_type=MESH,
        )

    def swap(self, block):
        return self.copy(block, self.stage.at[block], self.moved.at[block], self.core)

    def corner(self, i):
        if i == 0:
            return self.copy(4, self.moved.at[3, pl.ds(0, self.half)], self.top, self.x)
        return self.copy(5, self.moved.at[3, pl.ds(self.half, self.half)], self.low, self.y)

    def side(self, block, part):
        at = pl.ds(part * self.half, self.half)
        target, device = ((self.from_x, self.x), (self.from_y, self.y))[block - 1]
        return self.copy(4 + 2 * block + part, self.moved.at[block, at], target.at[at], device)

    def give(self):
        def step(i, carry):
            block = jnp.where((i == 0) | (i == 3), 3 - i, i)
            self.stage[block] = self.product(block, 1 - self.my_core)
            self.swap(block).start()
            return carry

        lax.fori_loop(0, 4, step, 0)

    def keep(self):
        def step(i, carry):
            block = jnp.where((i == 0) | (i == 3), 3 - i, i)
            self.swap(block).wait_recv()
            value = wide(self.product(block, self.my_core), self.moved[block])
            self.moved[block] = value.astype(bf16)

            @pl.when(i == 0)
            def _():
                self.corner(0).start()
                self.corner(1).start()

            @pl.when(i == 1)
            def _():
                self.side(1, 0).start()

            @pl.when(i == 2)
            def _():
                self.side(2, 1).start()

            if self.own is not None:

                @pl.when(i == 3)
                def _():
                    self.own[...] = value

            return carry

        lax.fori_loop(0, 4, step, 0)

    def others(self):
        self.corner(0).wait_recv()

        def add_top(at):
            self.moved[2, at] = wide(self.moved[2, at], self.top[at]).astype(bf16)

        by_rows(self.half, add_top)
        self.side(2, 0).start()
        self.corner(1).wait_recv()

        def add_low(at):
            below = pl.ds(pl.multiple_of(at.start + self.half, ROWS), ROWS)
            self.moved[1, below] = wide(self.moved[1, below], self.low[at]).astype(bf16)

        by_rows(self.half, add_low)
        self.side(1, 1).start()

    def total(self, store):
        for block in (1, 2):
            for part in range(2):
                self.side(block, part).wait_recv()

        own = self.moved.at[0] if self.own is None else self.own

        def add(at):
            store(at, wide(own[at], self.from_x[at], self.from_y[at]))

        by_rows(self.rows, add)

    def close_stage(self):
        for block in range(4):
            self.swap(block).wait_send()

    def close(self):
        for i in range(2):
            self.corner(i).wait_send()
        for block in (1, 2):
            for part in range(2):
                self.side(block, part).wait_send()


class Spread:
    def __init__(self, wires, my_dp, shard, full, own_sem, base=0):
        self.wires, self.my_dp, self.shard, self.full, self.own_sem = wires, my_dp, shard, full, own_sem
        self.rows, self.base = shard.shape[0], base
        self.core = {"dp": lax.bitwise_xor(my_dp, CORE)}
        self.x = {"dp": lax.bitwise_xor(my_dp, XLINK)}
        self.y = {"dp": lax.bitwise_xor(my_dp, YLINK)}

    def block(self, offset, first=0, count=None):
        half = self.rows // 2
        start = lax.bitwise_xor(self.my_dp, offset) * (self.full.shape[0] // 8) + self.base + first
        return self.full.at[pl.ds(pl.multiple_of(start, half), count or self.rows)]

    def start(self):
        own = self.block(0)
        self.own = pltpu.make_async_copy(self.shard, own, self.own_sem)
        self.own.start()
        self.over_x = self.wires.to(self.shard, own, **self.x)
        self.over_y = self.wires.to(self.shard, own, **self.y)
        self.cores = [self.wires.to(self.shard, own, **self.core)]

    def pass_on(self, block, **device):
        return self.wires.to(block, block, **device)

    def relay(self):
        half = self.rows // 2
        self.over_x.wait_recv()
        self.top = self.pass_on(self.block(XLINK, 0, half), **self.y)
        self.over_y.wait_recv()
        self.low = self.pass_on(self.block(YLINK, half, half), **self.x)
        self.cores += [self.pass_on(self.block(offset), **self.core) for offset in (XLINK, YLINK)]

    def finish(self):
        half = self.rows // 2
        for move, first in ((self.top, 0), (self.low, half)):
            move.wait_recv()
            self.cores.append(self.pass_on(self.block(XLINK | YLINK, first, half), **self.core))

    def complete(self):
        self.own.wait()
        for move in self.cores:
            move.wait_recv()

    def close(self):
        for move in (self.over_x, self.over_y, self.top, self.low, *self.cores):
            move.wait_send()


def head_kernel(
    span, mixer, gate, up, down, sens, inputs, gains, taps,
    in_own, in_far, back_own, back_far, gate_full, up_full, down_full, sens1, sens2, sens3,
    normed, proj_own, proj_far, conv_own, conv_far, gated_own, gated_far, rim_own, rim_far,
    hidden, normed_two, normed_next, normed_later, scale_one, scale_two, gain_one, gain_two,
    full_own, full_far, mixer_far, taps_far, total, lines_own, lines_far, mix_out, mix_in, gains_in,
    own_sems, out_sems, sends, recvs,
):
    my_dp, my_line = lax.axis_index("dp"), lax.axis_index("fsdp")
    right = {"fsdp": lax.rem(my_line + 1, 4)}
    pair = {"fsdp": lax.bitwise_xor(my_line, 1)}
    far = {"fsdp": lax.bitwise_xor(my_line, 2)}
    wires = Wires(sends, recvs)
    rows, width = inputs.shape
    piece = gains.shape[1]
    local = taps.shape[1]
    line_count = 2 * rows // span
    greet(my_dp, my_line)

    gain_moves = [
        wires.to(gains, gains_in.at[my_dp], dp=lax.bitwise_xor(my_dp, offset)) for offset in range(1, 8)
    ]
    taps_move = wires.to(taps, taps_far, **far)
    half = piece // 2
    halves = [pl.ds(0, half), pl.ds(half, half)]
    spreads = [
        Spread(wires, my_dp, shard, full, own_sems.at[i], base)
        for i, (shard, full, base) in enumerate(
            (
                (mixer, full_own, 0),
                (mixer_far.at[halves[0]], full_far, 0),
                (mixer_far.at[halves[1]], full_far, half),
                (gate, gate_full, 0),
                (up, up_full, 0),
                (down, down_full, 0),
            )
        )
    ]
    one, two_a, two_b, gates, ups, downs = spreads
    one.start()
    mixer_moves = [wires.to(mixer.at[at], mixer_far.at[at], **far) for at in halves]
    gains_in[my_dp] = gains[...]
    for move in gain_moves:
        move.wait_recv()
    for block in range(8):
        gain_one[:, block * piece : (block + 1) * piece] = gains_in[block, 0:1]
        gain_two[:, block * piece : (block + 1) * piece] = gains_in[block, 1:2]
    gain_row, gain_next = gain_one[...], gain_two[...]

    def first_norm(at):
        values = inputs[at].astype(f32)
        r = lax.rsqrt(jnp.mean(values * values, axis=-1, keepdims=True) + norm_eps)
        scale_one[at] = r
        normed[at] = (values * r * gain_row).astype(bf16)

    by_rows(rows, first_norm)
    normed_move = wires.to(normed.at[pl.ds(0, rows)], normed.at[pl.ds(rows, rows)], **pair)

    def mix(full, proj, conv, gated, rim, lines, taps_ref, first):
        def project(j, carry):
            columns = pl.ds(pl.multiple_of(j * local, local), local)
            proj[:, columns] = times(normed[...], full[:, columns])
            return carry

        lax.fori_loop(0, 3, project, 0)

        @pl.when(my_dp == 0)
        def _():
            lines[:, 0:8] = jnp.zeros((line_count, 8, local), f32)

        def gate_in(i, carry):
            at = pl.ds(pl.multiple_of(i * span, span), span)
            lines[i, 8 : 8 + span] = proj[at, 0:local] * proj[at, 2 * local : 3 * local]
            return carry

        lax.fori_loop(0, line_count, gate_in, 0)
        rim_move = pltpu.make_async_remote_copy(
            src_ref=lines.at[:, pl.ds(span, 8)],
            dst_ref=lines.at[:, pl.ds(0, 8)],
            send_sem=sends.at[wires.used],
            recv_sem=recvs.at[wires.used],
            device_id={"dp": jnp.minimum(my_dp + 1, 7)},
            device_id_type=MESH,
        )
        wires.used += 1

        @pl.when(my_dp < 7)
        def _():
            rim_move.start()

        @pl.when(my_dp > 0)
        def _():
            rim_move.wait_recv()

        rim[...] = lines[:, 0:8]
        tap_rows = [taps_ref[tap : tap + 1] for tap in range(TAPS)]

        def convolve(i, carry):
            for base in range(0, span, ROWS):
                at = pl.ds(pl.multiple_of(i * span + base, ROWS), ROWS)
                spot = my_dp * span + base + lax.broadcasted_iota(jnp.int32, (ROWS, 1), 0)
                position = lax.rem(spot, SEQ_LEN)
                value = tap_rows[0] * lines[i, 8 + base : 8 + base + ROWS]
                for tap in range(1, TAPS):
                    before = tap_rows[tap] * lines[i, 8 + base - tap : 8 + base - tap + ROWS]
                    value = value + jnp.where(position >= tap, before, 0.0)
                conv[at] = value
                gated[at] = (proj[at, local : 2 * local] * value).astype(bf16)
            return carry

        lax.fori_loop(0, line_count, convolve, 0)

        def back(j, carry):
            columns = pl.ds(pl.multiple_of(j * local, local), local)
            value = times_transposed(gated[...], full[columns, 3 * local : 4 * local])
            total[:, columns] = value if first else total[:, columns] + value
            return carry

        lax.fori_loop(0, width // local, back, 0)
        return rim_move

    def write_out(full, in_ref, back_ref, i):
        copies = [
            pltpu.make_async_copy(full.at[:, pl.ds(0, 3 * local)], in_ref, out_sems.at[2 * i]),
            pltpu.make_async_copy(full.at[:, pl.ds(3 * local, local)], back_ref, out_sems.at[2 * i + 1]),
        ]
        for copy in copies:
            copy.start()
        return copies

    one.relay()
    taps_move.wait_recv()
    mixer_moves[0].wait_recv()
    two_a.start()
    one.finish()
    one.complete()
    mixer_moves[1].wait_recv()
    two_b.start()
    sens_moves = [wires.to(sens, sens1, **right)]
    two_a.relay()
    normed_move.wait_recv()
    rims = [mix(full_own, proj_own, conv_own, gated_own, rim_own, lines_own, taps, True)]
    outs = write_out(full_own, in_own, back_own, 0)
    two_b.relay()
    gates.start()
    two_a.finish()
    two_b.finish()
    sens_moves[0].wait_recv()
    sens_moves.append(wires.to(sens1, sens2, **right))
    two_a.complete()
    two_b.complete()
    rims.append(mix(full_far, proj_far, conv_far, gated_far, rim_far, lines_far, taps_far, False))

    def shorten(at):
        mix_out[at] = total[pl.ds(pl.multiple_of(at.start + rows, ROWS), ROWS)].astype(bf16)

    by_rows(rows, shorten)
    mix_move = wires.to(mix_out, mix_in, **pair)
    outs += write_out(full_far, in_far, back_far, 1)
    gates.relay()
    ups.start()
    gates.finish()
    mix_move.wait_recv()

    def second_norm(at):
        values = wide(inputs[at], total[at], mix_in[at])
        hidden[at] = values
        r = lax.rsqrt(jnp.mean(values * values, axis=-1, keepdims=True) + norm_eps)
        scale_two[at] = r
        normed_two[at] = (values * r * gain_next).astype(bf16)

    by_rows(rows, second_norm)
    next_moves = [wires.to(normed_two, normed_next, **right)]
    sens_moves[1].wait_recv()
    sens_moves.append(wires.to(sens2, sens3, **right))
    ups.relay()
    downs.start()
    ups.finish()
    next_moves[0].wait_recv()
    next_moves.append(wires.to(normed_next, normed_later, **right))
    downs.relay()
    downs.finish()
    sens_moves[2].wait_recv()
    for spread in (gates, ups, downs):
        spread.complete()
    next_moves[1].wait_recv()
    for copy in outs:
        copy.wait()
    for spread in spreads:
        spread.close()

    @pl.when(my_dp < 7)
    def _():
        for move in rims:
            move.wait_send()

    for move in (taps_move, *mixer_moves, normed_move, mix_move, *next_moves, *gain_moves, *sens_moves):
        move.wait_send()


def head_call(mixer, gate, up, down, sens, inputs, gains, taps, span):
    rows, width = inputs.shape
    piece = mixer.shape[0]
    local = taps.shape[1]
    hidden = gate.shape[1]
    lines = 2 * rows // span
    vmem = pl.BlockSpec(memory_space=pltpu.VMEM)
    anywhere = pl.BlockSpec(memory_space=pl.ANY)
    low = lambda *shape: pltpu.VMEM(shape, bf16)
    full = lambda *shape: pltpu.VMEM(shape, f32)
    out = lambda kind, *shape: jax.ShapeDtypeStruct(shape, kind)
    copies = 96
    return pl.pallas_call(
        functools.partial(head_kernel, span),
        in_specs=[anywhere] * 5 + [vmem] * 3,
        out_specs=[anywhere] * 10 + [vmem] * 17,
        out_shape=[
            out(bf16, width, 3 * local),
            out(bf16, width, 3 * local),
            out(bf16, width, local),
            out(bf16, width, local),
            out(bf16, width, hidden),
            out(bf16, width, hidden),
            out(bf16, width, hidden),
            out(bf16, rows, width),
            out(bf16, rows, width),
            out(bf16, rows, width),
            out(bf16, 2 * rows, width),
            out(f32, 2 * rows, 3 * local),
            out(f32, 2 * rows, 3 * local),
            out(f32, 2 * rows, local),
            out(f32, 2 * rows, local),
            out(bf16, 2 * rows, local),
            out(bf16, 2 * rows, local),
            out(f32, lines, 8, local),
            out(f32, lines, 8, local),
            out(f32, rows, width),
            out(bf16, rows, width),
            out(bf16, rows, width),
            out(bf16, rows, width),
            out(f32, rows, 1),
            out(f32, rows, 1),
            out(f32, 1, width),
            out(f32, 1, width),
        ],
        scratch_shapes=[
            low(width, 4 * local),
            low(width, 4 * local),
            low(piece, 4 * local),
            full(*taps.shape),
            full(2 * rows, width),
            full(lines, 8 + span, local),
            full(lines, 8 + span, local),
            low(rows, width),
            low(rows, width),
            full(8, 8, piece),
            pltpu.SemaphoreType.DMA((6,)),
            pltpu.SemaphoreType.DMA((4,)),
            pltpu.SemaphoreType.DMA((copies,)),
            pltpu.SemaphoreType.DMA((copies,)),
        ],
        compiler_params=pltpu.CompilerParams(
            collective_id=3, has_side_effects=True, vmem_limit_bytes=60 * 2**20
        ),
        cost_estimate=pl.CostEstimate(
            flops=32 * rows * width * local, bytes_accessed=2 * 10**8, transcendentals=0
        ),
    )(mixer, gate, up, down, sens, inputs, gains, taps)


def rear_kernel(
    span, up_x, up_y, in_far, in_own, back_far, back_own, proj_far, proj_own, conv_far, conv_own, hop_in, term,
    normed, d_mix, d_hidden, gated_far, gated_own, rim_far, rim_own, inputs, scale, gain, gain_two, taps_own,
    mixer_out, token_out, gain_out, taps_out, up_from_x, up_from_y, hop_out,
    in_full, backs, parts, lines_far, lines_own, line, d_far, d_own, stage, moved_far, moved_own,
    tops, lows, from_x, from_y, far_in, total, back_in, hop_mid, hop_term,
    gain_cut, gain_in, gain_line, gain_lines, taps_given, taps_got, taps_part, taps_pair, taps_sum, taps_in,
    loads, cube_sends, cube_recvs, sends, recvs,
):
    my_dp, my_line = lax.axis_index("dp"), lax.axis_index("fsdp")
    my_chip = my_dp // 2
    pair = {"fsdp": lax.bitwise_xor(my_line, 1)}
    far = {"fsdp": lax.bitwise_xor(my_line, 2)}
    wires = Wires(sends, recvs)
    rows = inputs.shape[0]
    width = inputs.shape[1]
    piece = gain_out.shape[1]
    local = taps_own.shape[1]
    line_count = 2 * rows // span
    loaded = [0]

    def load(source, target):
        copy = pltpu.make_async_copy(source, target, loads.at[loaded[0]])
        loaded[0] += 1
        copy.start()
        return copy

    def column(proj, part):
        return proj.at[:, pl.ds(part * local, local)]

    early_far = [
        load(back_far, backs.at[0]), load(column(proj_far, 1), parts.at[0]), load(conv_far, parts.at[1])
    ]
    early_own = [
        load(back_own, backs.at[1]), load(column(proj_own, 1), parts.at[2]), load(conv_own, parts.at[3])
    ]
    in_load = load(in_far, in_full)
    term_load = load(term, hop_term)
    greet(my_dp, my_line)
    right = {"fsdp": lax.rem(my_line + 1, 4)}
    taps_move = wires.to(taps_own, taps_got, **far)
    hops = [wires.to(hop_in, hop_mid, **right)]

    def open_slice(i, early, lines, d_proj):
        for copy in early:
            copy.wait()

        def spread_rows(j, carry):
            at = pl.ds(pl.multiple_of(j * span, span), span)
            lines[j, 8 : 8 + span] = times(d_mix[at], backs[i])
            return carry

        lax.fori_loop(0, line_count, spread_rows, 0)

        @pl.when(my_dp == 7)
        def _():
            lines[:, 8 + span : 16 + span] = jnp.zeros((line_count, 8, local), f32)

        def share(j, carry):
            for base in range(0, span, ROWS):
                at = pl.ds(pl.multiple_of(j * span + base, ROWS), ROWS)
                d_gated = lines[j, 8 + base : 8 + base + ROWS]
                d_proj[at, local : 2 * local] = (d_gated * parts[2 * i + 1, at]).astype(bf16)
                lines[j, 8 + base : 8 + base + ROWS] = d_gated * parts[2 * i, at]
            return carry

        lax.fori_loop(0, line_count, share, 0)
        move = pltpu.make_async_remote_copy(
            src_ref=lines.at[:, pl.ds(8, 8)],
            dst_ref=lines.at[:, pl.ds(8 + span, 8)],
            send_sem=sends.at[wires.used],
            recv_sem=recvs.at[wires.used],
            device_id={"dp": jnp.maximum(my_dp - 1, 0)},
            device_id_type=MESH,
        )
        wires.used += 1

        @pl.when(my_dp > 0)
        def _():
            move.start()

        return move

    def close_slice(i, late, rim_move, lines, rim, d_proj, taps_ref):
        for copy in late:
            copy.wait()

        @pl.when(my_dp < 7)
        def _():
            rim_move.wait_recv()

        tap_rows = [taps_ref[tap : tap + 1] for tap in range(TAPS)]

        def convolve(j, sums):
            line[0:8] = rim[j]
            for base in range(0, span, ROWS):
                at = pl.ds(pl.multiple_of(j * span + base, ROWS), ROWS)
                line[8 + base : 8 + base + ROWS] = parts[2 * i, at] * parts[2 * i + 1, at]
            sums = list(sums)
            for base in range(0, span, ROWS):
                at = pl.ds(pl.multiple_of(j * span + base, ROWS), ROWS)
                spot = my_dp * span + base + lax.broadcasted_iota(jnp.int32, (ROWS, 1), 0)
                here = lines[j, 8 + base : 8 + base + ROWS]
                value = tap_rows[0] * here
                for tap in range(TAPS):
                    before = line[8 + base - tap : 8 + base - tap + ROWS]
                    valid = lax.rem(spot, SEQ_LEN) >= tap
                    grad = jnp.where(valid, here * before, 0.0)
                    sums[tap] = sums[tap] + jnp.sum(grad.reshape(ROWS // 8, 8, local), axis=0)
                for tap in range(1, TAPS):
                    after = tap_rows[tap] * lines[j, 8 + base + tap : 8 + base + tap + ROWS]
                    valid = lax.rem(spot + tap, SEQ_LEN) >= tap
                    value = value + jnp.where(valid, after, 0.0)
                d_proj[at, 0:local] = (value * parts[2 * i, at]).astype(bf16)
                d_proj[at, 2 * local : 3 * local] = (value * parts[2 * i + 1, at]).astype(bf16)
            return tuple(sums)

        sums = lax.fori_loop(0, line_count, convolve, (jnp.zeros((8, local), f32),) * TAPS)
        for tap in range(TAPS):
            taps_part[i, tap : tap + 1] = jnp.sum(sums[tap], axis=0, keepdims=True)

    def late_loads(i, proj):
        return [load(column(proj, 2), parts.at[2 * i]), load(column(proj, 0), parts.at[2 * i + 1])]

    def weigher(d_proj, gated):
        def product(block, side):
            place = 2 * lax.bitwise_xor(block, my_chip) + side
            columns = pl.ds(pl.multiple_of(place * piece, piece), piece)
            return jnp.concatenate(
                [
                    contract_rows(normed[:, columns], d_proj[...]).astype(bf16),
                    contract_rows(d_mix[:, columns], gated[...]).astype(bf16),
                ],
                1,
            )

        return product

    def back_rows(d_proj, first):
        def step(j, carry):
            columns = pl.ds(pl.multiple_of(j * local, local), local)
            value = times_transposed(d_proj[...], in_full[columns, :])
            total[:, columns] = value if first else total[:, columns] + value
            return carry

        lax.fori_loop(0, width // local, step, 0)

    rims = [open_slice(0, early_far, lines_far, d_far)]
    late_far = late_loads(0, proj_far)
    rims.append(open_slice(1, early_own, lines_own, d_own))
    late_own = late_loads(1, proj_own)
    taps_part[...] = jnp.zeros_like(taps_part)
    taps_move.wait_recv()
    close_slice(0, late_far, rims[0], lines_far, rim_far, d_far, taps_got)
    far_cube = CubeWires(
        my_dp, weigher(d_far, gated_far), stage, moved_far, tops.at[0], lows.at[0],
        from_x.at[0], from_y.at[0], None, cube_sends.at[0], cube_recvs.at[0],
    )
    own_cube = CubeWires(
        my_dp, weigher(d_own, gated_own), stage, moved_own, tops.at[1], lows.at[1],
        from_x.at[1], from_y.at[1], mixer_out, cube_sends.at[1], cube_recvs.at[1],
    )
    far_cube.give()
    far_cube.keep()
    close_slice(1, late_own, rims[1], lines_own, rim_own, d_own, taps_own)
    taps_given[...] = taps_part[0]
    taps_back = wires.to(taps_given, taps_pair, **far)
    in_load.wait()
    back_rows(d_far, True)
    in_load = load(in_own, in_full)
    term_load.wait()
    hops[0].wait_recv()

    def add_hop(at):
        hop_mid[at] = wide(hop_mid[at], hop_term[at]).astype(bf16)

    by_rows(rows, add_hop)
    hops.append(wires.to(hop_mid, hop_out, **right))
    far_cube.others()
    up_moves = [
        wires.to(up_x, up_from_x, dp=lax.bitwise_xor(my_dp, XLINK)),
        wires.to(up_y, up_from_y, dp=lax.bitwise_xor(my_dp, YLINK)),
    ]
    far_cube.close_stage()
    own_cube.give()
    own_cube.keep()
    in_load.wait()
    back_rows(d_own, False)

    own_cube.close_stage()

    def shorten(at):
        stage[0, at] = total[pl.ds(pl.multiple_of(at.start + rows, ROWS), ROWS)].astype(bf16)

    by_rows(rows, shorten)
    back_move = wires.to(stage.at[0], back_in, **pair)
    taps_back.wait_recv()
    taps_sum[...] = taps_part[1] + taps_pair[...]
    taps_moves = [
        wires.to(taps_sum, taps_in.at[my_dp], dp=lax.bitwise_xor(my_dp, offset)) for offset in range(1, 8)
    ]

    def keep_low(at, value):
        stage[1, at] = value.astype(bf16)

    far_cube.total(keep_low)
    far_move = wires.to(stage.at[1], far_in, **far)
    own_cube.others()
    back_move.wait_recv()
    gain_row = gain[...]
    gain_cut[...] = jnp.zeros_like(gain_cut)

    def finish(i, part):
        at = pl.ds(pl.multiple_of(i * ROWS, ROWS), ROWS)
        grad = wide(total[at], back_in[at])
        values = inputs[at].astype(f32)
        r = scale[at]
        along = values * grad
        mean = jnp.mean(along * gain_row, axis=-1, keepdims=True)
        token_out[at] = (d_hidden[at] + r * gain_row * grad - values * (r * r * r) * mean).astype(bf16)
        return part + jnp.sum((along * r).reshape(ROWS // 8, 8, -1), axis=0)

    part = lax.fori_loop(0, rows // ROWS, finish, jnp.zeros((8, width), f32))
    part = jnp.sum(part, axis=0, keepdims=True)
    for block in range(8):
        gain_cut[block, 0:1] = part[:, block * piece : (block + 1) * piece]
        gain_cut[block, 1:2] = gain_two[:, block * piece : (block + 1) * piece]
    gain_moves = []
    for offset in range(1, 8):
        peer = lax.bitwise_xor(my_dp, offset)
        gain_moves.append(wires.to(gain_cut.at[peer], gain_in.at[my_dp], dp=peer))
    gain_in[my_dp] = gain_cut[my_dp]
    for move in gain_moves:
        move.wait_recv()
    gain_line[...] = jnp.sum(gain_in[...], axis=0)
    line_moves = [
        wires.to(gain_line, gain_lines.at[my_line], fsdp=lax.bitwise_xor(my_line, offset))
        for offset in range(1, 4)
    ]
    for move in taps_moves:
        move.wait_recv()
    taps_in[my_dp] = taps_sum[...]
    taps_out[...] = jnp.sum(taps_in[...], axis=0)

    def keep_wide(at, value):
        mixer_out[at] = value

    own_cube.total(keep_wide)
    for move in line_moves:
        move.wait_recv()
    gain_lines[my_line] = gain_line[...]
    gain_out[...] = jnp.sum(gain_lines[...], axis=0)
    far_move.wait_recv()

    def add_far(at):
        mixer_out[at] = wide(mixer_out[at], far_in[at])

    by_rows(piece, add_far)
    for move in (*up_moves, hops[1]):
        move.wait_recv()
    far_cube.close()
    own_cube.close()

    @pl.when(my_dp > 0)
    def _():
        for move in rims:
            move.wait_send()

    for move in (taps_move, taps_back, back_move, far_move, *hops, *up_moves, *taps_moves, *gain_moves, *line_moves):
        move.wait_send()


def rear_call(up_sides, ins, backs, projs, convs, hop_in, term, normed, d_mix, d_hidden, gated, rims, inputs, scale, gain, gain_two, taps, span):
    rows, width = inputs.shape
    piece = up_sides[0].shape[0]
    local = taps.shape[1]
    grad_width = 4 * local
    lines = 2 * rows // span
    vmem = pl.BlockSpec(memory_space=pltpu.VMEM)
    anywhere = pl.BlockSpec(memory_space=pl.ANY)
    low = lambda *shape: pltpu.VMEM(shape, bf16)
    full = lambda *shape: pltpu.VMEM(shape, f32)
    out = lambda kind, *shape: jax.ShapeDtypeStruct(shape, kind)
    copies = 48
    return pl.pallas_call(
        functools.partial(rear_kernel, span),
        in_specs=[anywhere] * 12 + [vmem] * 12,
        out_specs=[vmem] * 4 + [anywhere] * 3,
        out_shape=[
            out(f32, piece, grad_width),
            out(bf16, rows, width),
            out(f32, 8, piece),
            out(f32, 8, local),
            out(bf16, *up_sides[0].shape),
            out(bf16, *up_sides[1].shape),
            out(bf16, rows, width),
        ],
        scratch_shapes=[
            low(width, 3 * local),
            low(2, width, local),
            full(4, 2 * rows, local),
            full(lines, span + 16, local),
            full(lines, span + 16, local),
            full(span + 8, local),
            low(2 * rows, 3 * local),
            low(2 * rows, 3 * local),
            low(4, piece, grad_width),
            low(4, piece, grad_width),
            low(4, piece, grad_width),
            low(2, piece // 2, grad_width),
            low(2, piece // 2, grad_width),
            low(2, piece, grad_width),
            low(2, piece, grad_width),
            low(piece, grad_width),
            full(2 * rows, width),
            low(rows, width),
            low(rows, width),
            low(rows, width),
            full(8, 8, piece),
            full(8, 8, piece),
            full(8, piece),
            full(4, 8, piece),
            full(8, local),
            full(8, local),
            full(2, 8, local),
            full(8, local),
            full(8, local),
            full(8, 8, local),
            pltpu.SemaphoreType.DMA((16,)),
            pltpu.SemaphoreType.DMA((2, 10)),
            pltpu.SemaphoreType.DMA((2, 10)),
            pltpu.SemaphoreType.DMA((copies,)),
            pltpu.SemaphoreType.DMA((copies,)),
        ],
        compiler_params=pltpu.CompilerParams(
            collective_id=1, has_side_effects=True, vmem_limit_bytes=60 * 2**20
        ),
        cost_estimate=pl.CostEstimate(
            flops=64 * rows * width * local, bytes_accessed=10**8, transcendentals=0
        ),
    )(
        *up_sides, *ins, *backs, *projs, *convs, hop_in, term, normed, d_mix, d_hidden, *gated, *rims,
        inputs, scale, gain, gain_two, taps,
    )


def last_kernel(
    down, gate, own, from_x, from_y, mixer, hidden, hop, term, live, token,
    down_out, gate_out, up_out, in_out, back_out, block_out, token_out,
):
    i = pl.program_id(0)
    down_out[...] = down[...].T
    gate_out[...] = gate[...]
    up_out[...] = wide(own[...], from_x[...], from_y[...])
    block_out[...] = (live[...] * wide(hidden[...], hop[...], term[...])).astype(bf16)
    token_out[...] = token[...]

    @pl.when(i < 6)
    def _():
        in_out[0] = mixer[...]

    @pl.when(i >= 6)
    def _():
        back_out[...] = mixer[...].T


def last_call(down, gate, up_parts, mixer, hidden, hop, term, live, token, local):
    rows, width = hidden.shape
    tile = width // 8
    part = pl.BlockSpec((rows, tile), lambda i: (0, i))
    out = lambda kind, *shape: jax.ShapeDtypeStruct(shape, kind)
    return pl.pallas_call(
        last_kernel,
        grid=(8,),
        in_specs=[part] * 9 + [pl.BlockSpec((rows, 1), lambda i: (0, 0)), part],
        out_specs=[
            pl.BlockSpec((tile, rows), lambda i: (i, 0)),
            part,
            part,
            pl.BlockSpec((1, rows, tile), lambda i: (jnp.minimum(i, 5) // 2, 0, jnp.minimum(i, 5) % 2)),
            pl.BlockSpec((tile, rows), lambda i: (jnp.maximum(i - 6, 0), 0)),
            part,
            part,
        ],
        out_shape=[
            out(f32, width, rows),
            out(f32, rows, width),
            out(f32, rows, width),
            out(f32, 3, rows, local),
            out(f32, local, rows),
            out(bf16, rows, width),
            out(bf16, rows, width),
        ],
        compiler_params=pltpu.CompilerParams(vmem_limit_bytes=60 * 2**20),
        cost_estimate=pl.CostEstimate(flops=0, bytes_accessed=44 * rows * width, transcendentals=0),
    )(down, gate, *up_parts, mixer, hidden, hop, term, live, token)


def turn_kernel(
    eb0, eb1, eb2, eb3, an0, an1, an2, an3, inner, d_gates, d_ups, hop_any, any0, any2, any3,
    hidden_any, scale, gain,
    down_out, gate_out, up_own, up_x, up_y, d_hidden, d_mix, gain_part,
    hop_in, term0, term2, term3, hidden, sens, normed, right_a, right_b, send_stage, moved, tops, lows, from_x, from_y, ring_in,
    load_sems, store_sems, swap_sends, swap_recvs, sends, recvs,
):
    my_dp, my_line = lax.axis_index("dp"), lax.axis_index("fsdp")
    my_chip, my_core = my_dp // 2, lax.rem(my_dp, 2)
    core = {"dp": lax.bitwise_xor(my_dp, CORE)}
    over_x = {"dp": lax.bitwise_xor(my_dp, XLINK)}
    over_y = {"dp": lax.bitwise_xor(my_dp, YLINK)}
    right = {"fsdp": lax.rem(my_line + 1, 4)}
    pair = {"fsdp": lax.bitwise_xor(my_line, 1)}
    rows = hidden_any.shape[0]
    piece = moved.shape[2]
    half = piece // 2

    loads = [0]

    def load(source, target):
        copy = pltpu.make_async_copy(source, target, load_sems.at[loads[0]])
        loads[0] += 1
        copy.start()
        return copy

    def load_rows(chunks, target):
        return [load(chunk, target.at[pl.ds(i * rows, rows)]) for i, chunk in enumerate(chunks)]

    now = [load(hop_any, hop_in), load(any2, term2)]
    first = load_rows((eb0, eb1, eb2, eb3), sens) + [load(inner, right_a)]
    second = load_rows((an0, an1, an2, an3), normed) + [load(d_gates, right_b)]
    later = [load(any3, term3), load(any0, term0), load(hidden_any, hidden)]
    greet(my_dp, my_line)
    wires = Wires(sends, recvs)

    def add_hop(source, term, step):
        def add(at):
            ring_in[step, at] = wide(source[at], term[at]).astype(bf16)

        by_rows(rows, add)
        return wires.to(ring_in.at[step], ring_in.at[step + 1], **right)

    for copy in now:
        copy.wait()
    hop2 = add_hop(hop_in, term2, 0)

    def swap(w, block):
        return pltpu.make_async_remote_copy(
            src_ref=send_stage.at[block],
            dst_ref=moved.at[w, block],
            send_sem=swap_sends.at[w, block],
            recv_sem=swap_recvs.at[w, block],
            device_id=core,
            device_id_type=MESH,
        )

    def across(w, side):
        source, target, device = (
            (moved.at[w, 3, pl.ds(0, half)], tops.at[w], over_x),
            (moved.at[w, 3, pl.ds(half, half)], lows.at[w], over_y),
        )[side]
        return pltpu.make_async_remote_copy(
            src_ref=source,
            dst_ref=target,
            send_sem=swap_sends.at[w, 4 + side],
            recv_sem=swap_recvs.at[w, 4 + side],
            device_id=device,
            device_id_type=MESH,
        )

    def weigh(w, left, right_ref, own):
        def product(block, side):
            place = 2 * lax.bitwise_xor(block, my_chip) + side
            columns = pl.ds(pl.multiple_of(place * piece, piece), piece)
            return contract_rows(left[:, columns], right_ref[...])

        def order(i):
            return jnp.where((i == 0) | (i == 3), 3 - i, i)

        if w:
            for block in range(4):
                swap(w - 1, block).wait_send()

        def give(i, carry):
            block = order(i)
            send_stage[block] = product(block, 1 - my_core).astype(bf16)
            swap(w, block).start()
            return carry

        def keep(i, carry):
            block = order(i)
            swap(w, block).wait_recv()
            value = product(block, my_core) + moved[w, block].astype(f32)
            moved[w, block] = value.astype(bf16)

            @pl.when(i == 0)
            def _():
                across(w, 0).start()
                across(w, 1).start()

            @pl.when(i == 3)
            def _():
                own[...] = value.astype(own.dtype)

            return carry

        lax.fori_loop(0, 4, give, 0)
        lax.fori_loop(0, 4, keep, 0)

    def sides(w):
        across(w, 0).wait_recv()
        across(w, 1).wait_recv()

        def add(at):
            below = pl.ds(pl.multiple_of(at.start + half, ROWS), ROWS)
            moved[w, 2, at] = wide(moved[w, 2, at], tops[w, at]).astype(bf16)
            moved[w, 1, below] = wide(moved[w, 1, below], lows[w, at]).astype(bf16)

        by_rows(half, add)

    for copy in first:
        copy.wait()
    weigh(0, sens, right_a, down_out)
    third = load(d_ups, right_a)
    for copy in second:
        copy.wait()
    weigh(1, normed, right_b, gate_out)
    sides(0)

    def sides_move(w):
        return [
            wires.to(moved.at[w, 1], from_x.at[w], **over_x),
            wires.to(moved.at[w, 2], from_y.at[w], **over_y),
        ]

    down_moves = sides_move(0)
    for copy in later:
        copy.wait()
    hop2.wait_recv()
    hop3 = add_hop(ring_in.at[1], term3, 1)
    third.wait()
    weigh(2, normed, right_a, up_own)
    sides(1)
    gate_moves = sides_move(1)
    hop3.wait_recv()
    gain_row = gain[...]

    def finish(i, total):
        at = pl.ds(pl.multiple_of(i * ROWS, ROWS), ROWS)
        grad = wide(ring_in[2, at], term0[at])
        values = hidden[at]
        r = scale[at]
        along = values * grad
        mean = jnp.mean(along * gain_row, axis=-1, keepdims=True)
        value = sens[at].astype(f32) + r * gain_row * grad - values * (r * r * r) * mean
        d_hidden[at] = value
        d_mix[at] = value.astype(bf16)
        return total + jnp.sum((along * r).reshape(ROWS // 8, 8, -1), axis=0)

    total = lax.fori_loop(0, rows // ROWS, finish, jnp.zeros((8, hidden.shape[1]), f32))
    pair_move = wires.to(d_mix.at[pl.ds(0, rows)], d_mix.at[pl.ds(rows, rows)], **pair)
    gain_part[...] = jnp.sum(total, axis=0, keepdims=True)
    sides(2)
    more = [
        pltpu.make_async_copy(moved.at[2, 1], up_x, store_sems.at[0]),
        pltpu.make_async_copy(moved.at[2, 2], up_y, store_sems.at[1]),
    ]
    for copy in more:
        copy.start()
    for w, moves, out in ((0, down_moves, down_out), (1, gate_moves, gate_out)):
        for move in moves:
            move.wait_recv()

        def add_sides(at):
            out[at] = wide(out[at], from_x[w, at], from_y[w, at])

        by_rows(piece, add_sides)
    pair_move.wait_recv()
    for copy in more:
        copy.wait()
    for block in range(4):
        swap(2, block).wait_send()
    for w in range(3):
        across(w, 0).wait_send()
        across(w, 1).wait_send()
    for move in (hop2, hop3, pair_move, *down_moves, *gate_moves):
        move.wait_send()


def turn_call(sens_all, normed_two, saved, hop_in, terms, hidden, scale, gain, piece):
    rows, width = hidden.shape
    inner_width = saved[0].shape[1]
    vmem = pl.BlockSpec(memory_space=pltpu.VMEM)
    anywhere = pl.BlockSpec(memory_space=pl.ANY)
    low = lambda *shape: pltpu.VMEM(shape, bf16)
    grad = jax.ShapeDtypeStruct((piece, inner_width), f32)
    side = jax.ShapeDtypeStruct((piece, inner_width), bf16)
    return pl.pallas_call(
        turn_kernel,
        in_specs=[anywhere] * 16 + [vmem] * 2,
        out_specs=[vmem] * 3 + [anywhere] * 2 + [vmem] * 3,
        out_shape=[
            grad,
            grad,
            side,
            side,
            side,
            jax.ShapeDtypeStruct((rows, width), f32),
            jax.ShapeDtypeStruct((2 * rows, width), bf16),
            jax.ShapeDtypeStruct((1, width), f32),
        ],
        scratch_shapes=[
            low(rows, width),
            low(rows, width),
            low(rows, width),
            low(rows, width),
            pltpu.VMEM((rows, width), f32),
            low(4 * rows, width),
            low(4 * rows, width),
            low(4 * rows, inner_width),
            low(4 * rows, inner_width),
            low(4, piece, inner_width),
            low(3, 4, piece, inner_width),
            low(3, piece // 2, inner_width),
            low(3, piece // 2, inner_width),
            low(2, piece, inner_width),
            low(2, piece, inner_width),
            low(3, rows, width),
            pltpu.SemaphoreType.DMA((20,)),
            pltpu.SemaphoreType.DMA((2,)),
            pltpu.SemaphoreType.DMA((3, 6)),
            pltpu.SemaphoreType.DMA((3, 6)),
            pltpu.SemaphoreType.DMA((8,)),
            pltpu.SemaphoreType.DMA((8,)),
        ],
        compiler_params=pltpu.CompilerParams(
            collective_id=2, has_side_effects=True, vmem_limit_bytes=60 * 2**20
        ),
        cost_estimate=pl.CostEstimate(
            flops=24 * rows * width * inner_width, bytes_accessed=2 * 10**8, transcendentals=0
        ),
    )(*sens_all, *normed_two, *saved, hop_in, *terms, hidden, scale, gain)


def total_all(value, axis):
    count = lax.axis_size(axis)
    offset = 1
    while offset < count:
        value = value + swapped(value, axis, offset)
        offset *= 2
    return value


def total_blocks(value, axis):
    count = lax.axis_size(axis)
    me = lax.axis_index(axis)
    offset = count // 2
    while offset:
        mine = me // offset % 2
        value = value.reshape((2, -1) + value.shape[1:])
        value = pick(value, 0, mine) + swapped(pick(value, 0, 1 - mine), axis, offset)
        offset //= 2
    return value[0]


def shards(
    tokens,
    cotangent,
    lengths,
    norm1_gain,
    in_weight,
    conv_taps,
    out_weight,
    norm2_gain,
    gate_weight,
    up_weight,
    down_weight,
):
    micro_count, group_count, span_len, model_width = tokens.shape
    line_count = micro_count * group_count
    row_count = line_count * span_len
    local_width = conv_taps.shape[1]
    piece = in_weight.shape[0]
    ring = lax.axis_size("fsdp")
    slices = range(0, ring, 2)
    cube = ring == 4 and lax.axis_size("dp") == 8 and row_count == piece
    my_line = lax.axis_index("fsdp")
    my_span = lax.axis_index("dp")
    slot_index = my_span * span_len + jnp.arange(span_len, dtype=jnp.int32)
    position = slot_index % SEQ_LEN
    seq_count = lengths.shape[2]
    seq_pick = (
        slot_index[:, None] // SEQ_LEN == jnp.arange(seq_count, dtype=jnp.int32)[None, :]
    ).astype(jnp.int32)
    valid_taps = [(position >= tap).astype(f32)[None, :, None] for tap in range(TAPS)]

    def from_owners(value):
        return lax.all_gather(value, "dp", axis=0, tiled=True)

    def to_owners(value):
        return lax.psum_scatter(value, "dp", scatter_dimension=0, tiled=True).astype(f32)

    inputs_f = tokens.reshape(row_count, model_width).astype(f32)
    lens = lengths.reshape(line_count, seq_count)
    seq_lens = jnp.sum(seq_pick[None, :, :] * lens[:, None, :], axis=2)
    live_mask = (position[None, :] < seq_lens).astype(f32).reshape(row_count, 1)
    sens_own = live_mask * cotangent.reshape(row_count, model_width).astype(f32)

    mixer_shard = jnp.concatenate([in_weight.reshape(piece, -1), out_weight.T], 1)
    pair_lines, pair_rows = 2 * line_count, 2 * row_count
    if cube:
        sens_low = sens_own.astype(bf16)
        taps_low = jnp.pad(conv_taps.astype(f32), ((0, 8 - TAPS), (0, 0)))
        (
            in_own, in_far, back_own, back_far, gate_full, up_full, down_back, sens1, sens2, sens3,
            normed_pair, proj_own, proj_far, conv_own, conv_far, gated_own, gated_far, rim_own, rim_far,
            hidden_one, normed, normed_next, normed_later, scale_one, scale_two, gain_one, gain_two,
        ) = head_call(
            mixer_shard,
            gate_weight,
            up_weight,
            down_weight.T,
            sens_low,
            tokens.reshape(row_count, model_width),
            jnp.pad(jnp.stack([norm1_gain, norm2_gain]).astype(f32), ((0, 6), (0, 0))),
            taps_low,
            span_len,
        )
        gain_one, gain_two = gain_one[0], gain_two[0]
        sens_all = [sens_low, sens1, sens2, sens3]
    else:
        gains = from_owners(jnp.stack([norm1_gain, norm2_gain], 1)).astype(f32)
        gain_one, gain_two = gains[:, 0], gains[:, 1]
        gain_one, mixer_shard, gate_weight, up_weight, down_weight = lax.optimization_barrier(
            (gain_one, mixer_shard, gate_weight, up_weight, down_weight)
        )
        shards_of = [mixer_shard] + [swapped(mixer_shard, "fsdp", c) for c in slices[1:]]
        taps_of = [conv_taps] + [swapped(conv_taps, "fsdp", c) for c in slices[1:]]
        mixer_widths = (3 * local_width, local_width)
        mixers, sent = [None], ()
        mixers[0], sent = gather_cube(mixer_shard, mixer_widths, sent)
        for shard in shards_of[1:]:
            mixer, sent = gather_cube(shard, mixer_widths, sent)
            mixers.append(mixer)
        gate_full = from_owners(gate_weight)
        up_full = from_owners(up_weight)
        down_back = from_owners(down_weight.T)

        scale_one = rms_scale(inputs_f)
        normed_own = (inputs_f * scale_one * gain_one).astype(bf16)
        normed_pair = jnp.concatenate([normed_own, swapped(normed_own, "fsdp", 1)], 0)
        sens_low, _ = lax.optimization_barrier((sens_own.astype(bf16), shards_of[-1]))
        sens_all = ring_gather(sens_low, "fsdp")

        kept = []
        mixed = jnp.zeros((pair_rows, model_width), f32)
        for (in_full, out_back), taps in zip(mixers, taps_of):
            taps_f = taps.astype(f32)
            early = ring // 2 if not kept else ring - 1
            normed_pair, sens_all[early] = lax.optimization_barrier((normed_pair, sens_all[early]))
            projected = times(normed_pair, in_full)
            b_part = projected[:, :local_width]
            c_part = projected[:, local_width : 2 * local_width]
            x_part = projected[:, 2 * local_width :]
            mixed_in = (b_part * x_part).reshape(pair_lines, span_len, local_width)
            rim_in = passed_along(mixed_in[:, span_len - (TAPS - 1) :], "dp", 1)
            padded = jnp.concatenate([rim_in, mixed_in], 1)
            convolved = jnp.zeros_like(mixed_in)
            for tap in range(TAPS):
                convolved = (
                    convolved
                    + taps_f[tap][None, None, :]
                    * padded[:, TAPS - 1 - tap : TAPS - 1 - tap + span_len]
                    * valid_taps[tap]
                )
            convolved = convolved.reshape(pair_rows, local_width)
            gated = (c_part * convolved).astype(bf16)
            kept.append((in_full, out_back, taps_f, b_part, c_part, x_part, padded, convolved, gated))
            mixed = mixed + times_transposed(gated, out_back)
        moved = swapped(mixed[row_count:].astype(bf16), "fsdp", 1)
        hidden_one = inputs_f + mixed[:row_count] + moved.astype(f32)
        scale_two = rms_scale(hidden_one)
        normed = (hidden_one * scale_two * gain_two).astype(bf16)

    if cube:
        normed_last = passed_round(normed_later, "fsdp")
        *saved, term0, term1, back0, back1 = ffn_pair(
            (normed, normed_next), sens_all[:2], gate_full, up_full, down_back, (), 0, 2
        )
        normed_last, back1 = lax.optimization_barrier((normed_last, back1))
        hop_in = passed_round(back1, "fsdp")
        *saved, term2, term3, back2, back3 = ffn_pair(
            (normed_later, normed_last), sens_all[2:], gate_full, up_full, down_back, saved, 1, 2
        )
        normed_two = [normed, normed_next, normed_later, normed_last]
        terms, back_terms = [term0, term1, term2, term3], [back0, back1, back2, back3]
        hop_in, terms[1] = lax.optimization_barrier((hop_in, terms[1]))
        hop = passed_round(terms[1], "fsdp")
        (
            down_grad, gate_grad, up_own, up_x, up_y, d_hidden, d_mix, gain_two_part,
        ) = turn_call(
            sens_all,
            normed_two,
            saved,
            hop_in,
            (back_terms[0], back_terms[2], back_terms[3]),
            hidden_one,
            scale_two,
            gain_two[None],
            piece,
        )
        hop = wide(hop, terms[2]).astype(bf16)
        mixer_sum, token_grad, gain_grads, taps_grad, *up_from, hop = rear_call(
            (up_x, up_y),
            (in_far, in_own),
            (back_far, back_own),
            (proj_far, proj_own),
            (conv_far, conv_own),
            hop,
            terms[3],
            normed_pair,
            d_mix,
            d_hidden,
            (gated_far, gated_own),
            (rim_far, rim_own),
            tokens.reshape(row_count, model_width),
            scale_one,
            gain_one[None],
            gain_two_part,
            taps_low,
            span_len,
        )
        down_grad, gate_grad, up_grad, in_grad, out_grad, block_out, token_grad = last_call(
            down_grad,
            gate_grad,
            (up_own, *up_from),
            mixer_sum,
            hidden_one,
            hop,
            terms[0],
            live_mask,
            token_grad,
            local_width,
        )
        return (
            block_out.reshape(tokens.shape),
            token_grad.reshape(tokens.shape),
            gain_grads[0],
            in_grad.transpose(1, 0, 2),
            taps_grad[:TAPS],
            out_grad,
            gain_grads[1],
            gate_grad,
            up_grad,
            down_grad,
        )
    normed_two, terms, back_terms, saved = [], [], [], ()
    for step, sens in enumerate(sens_all):
        normed_two.append(normed)
        if step < ring - 1:
            coming = passed_round(normed, "fsdp")
        *saved, term, back_term = ffn_chunk(
            normed, sens, gate_full, up_full, down_back, saved, step, ring
        )
        terms.append(term)
        back_terms.append(back_term)
        normed = coming
    d_normed_two = ring_collect([term.astype(f32) for term in back_terms], "fsdp")
    inner, d_gates, d_ups = saved
    sens_rows = jnp.concatenate(sens_all, 0)
    normed_rows = jnp.concatenate(normed_two, 0)
    down_grad = to_owners(contract_rows(sens_rows, inner).astype(bf16))
    gate_grad = to_owners(contract_rows(normed_rows, d_gates).astype(bf16))
    up_grad = to_owners(contract_rows(normed_rows, d_ups).astype(bf16))
    gain_two_part = jnp.sum(d_normed_two * hidden_one * scale_two, axis=0)
    d_hidden = (
        sens_own
        + scale_two * gain_two * d_normed_two
        - hidden_one
        * scale_two**3
        * jnp.mean(hidden_one * gain_two * d_normed_two, axis=-1, keepdims=True)
    )
    d_hidden_low = d_hidden.astype(bf16)
    d_mix = jnp.concatenate([d_hidden_low, swapped(d_hidden_low, "fsdp", 1)], 0)

    tap_parts, sums = [], []
    d_normed = jnp.zeros((pair_rows, model_width), f32)
    for in_full, out_back, taps_f, b_part, c_part, x_part, padded, convolved, gated in kept[::-1]:
        d_gated = times(d_mix, out_back)
        d_c_part = d_gated * convolved
        d_conv = (d_gated * c_part).reshape(pair_lines, span_len, local_width)
        d_padded = jnp.zeros_like(padded)
        tap_rows = []
        for tap in range(TAPS):
            weighted = d_conv * valid_taps[tap]
            d_padded = d_padded + jnp.pad(
                taps_f[tap][None, None, :] * weighted,
                ((0, 0), (TAPS - 1 - tap, tap), (0, 0)),
            )
            tap_rows.append(
                jnp.sum(weighted * padded[:, TAPS - 1 - tap : TAPS - 1 - tap + span_len], axis=(0, 1))
            )
        tap_parts.append(jnp.stack(tap_rows, 0))
        rim_back = passed_along(d_padded[:, : TAPS - 1], "dp", -1)
        d_mixed = (
            d_padded[:, TAPS - 1 :]
            + jnp.pad(rim_back, ((0, 0), (span_len - (TAPS - 1), 0), (0, 0)))
        ).reshape(pair_rows, local_width)
        d_proj = jnp.concatenate([d_mixed * x_part, d_c_part, d_mixed * b_part], axis=1).astype(bf16)
        d_normed = d_normed + times_transposed(d_proj, in_full)
        parts = weight_grad([([normed_pair], d_proj), ([d_mix], gated)], piece)
        d_mix, d_normed, *parts = lax.optimization_barrier((d_mix, d_normed, *parts))
        sums.append(CubeSum(parts))
    moved = swapped(d_normed[row_count:].astype(bf16), "fsdp", 1)
    for step in sums[:-1]:
        (moved,) = step.diagonal(moved)
    for step in sums[:-1]:
        (moved,) = step.sides(moved)
    (moved,) = sums[-1].diagonal(moved)
    (moved,) = sums[-1].sides(moved)
    d_normed_one = d_normed[:row_count] + moved.astype(f32)
    gain_one_part = jnp.sum(d_normed_one * inputs_f * scale_one, axis=0)
    token_grad = (
        d_hidden
        + scale_one * gain_one * d_normed_one
        - inputs_f
        * scale_one**3
        * jnp.mean(inputs_f * gain_one * d_normed_one, axis=-1, keepdims=True)
    ).astype(bf16)

    mixer_sum = sums[-1].total()
    for c, step in list(zip(slices[::-1], sums))[:-1]:
        mixer_sum = mixer_sum + swapped(step.total().astype(bf16), "fsdp", c).astype(f32)
    in_grad = mixer_sum[:, : 3 * local_width].reshape(in_weight.shape)
    out_grad = mixer_sum[:, 3 * local_width :].T

    ffn_out = ring_collect([term.astype(f32) for term in terms], "fsdp")
    block_out = (live_mask * (hidden_one + ffn_out)).astype(bf16)

    taps_sum = tap_parts[-1]
    for c, part in list(zip(slices[::-1], tap_parts))[:-1]:
        taps_sum = taps_sum + swapped(part, "fsdp", c)
    taps_grad = total_all(taps_sum, "dp")
    gain_grads = total_blocks(
        jnp.concatenate(
            [gain_one_part.reshape(-1, piece), gain_two_part.reshape(-1, piece)], 1
        ),
        "dp",
    )
    gain_grads = total_all(gain_grads, "fsdp").reshape(2, piece)
    return (
        block_out.reshape(tokens.shape),
        token_grad.reshape(tokens.shape),
        gain_grads[0],
        in_grad,
        taps_grad,
        out_grad,
        gain_grads[1],
        gate_grad,
        up_grad,
        down_grad.T,
    )


def solution(mesh):
    rows = P(None, "fsdp", "dp", None)
    return jax.shard_map(
        shards,
        mesh=mesh,
        in_specs=(
            rows,
            rows,
            P(None, "fsdp", None),
            P("dp"),
            P("dp", None, "fsdp"),
            P(None, "fsdp"),
            P("fsdp", "dp"),
            P("dp"),
            P("dp", "fsdp"),
            P("dp", "fsdp"),
            P("fsdp", "dp"),
        ),
        out_specs=(
            rows,
            rows,
            P("dp"),
            P("dp", None, "fsdp"),
            P(None, "fsdp"),
            P("fsdp", "dp"),
            P("dp"),
            P("dp", "fsdp"),
            P("dp", "fsdp"),
            P("fsdp", "dp"),
        ),
        check_vma=False,
    )
```

```python
import functools

import jax
import jax.numpy as jnp
from jax import lax
from jax.experimental import pallas as pl
from jax.experimental.pallas import tpu as pltpu
from jax.sharding import PartitionSpec as P

SEQ_LEN = 1024
TAPS = 3

norm_eps = 1e-05
f32 = jnp.float32
bf16 = jnp.bfloat16


def passed_along(value, axis, steps):
    count = lax.axis_size(axis)
    first, last = (max(0, -steps), min(count, count - steps))
    return lax.ppermute(value, axis, [(source, source + steps) for source in range(first, last)])


def passed_round(value, axis):
    count = lax.axis_size(axis)
    return lax.ppermute(value, axis, [(source, (source + 1) % count) for source in range(count)])


def ring_gather(value, axis):
    chunks = [value]
    for _ in range(lax.axis_size(axis) - 1):
        chunks.append(passed_round(chunks[-1], axis))
    return chunks


def ring_collect(terms, axis):
    count = lax.axis_size(axis)
    total = terms[1 % count]
    for step in range(1, count):
        moved = passed_round(total.astype(bf16), axis)
        total = wide(moved, terms[(step + 1) % count])
    return total


def rms_scale(values):
    return lax.rsqrt(jnp.mean(values * values, axis=-1, keepdims=True) + norm_eps)


def times(left, right):
    return jnp.dot(left, right, preferred_element_type=f32)


def times_transposed(left, right):
    return lax.dot_general(left, right, (((1,), (1,)), ((), ())), preferred_element_type=f32)


def contract_rows(left, right):
    return lax.dot_general(left, right, (((0,), (0,)), ((), ())), preferred_element_type=f32)


def ffn_tile(a_ref, e_ref, gate_ref, up_ref, down_ref, m_ref, dg_ref, du_ref, out_ref, da_ref):
    rows, sens = a_ref[...], e_ref[...]
    gate_pre = times(rows, gate_ref[...])
    up_pre = times(rows, up_ref[...])
    d_inner = times(sens, down_ref[...])
    sigmoid_gate = 1.0 / (1.0 + jnp.exp(-gate_pre))
    silu_gate = gate_pre * sigmoid_gate
    inner = (silu_gate * up_pre).astype(bf16)
    d_gate = (d_inner * up_pre * (sigmoid_gate * (1.0 + gate_pre * (1.0 - sigmoid_gate)))).astype(bf16)
    d_up = (d_inner * silu_gate).astype(bf16)
    m_ref[...] = inner
    dg_ref[...] = d_gate
    du_ref[...] = d_up
    out_ref[...] += times_transposed(inner, down_ref[...])
    da_ref[...] += times_transposed(d_gate, gate_ref[...]) + times_transposed(d_up, up_ref[...])


def ffn_kernel(a_ref, e_ref, gate_ref, up_ref, down_ref, *refs):
    m_ref, dg_ref, du_ref, term_ref, back_ref, out_ref, da_ref = refs[-7:]

    @pl.when(pl.program_id(0) == 0)
    def _():
        out_ref[...] = jnp.zeros_like(out_ref)
        da_ref[...] = jnp.zeros_like(da_ref)

    ffn_tile(a_ref, e_ref, gate_ref, up_ref, down_ref, m_ref, dg_ref, du_ref, out_ref, da_ref)

    @pl.when(pl.program_id(0) == pl.num_programs(0) - 1)
    def _():
        term_ref[...] = out_ref[...].astype(bf16)
        back_ref[...] = da_ref[...].astype(bf16)


def ffn_pair_kernel(a0, a1, e0, e1, gate_ref, up_ref, down_ref, *refs):
    m_ref, dg_ref, du_ref, term0, term1, back0, back1, a_ref, e_ref, out_ref, da_ref = refs[-11:]
    rows = a0.shape[0]

    @pl.when(pl.program_id(0) == 0)
    def _():
        a_ref[:rows] = a0[...]
        a_ref[rows:] = a1[...]
        e_ref[:rows] = e0[...]
        e_ref[rows:] = e1[...]
        out_ref[...] = jnp.zeros_like(out_ref)
        da_ref[...] = jnp.zeros_like(da_ref)

    ffn_tile(a_ref, e_ref, gate_ref, up_ref, down_ref, m_ref, dg_ref, du_ref, out_ref, da_ref)

    @pl.when(pl.program_id(0) == pl.num_programs(0) - 1)
    def _():
        term0[...] = out_ref[:rows].astype(bf16)
        term1[...] = out_ref[rows:].astype(bf16)
        back0[...] = da_ref[:rows].astype(bf16)
        back1[...] = da_ref[rows:].astype(bf16)


def ffn_pair(normed, sens, gate_full, up_full, down_back, saved, step, steps, tile=256):
    rows, width = normed[0].shape
    hidden = gate_full.shape[1]
    whole = pl.BlockSpec((rows, width), lambda i: (0, 0))
    weight = pl.BlockSpec((width, tile), lambda i: (0, i))
    part = pl.BlockSpec((2 * rows, tile), lambda i: (step, i))
    act = jax.ShapeDtypeStruct((2 * steps * rows, hidden), bf16)
    total = jax.ShapeDtypeStruct((rows, width), bf16)
    return pl.pallas_call(
        ffn_pair_kernel,
        grid=(hidden // tile,),
        in_specs=[whole] * 4
        + [weight] * 3
        + [pl.BlockSpec(memory_space=pl.ANY)] * len(saved),
        out_specs=[part] * 3 + [whole] * 4,
        out_shape=[act] * 3 + [total] * 4,
        scratch_shapes=[pltpu.VMEM((2 * rows, width), bf16)] * 2 + [pltpu.VMEM((2 * rows, width), f32)] * 2,
        input_output_aliases={7 + i: i for i in range(len(saved))},
        compiler_params=pltpu.CompilerParams(vmem_limit_bytes=60 * 2**20),
        cost_estimate=pl.CostEstimate(
            flops=24 * rows * width * hidden,
            bytes_accessed=6 * width * hidden + 24 * rows * width + 12 * rows * hidden,
            transcendentals=2 * rows * hidden,
        ),
    )(*normed, *sens, gate_full, up_full, down_back, *saved)


def ffn_chunk(normed, sens, gate_full, up_full, down_back, saved, step, steps, tile=512):
    rows, width = normed.shape
    hidden = gate_full.shape[1]
    whole = pl.BlockSpec((rows, width), lambda i: (0, 0))
    weight = pl.BlockSpec((width, tile), lambda i: (0, i))
    part = pl.BlockSpec((rows, tile), lambda i: (step, i))
    act = jax.ShapeDtypeStruct((steps * rows, hidden), bf16)
    total = jax.ShapeDtypeStruct((rows, width), bf16)
    return pl.pallas_call(
        ffn_kernel,
        grid=(hidden // tile,),
        in_specs=[whole, whole, weight, weight, weight]
        + [pl.BlockSpec(memory_space=pl.ANY)] * len(saved),
        out_specs=[part, part, part, whole, whole],
        out_shape=[act, act, act, total, total],
        scratch_shapes=[pltpu.VMEM((rows, width), f32)] * 2,
        input_output_aliases={5 + i: i for i in range(len(saved))},
        compiler_params=pltpu.CompilerParams(vmem_limit_bytes=48 * 2**20),
        cost_estimate=pl.CostEstimate(
            flops=12 * rows * width * hidden,
            bytes_accessed=6 * width * hidden + 12 * rows * width + 6 * rows * hidden,
            transcendentals=rows * hidden,
        ),
    )(normed, sens, gate_full, up_full, down_back, *saved)


def swapped(value, axis, offset):
    count = lax.axis_size(axis)
    return lax.ppermute(value, axis, [(source, source ^ offset) for source in range(count)])


CORE, XLINK, YLINK = 1, 2, 4


def gather_cube(shard, widths, after):
    if after:
        shard = lax.optimization_barrier((shard, *after))[0]
    if lax.axis_size("dp") != 8:
        full = lax.all_gather(shard, "dp", axis=0, tiled=True)
        ends = [sum(widths[: i + 1]) for i in range(len(widths))]
        return [full[:, end - width : end] for end, width in zip(ends, widths)], ()
    rows = shard.shape[0]
    half = rows // 2
    over_x = swapped(shard, "dp", XLINK)
    over_y = swapped(shard, "dp", YLINK)
    diag_top = swapped(over_x[:half], "dp", YLINK)
    diag_low = swapped(over_y[half:], "dp", XLINK)
    pieces = [
        (shard, 0, 0),
        (over_x, XLINK, 0),
        (over_y, YLINK, 0),
        (diag_top, XLINK | YLINK, 0),
        (diag_low, XLINK | YLINK, half),
    ]
    pieces += [(swapped(v, "dp", CORE), offset ^ CORE, at) for v, offset, at in pieces]

    count = len(pieces)

    def kernel(*refs):
        ins, outs = refs[:count], refs[count : count + len(widths)]
        held, in_sems, out_sems = refs[count + len(widths) :]
        me = lax.axis_index("dp")
        copies = []
        for i, (value, offset, at) in enumerate(pieces):
            start = pl.multiple_of(lax.bitwise_xor(me, offset) * rows + at, half)
            copies.append(
                pltpu.make_async_copy(
                    ins[i], held.at[pl.ds(start, value.shape[0]), :], in_sems.at[i]
                )
            )
        for copy in copies:
            copy.start()
        for copy in copies:
            copy.wait()
        copies, first = [], 0
        for j, width in enumerate(widths):
            copies.append(
                pltpu.make_async_copy(held.at[:, pl.ds(first, width)], outs[j], out_sems.at[j])
            )
            first += width
        for copy in copies:
            copy.start()
        for copy in copies:
            copy.wait()

    spec = pl.BlockSpec(memory_space=pl.ANY)
    full = pl.pallas_call(
        kernel,
        in_specs=[spec] * count,
        out_specs=[spec] * len(widths),
        out_shape=[jax.ShapeDtypeStruct((8 * rows, width), shard.dtype) for width in widths],
        scratch_shapes=[
            pltpu.VMEM((8 * rows, sum(widths)), shard.dtype),
            pltpu.SemaphoreType.DMA((count,)),
            pltpu.SemaphoreType.DMA((len(widths),)),
        ],
        cost_estimate=pl.CostEstimate(
            flops=0, bytes_accessed=32 * rows * sum(widths), transcendentals=0
        ),
    )(*[value for value, _, _ in pieces])
    return full, (over_x, over_y)


def pick(value, axis, index):
    return lax.dynamic_index_in_dim(value, index, axis, keepdims=False)


def grad_kernel(pairs, chunks, order_ref, *refs):
    keep_ref, send_ref = refs[-2:]
    for out_ref, at in ((keep_ref, 0), (send_ref, 1)):
        first = 0
        for pair in range(pairs):
            base = pair * (2 * chunks + 1)
            left = [refs[base + at * chunks + i][...] for i in range(chunks)]
            left = left[0] if chunks == 1 else jnp.concatenate(left, 0)
            right = refs[base + 2 * chunks]
            width = right.shape[1]
            out_ref[0, :, first : first + width] = contract_rows(left, right[...]).astype(bf16)
            first += width


def weight_grad(pairs, piece):
    chunks = len(pairs[0][0])
    width = sum(right.shape[1] for _, right in pairs)
    rows = pairs[0][1].shape[0]
    if lax.axis_size("dp") != 8:
        return (
            jnp.concatenate(
                [contract_rows(jnp.concatenate(left, 0), right).astype(bf16) for left, right in pairs], 1
            ),
        )
    me = lax.axis_index("dp")
    order = jnp.stack([me % 2, me // 2]).astype(jnp.int32)
    out = pl.BlockSpec((1, piece, width), lambda i, o: (i, 0, 0))
    chip = jax.ShapeDtypeStruct((4, piece, width), bf16)
    specs, values = [], []
    for left, right in pairs:
        lead = (left[0].shape[0], piece)
        specs += [pl.BlockSpec(lead, lambda i, o: (0, 2 * (i ^ o[1]) + o[0]))] * chunks
        specs += [pl.BlockSpec(lead, lambda i, o: (0, 2 * (i ^ o[1]) + 1 - o[0]))] * chunks
        specs += [pl.BlockSpec(right.shape, lambda i, o: (0, 0))]
        values += list(left) + list(left) + [right]
    return pl.pallas_call(
        functools.partial(grad_kernel, len(pairs), chunks),
        grid_spec=pltpu.PrefetchScalarGridSpec(
            num_scalar_prefetch=1, grid=(4,), in_specs=specs, out_specs=[out, out]
        ),
        out_shape=[chip, chip],
        compiler_params=pltpu.CompilerParams(vmem_limit_bytes=48 * 2**20),
        cost_estimate=pl.CostEstimate(
            flops=16 * rows * piece * width,
            bytes_accessed=16 * piece * width + 16 * rows * piece + 2 * rows * width,
            transcendentals=0,
        ),
    )(order, *values)


def wide(*values):
    total = values[0].astype(f32)
    for value in values[1:]:
        total = total + value.astype(f32)
    return total


class CubeSum:
    def __init__(self, parts):
        if len(parts) == 1:
            self.whole = lax.psum_scatter(parts[0], "dp", scatter_dimension=0, tiled=True).astype(f32)
            return
        self.whole = None
        self.keep = parts[0]
        self.moved = swapped(parts[1], "dp", CORE)

    def diagonal(self, *after):
        if self.whole is not None:
            return after
        half = self.keep.shape[1] // 2
        diag, *after = lax.optimization_barrier(
            (wide(self.keep[3], self.moved[3]).astype(bf16), *after)
        )
        self.top = swapped(diag[:half], "dp", XLINK)
        self.low = swapped(diag[half:], "dp", YLINK)
        return after

    def sides(self, *after):
        if self.whole is not None:
            return after
        half = self.keep.shape[1] // 2
        over_x = jnp.concatenate(
            [
                wide(self.keep[1, :half], self.moved[1, :half]).astype(bf16),
                wide(self.keep[1, half:], self.moved[1, half:], self.low).astype(bf16),
            ],
            0,
        )
        over_y = jnp.concatenate(
            [
                wide(self.keep[2, :half], self.moved[2, :half], self.top).astype(bf16),
                wide(self.keep[2, half:], self.moved[2, half:]).astype(bf16),
            ],
            0,
        )
        over_x, over_y, *after = lax.optimization_barrier((over_x, over_y, *after))
        self.from_x = swapped(over_x, "dp", XLINK)
        self.from_y = swapped(over_y, "dp", YLINK)
        return after

    def total(self):
        if self.whole is not None:
            return self.whole
        return wide(self.keep[0], self.moved[0], self.from_x, self.from_y)


MESH = pl.DeviceIdType.MESH
ROWS = 16


class Wires:
    def __init__(self, sends, recvs):
        self.sends, self.recvs, self.used = sends, recvs, 0

    def to(self, source, target, **device):
        copy = pltpu.make_async_remote_copy(
            src_ref=source,
            dst_ref=target,
            send_sem=self.sends.at[self.used],
            recv_sem=self.recvs.at[self.used],
            device_id=device,
            device_id_type=MESH,
        )
        self.used += 1
        copy.start()
        return copy


def greet(my_dp, my_line):
    barrier = pltpu.get_barrier_semaphore()
    for offset in range(1, 8):
        pl.semaphore_signal(
            barrier, inc=1, device_id={"dp": lax.bitwise_xor(my_dp, offset)}, device_id_type=MESH
        )
    for offset in range(1, 4):
        pl.semaphore_signal(
            barrier, inc=1, device_id={"fsdp": lax.bitwise_xor(my_line, offset)}, device_id_type=MESH
        )
    pl.semaphore_wait(barrier, 10)


def by_rows(count, body):
    def step(i, carry):
        body(pl.ds(pl.multiple_of(i * ROWS, ROWS), ROWS))
        return carry

    lax.fori_loop(0, count // ROWS, step, 0)


class CubeWires:
    def __init__(self, my_dp, product, stage, moved, top, low, from_x, from_y, own, sends, recvs):
        self.product, self.stage, self.moved, self.own = product, stage, moved, own
        self.top, self.low, self.from_x, self.from_y = top, low, from_x, from_y
        self.sends, self.recvs = sends, recvs
        self.my_core = lax.rem(my_dp, 2)
        self.core = {"dp": lax.bitwise_xor(my_dp, CORE)}
        self.x = {"dp": lax.bitwise_xor(my_dp, XLINK)}
        self.y = {"dp": lax.bitwise_xor(my_dp, YLINK)}
        self.rows = moved.shape[1]
        self.half = moved.shape[1] // 2

    def copy(self, i, source, target, device):
        return pltpu.make_async_remote_copy(
            src_ref=source,
            dst_ref=target,
            send_sem=self.sends.at[i],
            recv_sem=self.recvs.at[i],
            device_id=device,
            device_id_type=MESH,
        )

    def swap(self, block):
        return self.copy(block, self.stage.at[block], self.moved.at[block], self.core)

    def corner(self, i):
        if i == 0:
            return self.copy(4, self.moved.at[3, pl.ds(0, self.half)], self.top, self.x)
        return self.copy(5, self.moved.at[3, pl.ds(self.half, self.half)], self.low, self.y)

    def side(self, block, part):
        at = pl.ds(part * self.half, self.half)
        target, device = ((self.from_x, self.x), (self.from_y, self.y))[block - 1]
        return self.copy(4 + 2 * block + part, self.moved.at[block, at], target.at[at], device)

    def run(self):
        def order(i):
            return jnp.where((i == 0) | (i == 3), 3 - i, i)

        def step(i, carry):
            @pl.when(i < 4)
            def _():
                block = order(i)
                self.stage[block] = self.product(block, 1 - self.my_core).astype(bf16)
                self.swap(block).start()

            @pl.when(i > 0)
            def _():
                block = order(i - 1)
                self.swap(block).wait_recv()
                value = wide(self.product(block, self.my_core), self.moved[block])
                self.moved[block] = value.astype(bf16)

                @pl.when(i == 1)
                def _():
                    self.corner(0).start()
                    self.corner(1).start()

                if self.from_x is not None:

                    @pl.when(i == 2)
                    def _():
                        self.side(1, 0).start()

                    @pl.when(i == 3)
                    def _():
                        self.side(2, 1).start()

                if self.own is not None:

                    @pl.when(i == 4)
                    def _():
                        self.own[...] = value.astype(self.own.dtype)

            return carry

        lax.fori_loop(0, 5, step, 0)

    def others(self):
        self.corner(0).wait_recv()

        def add_top(at):
            self.moved[2, at] = wide(self.moved[2, at], self.top[at]).astype(bf16)

        by_rows(self.half, add_top)
        if self.from_x is not None:
            self.side(2, 0).start()
        self.corner(1).wait_recv()

        def add_low(at):
            below = pl.ds(pl.multiple_of(at.start + self.half, ROWS), ROWS)
            self.moved[1, below] = wide(self.moved[1, below], self.low[at]).astype(bf16)

        by_rows(self.half, add_low)
        if self.from_x is not None:
            self.side(1, 1).start()

    def total(self, store):
        for block in (1, 2):
            for part in range(2):
                self.side(block, part).wait_recv()

        own = self.moved.at[0] if self.own is None else self.own

        def add(at):
            store(at, wide(own[at], self.from_x[at], self.from_y[at]))

        by_rows(self.rows, add)

    def close_stage(self):
        for block in range(4):
            self.swap(block).wait_send()

    def close(self):
        for i in range(2):
            self.corner(i).wait_send()
        for block in (1, 2) if self.from_x is not None else ():
            for part in range(2):
                self.side(block, part).wait_send()


class Spread:
    def __init__(self, wires, my_dp, shard, full, own_sem, base=0):
        self.wires, self.my_dp, self.shard, self.full, self.own_sem = wires, my_dp, shard, full, own_sem
        self.rows, self.base = shard.shape[0], base
        self.core = {"dp": lax.bitwise_xor(my_dp, CORE)}
        self.x = {"dp": lax.bitwise_xor(my_dp, XLINK)}
        self.y = {"dp": lax.bitwise_xor(my_dp, YLINK)}

    def block(self, offset, first=0, count=None):
        half = self.rows // 2
        start = lax.bitwise_xor(self.my_dp, offset) * (self.full.shape[0] // 8) + self.base + first
        return self.full.at[pl.ds(pl.multiple_of(start, half), count or self.rows)]

    def start(self):
        own = self.block(0)
        self.own = pltpu.make_async_copy(self.shard, own, self.own_sem)
        self.own.start()
        self.over_x = self.wires.to(self.shard, own, **self.x)
        self.over_y = self.wires.to(self.shard, own, **self.y)
        self.cores = [self.wires.to(self.shard, own, **self.core)]

    def pass_on(self, block, **device):
        return self.wires.to(block, block, **device)

    def relay(self):
        half = self.rows // 2
        self.over_x.wait_recv()
        self.top = self.pass_on(self.block(XLINK, 0, half), **self.y)
        self.over_y.wait_recv()
        self.low = self.pass_on(self.block(YLINK, half, half), **self.x)
        self.cores += [self.pass_on(self.block(offset), **self.core) for offset in (XLINK, YLINK)]

    def finish(self):
        half = self.rows // 2
        for move, first in ((self.top, 0), (self.low, half)):
            move.wait_recv()
            self.cores.append(self.pass_on(self.block(XLINK | YLINK, first, half), **self.core))

    def complete(self):
        self.own.wait()
        for move in self.cores:
            move.wait_recv()

    def close(self):
        for move in (self.over_x, self.over_y, self.top, self.low, *self.cores):
            move.wait_send()


def head_kernel(
    span, mixer, gate, up, down, sens, inputs, gains, taps,
    in_own, in_far, back_own, back_far, gate_full, up_full, down_full, sens1, sens2, sens3,
    normed, proj_own, proj_far, conv_own, conv_far, gated_own, gated_far, rim_own, rim_far,
    hidden, normed_two, normed_next, normed_later, scale_one, scale_two, gain_one, gain_two,
    full_own, full_far, mixer_far, taps_far, total, lines_own, lines_far, mix_out, mix_in, gains_in,
    own_sems, out_sems, sends, recvs,
):
    my_dp, my_line = lax.axis_index("dp"), lax.axis_index("fsdp")
    right = {"fsdp": lax.rem(my_line + 1, 4)}
    pair = {"fsdp": lax.bitwise_xor(my_line, 1)}
    far = {"fsdp": lax.bitwise_xor(my_line, 2)}
    wires = Wires(sends, recvs)
    rows, width = inputs.shape
    piece = gains.shape[1]
    local = taps.shape[1]
    line_count = 2 * rows // span
    greet(my_dp, my_line)

    gain_moves = [
        wires.to(gains, gains_in.at[my_dp], dp=lax.bitwise_xor(my_dp, offset)) for offset in range(1, 8)
    ]
    taps_move = wires.to(taps, taps_far, **far)
    half = piece // 2
    halves = [pl.ds(0, half), pl.ds(half, half)]
    spreads = [
        Spread(wires, my_dp, shard, full, own_sems.at[i], base)
        for i, (shard, full, base) in enumerate(
            (
                (mixer, full_own, 0),
                (mixer_far.at[halves[0]], full_far, 0),
                (mixer_far.at[halves[1]], full_far, half),
                (gate, gate_full, 0),
                (up, up_full, 0),
                (down, down_full, 0),
            )
        )
    ]
    one, two_a, two_b, gates, ups, downs = spreads
    one.start()
    mixer_moves = [wires.to(mixer.at[at], mixer_far.at[at], **far) for at in halves]
    gains_in[my_dp] = gains[...]
    for move in gain_moves:
        move.wait_recv()
    for block in range(8):
        gain_one[:, block * piece : (block + 1) * piece] = gains_in[block, 0:1]
        gain_two[:, block * piece : (block + 1) * piece] = gains_in[block, 1:2]
    gain_row, gain_next = gain_one[...], gain_two[...]

    def first_norm(at):
        values = inputs[at].astype(f32)
        r = lax.rsqrt(jnp.mean(values * values, axis=-1, keepdims=True) + norm_eps)
        scale_one[at] = r
        normed[at] = (values * r * gain_row).astype(bf16)

    by_rows(rows, first_norm)
    normed_move = wires.to(normed.at[pl.ds(0, rows)], normed.at[pl.ds(rows, rows)], **pair)

    def mix(full, proj, conv, gated, rim, lines, taps_ref, first):
        def project(j, carry):
            columns = pl.ds(pl.multiple_of(j * local, local), local)
            proj[:, columns] = times(normed[...], full[:, columns])
            return carry

        lax.fori_loop(0, 3, project, 0)

        @pl.when(my_dp == 0)
        def _():
            lines[:, 0:8] = jnp.zeros((line_count, 8, local), f32)

        def gate_in(i, carry):
            at = pl.ds(pl.multiple_of(i * span, span), span)
            lines[i, 8 : 8 + span] = proj[at, 0:local] * proj[at, 2 * local : 3 * local]
            return carry

        lax.fori_loop(0, line_count, gate_in, 0)
        rim_move = pltpu.make_async_remote_copy(
            src_ref=lines.at[:, pl.ds(span, 8)],
            dst_ref=lines.at[:, pl.ds(0, 8)],
            send_sem=sends.at[wires.used],
            recv_sem=recvs.at[wires.used],
            device_id={"dp": jnp.minimum(my_dp + 1, 7)},
            device_id_type=MESH,
        )
        wires.used += 1

        @pl.when(my_dp < 7)
        def _():
            rim_move.start()

        @pl.when(my_dp > 0)
        def _():
            rim_move.wait_recv()

        rim[...] = lines[:, 0:8]
        tap_rows = [taps_ref[tap : tap + 1] for tap in range(TAPS)]

        def convolve(i, carry):
            for base in range(0, span, ROWS):
                at = pl.ds(pl.multiple_of(i * span + base, ROWS), ROWS)
                spot = my_dp * span + base + lax.broadcasted_iota(jnp.int32, (ROWS, 1), 0)
                position = lax.rem(spot, SEQ_LEN)
                value = tap_rows[0] * lines[i, 8 + base : 8 + base + ROWS]
                for tap in range(1, TAPS):
                    before = tap_rows[tap] * lines[i, 8 + base - tap : 8 + base - tap + ROWS]
                    value = value + jnp.where(position >= tap, before, 0.0)
                conv[at] = value
                gated[at] = (proj[at, local : 2 * local] * value).astype(bf16)
            return carry

        lax.fori_loop(0, line_count, convolve, 0)

        def back(j, carry):
            columns = pl.ds(pl.multiple_of(j * local, local), local)
            value = times_transposed(gated[...], full[columns, 3 * local : 4 * local])
            total[:, columns] = value if first else total[:, columns] + value
            return carry

        lax.fori_loop(0, width // local, back, 0)
        return rim_move

    def write_out(full, in_ref, back_ref, i):
        copies = [
            pltpu.make_async_copy(full.at[:, pl.ds(0, 3 * local)], in_ref, out_sems.at[2 * i]),
            pltpu.make_async_copy(full.at[:, pl.ds(3 * local, local)], back_ref, out_sems.at[2 * i + 1]),
        ]
        for copy in copies:
            copy.start()
        return copies

    one.relay()
    taps_move.wait_recv()
    mixer_moves[0].wait_recv()
    two_a.start()
    one.finish()
    one.complete()
    mixer_moves[1].wait_recv()
    two_b.start()
    sens_moves = [wires.to(sens, sens1, **right)]
    two_a.relay()
    normed_move.wait_recv()
    rims = [mix(full_own, proj_own, conv_own, gated_own, rim_own, lines_own, taps, True)]
    outs = write_out(full_own, in_own, back_own, 0)
    two_b.relay()
    gates.start()
    two_a.finish()
    two_b.finish()
    sens_moves[0].wait_recv()
    sens_moves.append(wires.to(sens1, sens2, **right))
    two_a.complete()
    two_b.complete()
    rims.append(mix(full_far, proj_far, conv_far, gated_far, rim_far, lines_far, taps_far, False))

    def shorten(at):
        mix_out[at] = total[pl.ds(pl.multiple_of(at.start + rows, ROWS), ROWS)].astype(bf16)

    by_rows(rows, shorten)
    mix_move = wires.to(mix_out, mix_in, **pair)
    outs += write_out(full_far, in_far, back_far, 1)
    gates.relay()
    ups.start()
    gates.finish()
    mix_move.wait_recv()

    def second_norm(at):
        values = wide(inputs[at], total[at], mix_in[at])
        hidden[at] = values
        r = lax.rsqrt(jnp.mean(values * values, axis=-1, keepdims=True) + norm_eps)
        scale_two[at] = r
        normed_two[at] = (values * r * gain_next).astype(bf16)

    by_rows(rows, second_norm)
    next_moves = [wires.to(normed_two, normed_next, **right)]
    sens_moves[1].wait_recv()
    sens_moves.append(wires.to(sens2, sens3, **right))
    ups.relay()
    downs.start()
    ups.finish()
    next_moves[0].wait_recv()
    next_moves.append(wires.to(normed_next, normed_later, **right))
    downs.relay()
    downs.finish()
    sens_moves[2].wait_recv()
    for spread in (gates, ups, downs):
        spread.complete()
    next_moves[1].wait_recv()
    for copy in outs:
        copy.wait()
    for spread in spreads:
        spread.close()

    @pl.when(my_dp < 7)
    def _():
        for move in rims:
            move.wait_send()

    for move in (taps_move, *mixer_moves, normed_move, mix_move, *next_moves, *gain_moves, *sens_moves):
        move.wait_send()


def head_call(mixer, gate, up, down, sens, inputs, gains, taps, span):
    rows, width = inputs.shape
    piece = mixer.shape[0]
    local = taps.shape[1]
    hidden = gate.shape[1]
    lines = 2 * rows // span
    vmem = pl.BlockSpec(memory_space=pltpu.VMEM)
    anywhere = pl.BlockSpec(memory_space=pl.ANY)
    low = lambda *shape: pltpu.VMEM(shape, bf16)
    full = lambda *shape: pltpu.VMEM(shape, f32)
    out = lambda kind, *shape: jax.ShapeDtypeStruct(shape, kind)
    copies = 96
    return pl.pallas_call(
        functools.partial(head_kernel, span),
        in_specs=[anywhere] * 5 + [vmem] * 3,
        out_specs=[anywhere] * 10 + [vmem] * 17,
        out_shape=[
            out(bf16, width, 3 * local),
            out(bf16, width, 3 * local),
            out(bf16, width, local),
            out(bf16, width, local),
            out(bf16, width, hidden),
            out(bf16, width, hidden),
            out(bf16, width, hidden),
            out(bf16, rows, width),
            out(bf16, rows, width),
            out(bf16, rows, width),
            out(bf16, 2 * rows, width),
            out(f32, 2 * rows, 3 * local),
            out(f32, 2 * rows, 3 * local),
            out(f32, 2 * rows, local),
            out(f32, 2 * rows, local),
            out(bf16, 2 * rows, local),
            out(bf16, 2 * rows, local),
            out(f32, lines, 8, local),
            out(f32, lines, 8, local),
            out(f32, rows, width),
            out(bf16, rows, width),
            out(bf16, rows, width),
            out(bf16, rows, width),
            out(f32, rows, 1),
            out(f32, rows, 1),
            out(f32, 1, width),
            out(f32, 1, width),
        ],
        scratch_shapes=[
            low(width, 4 * local),
            low(width, 4 * local),
            low(piece, 4 * local),
            full(*taps.shape),
            full(2 * rows, width),
            full(lines, 8 + span, local),
            full(lines, 8 + span, local),
            low(rows, width),
            low(rows, width),
            full(8, 8, piece),
            pltpu.SemaphoreType.DMA((6,)),
            pltpu.SemaphoreType.DMA((4,)),
            pltpu.SemaphoreType.DMA((copies,)),
            pltpu.SemaphoreType.DMA((copies,)),
        ],
        compiler_params=pltpu.CompilerParams(
            collective_id=3, has_side_effects=True, vmem_limit_bytes=60 * 2**20
        ),
        cost_estimate=pl.CostEstimate(
            flops=32 * rows * width * local, bytes_accessed=2 * 10**8, transcendentals=0
        ),
    )(mixer, gate, up, down, sens, inputs, gains, taps)


def rear_kernel(
    span, up_x, up_y, in_far, in_own, back_far, back_own, proj_far, proj_own, conv_far, conv_own, hop_in, term,
    normed, d_mix, d_hidden, gated_far, gated_own, rim_far, rim_own, inputs, scale, gain, gain_two, taps_own,
    mixer_out, token_out, gain_out, taps_out, up_from_x, up_from_y, hop_out,
    in_full, backs, parts, lines_far, lines_own, line, d_far, d_own, stage, moved_far, moved_own,
    tops, lows, from_x, from_y, far_in, total, back_in, hop_mid, hop_term,
    gain_cut, gain_in, gain_line, gain_lines, taps_given, taps_got, taps_part, taps_pair, taps_sum, taps_in,
    loads, cube_sends, cube_recvs, sends, recvs,
):
    my_dp, my_line = lax.axis_index("dp"), lax.axis_index("fsdp")
    my_chip = my_dp // 2
    pair = {"fsdp": lax.bitwise_xor(my_line, 1)}
    far = {"fsdp": lax.bitwise_xor(my_line, 2)}
    wires = Wires(sends, recvs)
    rows = inputs.shape[0]
    width = inputs.shape[1]
    piece = gain_out.shape[1]
    local = taps_own.shape[1]
    line_count = 2 * rows // span
    loaded = [0]

    def load(source, target):
        copy = pltpu.make_async_copy(source, target, loads.at[loaded[0]])
        loaded[0] += 1
        copy.start()
        return copy

    def column(proj, part):
        return proj.at[:, pl.ds(part * local, local)]

    early_far = [
        load(back_far, backs.at[0]), load(column(proj_far, 1), parts.at[0]), load(conv_far, parts.at[1])
    ]
    early_own = [
        load(back_own, backs.at[1]), load(column(proj_own, 1), parts.at[2]), load(conv_own, parts.at[3])
    ]
    in_load = load(in_far, in_full)
    term_load = load(term, hop_term)
    greet(my_dp, my_line)
    right = {"fsdp": lax.rem(my_line + 1, 4)}
    taps_move = wires.to(taps_own, taps_got, **far)
    hops = [wires.to(hop_in, hop_mid, **right)]

    def open_slice(i, early, lines, d_proj):
        for copy in early:
            copy.wait()

        def spread_rows(j, carry):
            at = pl.ds(pl.multiple_of(j * span, span), span)
            lines[j, 8 : 8 + span] = times(d_mix[at], backs[i])
            return carry

        lax.fori_loop(0, line_count, spread_rows, 0)

        @pl.when(my_dp == 7)
        def _():
            lines[:, 8 + span : 16 + span] = jnp.zeros((line_count, 8, local), f32)

        def share(j, carry):
            for base in range(0, span, ROWS):
                at = pl.ds(pl.multiple_of(j * span + base, ROWS), ROWS)
                d_gated = lines[j, 8 + base : 8 + base + ROWS]
                d_proj[at, local : 2 * local] = (d_gated * parts[2 * i + 1, at]).astype(bf16)
                lines[j, 8 + base : 8 + base + ROWS] = d_gated * parts[2 * i, at]
            return carry

        lax.fori_loop(0, line_count, share, 0)
        move = pltpu.make_async_remote_copy(
            src_ref=lines.at[:, pl.ds(8, 8)],
            dst_ref=lines.at[:, pl.ds(8 + span, 8)],
            send_sem=sends.at[wires.used],
            recv_sem=recvs.at[wires.used],
            device_id={"dp": jnp.maximum(my_dp - 1, 0)},
            device_id_type=MESH,
        )
        wires.used += 1

        @pl.when(my_dp > 0)
        def _():
            move.start()

        return move

    def close_slice(i, late, rim_move, lines, rim, d_proj, taps_ref):
        for copy in late:
            copy.wait()

        @pl.when(my_dp < 7)
        def _():
            rim_move.wait_recv()

        tap_rows = [taps_ref[tap : tap + 1] for tap in range(TAPS)]

        def convolve(j, sums):
            line[0:8] = rim[j]
            for base in range(0, span, ROWS):
                at = pl.ds(pl.multiple_of(j * span + base, ROWS), ROWS)
                line[8 + base : 8 + base + ROWS] = parts[2 * i, at] * parts[2 * i + 1, at]
            sums = list(sums)
            for base in range(0, span, ROWS):
                at = pl.ds(pl.multiple_of(j * span + base, ROWS), ROWS)
                spot = my_dp * span + base + lax.broadcasted_iota(jnp.int32, (ROWS, 1), 0)
                here = lines[j, 8 + base : 8 + base + ROWS]
                value = tap_rows[0] * here
                for tap in range(TAPS):
                    before = line[8 + base - tap : 8 + base - tap + ROWS]
                    valid = lax.rem(spot, SEQ_LEN) >= tap
                    grad = jnp.where(valid, here * before, 0.0)
                    sums[tap] = sums[tap] + jnp.sum(grad.reshape(ROWS // 8, 8, local), axis=0)
                for tap in range(1, TAPS):
                    after = tap_rows[tap] * lines[j, 8 + base + tap : 8 + base + tap + ROWS]
                    valid = lax.rem(spot + tap, SEQ_LEN) >= tap
                    value = value + jnp.where(valid, after, 0.0)
                d_proj[at, 0:local] = (value * parts[2 * i, at]).astype(bf16)
                d_proj[at, 2 * local : 3 * local] = (value * parts[2 * i + 1, at]).astype(bf16)
            return tuple(sums)

        sums = lax.fori_loop(0, line_count, convolve, (jnp.zeros((8, local), f32),) * TAPS)
        for tap in range(TAPS):
            taps_part[i, tap : tap + 1] = jnp.sum(sums[tap], axis=0, keepdims=True)

    def late_loads(i, proj):
        return [load(column(proj, 2), parts.at[2 * i]), load(column(proj, 0), parts.at[2 * i + 1])]

    def weigher(d_proj, gated):
        def product(block, side):
            place = 2 * lax.bitwise_xor(block, my_chip) + side
            columns = pl.ds(pl.multiple_of(place * piece, piece), piece)
            return jnp.concatenate(
                [
                    contract_rows(normed[:, columns], d_proj[...]).astype(bf16),
                    contract_rows(d_mix[:, columns], gated[...]).astype(bf16),
                ],
                1,
            )

        return product

    def back_rows(d_proj, first):
        def step(j, carry):
            columns = pl.ds(pl.multiple_of(j * local, local), local)
            value = times_transposed(d_proj[...], in_full[columns, :])
            total[:, columns] = value if first else total[:, columns] + value
            return carry

        lax.fori_loop(0, width // local, step, 0)

    rims = [open_slice(0, early_far, lines_far, d_far)]
    late_far = late_loads(0, proj_far)
    rims.append(open_slice(1, early_own, lines_own, d_own))
    late_own = late_loads(1, proj_own)

    def send_up(start):
        at = pl.ds(start, piece // 2)
        return [
            wires.to(up_x.at[at], up_from_x.at[at], dp=lax.bitwise_xor(my_dp, XLINK)),
            wires.to(up_y.at[at], up_from_y.at[at], dp=lax.bitwise_xor(my_dp, YLINK)),
        ]

    up_moves = send_up(0)
    taps_part[...] = jnp.zeros_like(taps_part)
    taps_move.wait_recv()
    close_slice(0, late_far, rims[0], lines_far, rim_far, d_far, taps_got)
    far_cube = CubeWires(
        my_dp, weigher(d_far, gated_far), stage, moved_far, tops.at[0], lows.at[0],
        from_x.at[0], from_y.at[0], None, cube_sends.at[0], cube_recvs.at[0],
    )
    own_cube = CubeWires(
        my_dp, weigher(d_own, gated_own), stage, moved_own, tops.at[1], lows.at[1],
        from_x.at[1], from_y.at[1], mixer_out, cube_sends.at[1], cube_recvs.at[1],
    )
    far_cube.run()
    close_slice(1, late_own, rims[1], lines_own, rim_own, d_own, taps_own)
    taps_given[...] = taps_part[0]
    taps_back = wires.to(taps_given, taps_pair, **far)
    in_load.wait()
    back_rows(d_far, True)
    in_load = load(in_own, in_full)
    term_load.wait()
    hops[0].wait_recv()

    def add_hop(at):
        hop_mid[at] = wide(hop_mid[at], hop_term[at]).astype(bf16)

    by_rows(rows, add_hop)
    hops.append(wires.to(hop_mid, hop_out, **right))
    far_cube.others()
    up_moves += send_up(piece // 2)
    far_cube.close_stage()
    own_cube.run()
    in_load.wait()
    back_rows(d_own, False)

    own_cube.close_stage()

    def shorten(at):
        stage[0, at] = total[pl.ds(pl.multiple_of(at.start + rows, ROWS), ROWS)].astype(bf16)

    by_rows(rows, shorten)
    back_move = wires.to(stage.at[0], back_in, **pair)
    taps_back.wait_recv()
    taps_sum[...] = taps_part[1] + taps_pair[...]
    taps_moves = [
        wires.to(taps_sum, taps_in.at[my_dp], dp=lax.bitwise_xor(my_dp, offset)) for offset in range(1, 8)
    ]

    def keep_low(at, value):
        stage[1, at] = value.astype(bf16)

    far_cube.total(keep_low)
    far_move = wires.to(stage.at[1], far_in, **far)
    own_cube.others()
    back_move.wait_recv()
    gain_row = gain[...]
    gain_cut[...] = jnp.zeros_like(gain_cut)

    def finish(i, part):
        at = pl.ds(pl.multiple_of(i * ROWS, ROWS), ROWS)
        grad = wide(total[at], back_in[at])
        values = inputs[at].astype(f32)
        r = scale[at]
        along = values * grad
        mean = jnp.mean(along * gain_row, axis=-1, keepdims=True)
        token_out[at] = (d_hidden[at] + r * gain_row * grad - values * (r * r * r) * mean).astype(bf16)
        return part + jnp.sum((along * r).reshape(ROWS // 8, 8, -1), axis=0)

    part = lax.fori_loop(0, rows // ROWS, finish, jnp.zeros((8, width), f32))
    part = jnp.sum(part, axis=0, keepdims=True)
    for block in range(8):
        gain_cut[block, 0:1] = part[:, block * piece : (block + 1) * piece]
        gain_cut[block, 1:2] = gain_two[:, block * piece : (block + 1) * piece]
    gain_moves = []
    for offset in range(1, 8):
        peer = lax.bitwise_xor(my_dp, offset)
        gain_moves.append(wires.to(gain_cut.at[peer], gain_in.at[my_dp], dp=peer))
    gain_in[my_dp] = gain_cut[my_dp]
    for move in gain_moves:
        move.wait_recv()
    gain_line[...] = jnp.sum(gain_in[...], axis=0)
    line_moves = [
        wires.to(gain_line, gain_lines.at[my_line], fsdp=lax.bitwise_xor(my_line, offset))
        for offset in range(1, 4)
    ]
    for move in taps_moves:
        move.wait_recv()
    taps_in[my_dp] = taps_sum[...]
    taps_out[...] = jnp.sum(taps_in[...], axis=0)

    def keep_wide(at, value):
        mixer_out[at] = value

    own_cube.total(keep_wide)
    for move in line_moves:
        move.wait_recv()
    gain_lines[my_line] = gain_line[...]
    gain_out[...] = jnp.sum(gain_lines[...], axis=0)
    far_move.wait_recv()

    def add_far(at):
        mixer_out[at] = wide(mixer_out[at], far_in[at])

    by_rows(piece, add_far)
    for move in (*up_moves, hops[1]):
        move.wait_recv()
    far_cube.close()
    own_cube.close()

    @pl.when(my_dp > 0)
    def _():
        for move in rims:
            move.wait_send()

    for move in (taps_move, taps_back, back_move, far_move, *hops, *up_moves, *taps_moves, *gain_moves, *line_moves):
        move.wait_send()


def rear_call(up_sides, ins, backs, projs, convs, hop_in, term, normed, d_mix, d_hidden, gated, rims, inputs, scale, gain, gain_two, taps, span):
    rows, width = inputs.shape
    piece = up_sides[0].shape[0]
    local = taps.shape[1]
    grad_width = 4 * local
    lines = 2 * rows // span
    vmem = pl.BlockSpec(memory_space=pltpu.VMEM)
    anywhere = pl.BlockSpec(memory_space=pl.ANY)
    low = lambda *shape: pltpu.VMEM(shape, bf16)
    full = lambda *shape: pltpu.VMEM(shape, f32)
    out = lambda kind, *shape: jax.ShapeDtypeStruct(shape, kind)
    copies = 48
    return pl.pallas_call(
        functools.partial(rear_kernel, span),
        in_specs=[anywhere] * 12 + [vmem] * 12,
        out_specs=[vmem] * 4 + [anywhere] * 3,
        out_shape=[
            out(f32, piece, grad_width),
            out(bf16, rows, width),
            out(f32, 8, piece),
            out(f32, 8, local),
            out(bf16, *up_sides[0].shape),
            out(bf16, *up_sides[1].shape),
            out(bf16, rows, width),
        ],
        scratch_shapes=[
            low(width, 3 * local),
            low(2, width, local),
            full(4, 2 * rows, local),
            full(lines, span + 16, local),
            full(lines, span + 16, local),
            full(span + 8, local),
            low(2 * rows, 3 * local),
            low(2 * rows, 3 * local),
            low(4, piece, grad_width),
            low(4, piece, grad_width),
            low(4, piece, grad_width),
            low(2, piece // 2, grad_width),
            low(2, piece // 2, grad_width),
            low(2, piece, grad_width),
            low(2, piece, grad_width),
            low(piece, grad_width),
            full(2 * rows, width),
            low(rows, width),
            low(rows, width),
            low(rows, width),
            full(8, 8, piece),
            full(8, 8, piece),
            full(8, piece),
            full(4, 8, piece),
            full(8, local),
            full(8, local),
            full(2, 8, local),
            full(8, local),
            full(8, local),
            full(8, 8, local),
            pltpu.SemaphoreType.DMA((16,)),
            pltpu.SemaphoreType.DMA((2, 10)),
            pltpu.SemaphoreType.DMA((2, 10)),
            pltpu.SemaphoreType.DMA((copies,)),
            pltpu.SemaphoreType.DMA((copies,)),
        ],
        compiler_params=pltpu.CompilerParams(
            collective_id=1, has_side_effects=True, vmem_limit_bytes=61 * 2**20
        ),
        cost_estimate=pl.CostEstimate(
            flops=64 * rows * width * local, bytes_accessed=10**8, transcendentals=0
        ),
    )(
        *up_sides, *ins, *backs, *projs, *convs, hop_in, term, normed, d_mix, d_hidden, *gated, *rims,
        inputs, scale, gain, gain_two, taps,
    )


def last_kernel(
    down, gate, own, from_x, from_y, mixer, hidden, hop, term, live, token,
    down_out, gate_out, up_out, in_out, back_out, block_out, token_out,
):
    i = pl.program_id(0)
    down_out[...] = down[...].T
    gate_out[...] = gate[...]
    up_out[...] = wide(own[...], from_x[...], from_y[...])
    block_out[...] = (live[...] * wide(hidden[...], hop[...], term[...])).astype(bf16)
    token_out[...] = token[...]

    @pl.when(i < 6)
    def _():
        in_out[0] = mixer[...]

    @pl.when(i >= 6)
    def _():
        back_out[...] = mixer[...].T


def last_call(down, gate, up_parts, mixer, hidden, hop, term, live, token, local):
    rows, width = hidden.shape
    tile = width // 8
    part = pl.BlockSpec((rows, tile), lambda i: (0, i))
    out = lambda kind, *shape: jax.ShapeDtypeStruct(shape, kind)
    return pl.pallas_call(
        last_kernel,
        grid=(8,),
        in_specs=[part] * 9 + [pl.BlockSpec((rows, 1), lambda i: (0, 0)), part],
        out_specs=[
            pl.BlockSpec((tile, rows), lambda i: (i, 0)),
            part,
            part,
            pl.BlockSpec((1, rows, tile), lambda i: (jnp.minimum(i, 5) // 2, 0, jnp.minimum(i, 5) % 2)),
            pl.BlockSpec((tile, rows), lambda i: (jnp.maximum(i - 6, 0), 0)),
            part,
            part,
        ],
        out_shape=[
            out(f32, width, rows),
            out(f32, rows, width),
            out(f32, rows, width),
            out(f32, 3, rows, local),
            out(f32, local, rows),
            out(bf16, rows, width),
            out(bf16, rows, width),
        ],
        compiler_params=pltpu.CompilerParams(vmem_limit_bytes=60 * 2**20),
        cost_estimate=pl.CostEstimate(flops=0, bytes_accessed=44 * rows * width, transcendentals=0),
    )(down, gate, *up_parts, mixer, hidden, hop, term, live, token)


def turn_kernel(
    eb0, eb1, eb2, eb3, an0, an1, an2, an3, inner, d_gates, d_ups, hop_any, any0, any2, any3,
    hidden_any, scale, gain,
    down_out, gate_out, up_own, up_x, up_y, d_hidden, d_mix, gain_part,
    hop_in, term0, term2, term3, hidden, sens, normed, right_a, right_b, send_stage, moved, tops, lows, from_x, from_y, ring_in,
    load_sems, store_sems, cube_sends, cube_recvs, sends, recvs,
):
    my_dp, my_line = lax.axis_index("dp"), lax.axis_index("fsdp")
    my_chip = my_dp // 2
    right = {"fsdp": lax.rem(my_line + 1, 4)}
    pair = {"fsdp": lax.bitwise_xor(my_line, 1)}
    rows = hidden_any.shape[0]
    piece = moved.shape[2]
    half = piece // 2

    loads = [0]

    def load(source, target):
        copy = pltpu.make_async_copy(source, target, load_sems.at[loads[0]])
        loads[0] += 1
        copy.start()
        return copy

    def load_rows(chunks, target):
        return [load(chunk, target.at[pl.ds(i * rows, rows)]) for i, chunk in enumerate(chunks)]

    now = [load(hop_any, hop_in), load(any2, term2)]
    first = load_rows((eb0, eb1, eb2, eb3), sens) + [load(inner, right_a)]
    second = load_rows((an0, an1, an2, an3), normed) + [load(d_gates, right_b)]
    later = [load(any3, term3), load(any0, term0), load(hidden_any, hidden)]
    greet(my_dp, my_line)
    wires = Wires(sends, recvs)

    def add_hop(source, term, step):
        def add(at):
            ring_in[step, at] = wide(source[at], term[at]).astype(bf16)

        by_rows(rows, add)
        return wires.to(ring_in.at[step], ring_in.at[step + 1], **right)

    for copy in now:
        copy.wait()
    hop2 = add_hop(hop_in, term2, 0)

    def weigher(left, right_ref):
        def product(block, side):
            place = 2 * lax.bitwise_xor(block, my_chip) + side
            columns = pl.ds(pl.multiple_of(place * piece, piece), piece)
            return contract_rows(left[:, columns], right_ref[...])

        return product

    cubes = [
        CubeWires(
            my_dp, weigher(left, right_ref), send_stage, moved.at[w], tops.at[w], lows.at[w],
            from_x.at[w] if w < 2 else None, from_y.at[w] if w < 2 else None, own,
            cube_sends.at[w], cube_recvs.at[w],
        )
        for w, (left, right_ref, own) in enumerate(
            ((sens, right_a, down_out), (normed, right_b, gate_out), (normed, right_a, up_own))
        )
    ]
    for copy in first:
        copy.wait()
    cubes[0].run()
    third = load(d_ups, right_a)
    for copy in second:
        copy.wait()
    cubes[0].close_stage()
    cubes[1].run()
    cubes[0].others()
    for copy in later:
        copy.wait()
    hop2.wait_recv()
    hop3 = add_hop(ring_in.at[1], term3, 1)
    third.wait()
    cubes[1].close_stage()
    cubes[2].run()
    cubes[1].others()
    hop3.wait_recv()
    gain_row = gain[...]

    def finish(i, total):
        at = pl.ds(pl.multiple_of(i * ROWS, ROWS), ROWS)
        grad = wide(ring_in[2, at], term0[at])
        values = hidden[at]
        r = scale[at]
        along = values * grad
        mean = jnp.mean(along * gain_row, axis=-1, keepdims=True)
        value = sens[at].astype(f32) + r * gain_row * grad - values * (r * r * r) * mean
        d_hidden[at] = value
        d_mix[at] = value.astype(bf16)
        return total + jnp.sum((along * r).reshape(ROWS // 8, 8, -1), axis=0)

    total = lax.fori_loop(0, rows // ROWS, finish, jnp.zeros((8, hidden.shape[1]), f32))
    pair_move = wires.to(d_mix.at[pl.ds(0, rows)], d_mix.at[pl.ds(rows, rows)], **pair)
    gain_part[...] = jnp.sum(total, axis=0, keepdims=True)
    cubes[2].others()
    more = [
        pltpu.make_async_copy(moved.at[2, 1], up_x, store_sems.at[0]),
        pltpu.make_async_copy(moved.at[2, 2], up_y, store_sems.at[1]),
    ]
    for copy in more:
        copy.start()
    for cube, out in ((cubes[0], down_out), (cubes[1], gate_out)):

        def store(at, value):
            out[at] = value

        cube.total(store)
    pair_move.wait_recv()
    for copy in more:
        copy.wait()
    cubes[2].close_stage()
    for cube in cubes:
        cube.close()
    for move in (hop2, hop3, pair_move):
        move.wait_send()


def turn_call(sens_all, normed_two, saved, hop_in, terms, hidden, scale, gain, piece):
    rows, width = hidden.shape
    inner_width = saved[0].shape[1]
    vmem = pl.BlockSpec(memory_space=pltpu.VMEM)
    anywhere = pl.BlockSpec(memory_space=pl.ANY)
    low = lambda *shape: pltpu.VMEM(shape, bf16)
    grad = jax.ShapeDtypeStruct((piece, inner_width), f32)
    side = jax.ShapeDtypeStruct((piece, inner_width), bf16)
    return pl.pallas_call(
        turn_kernel,
        in_specs=[anywhere] * 16 + [vmem] * 2,
        out_specs=[vmem] * 3 + [anywhere] * 2 + [vmem] * 3,
        out_shape=[
            grad,
            grad,
            side,
            side,
            side,
            jax.ShapeDtypeStruct((rows, width), f32),
            jax.ShapeDtypeStruct((2 * rows, width), bf16),
            jax.ShapeDtypeStruct((1, width), f32),
        ],
        scratch_shapes=[
            low(rows, width),
            low(rows, width),
            low(rows, width),
            low(rows, width),
            pltpu.VMEM((rows, width), f32),
            low(4 * rows, width),
            low(4 * rows, width),
            low(4 * rows, inner_width),
            low(4 * rows, inner_width),
            low(4, piece, inner_width),
            low(3, 4, piece, inner_width),
            low(3, piece // 2, inner_width),
            low(3, piece // 2, inner_width),
            low(2, piece, inner_width),
            low(2, piece, inner_width),
            low(3, rows, width),
            pltpu.SemaphoreType.DMA((20,)),
            pltpu.SemaphoreType.DMA((2,)),
            pltpu.SemaphoreType.DMA((3, 10)),
            pltpu.SemaphoreType.DMA((3, 10)),
            pltpu.SemaphoreType.DMA((8,)),
            pltpu.SemaphoreType.DMA((8,)),
        ],
        compiler_params=pltpu.CompilerParams(
            collective_id=2, has_side_effects=True, vmem_limit_bytes=60 * 2**20
        ),
        cost_estimate=pl.CostEstimate(
            flops=24 * rows * width * inner_width, bytes_accessed=2 * 10**8, transcendentals=0
        ),
    )(*sens_all, *normed_two, *saved, hop_in, *terms, hidden, scale, gain)


def total_all(value, axis):
    count = lax.axis_size(axis)
    offset = 1
    while offset < count:
        value = value + swapped(value, axis, offset)
        offset *= 2
    return value


def total_blocks(value, axis):
    count = lax.axis_size(axis)
    me = lax.axis_index(axis)
    offset = count // 2
    while offset:
        mine = me // offset % 2
        value = value.reshape((2, -1) + value.shape[1:])
        value = pick(value, 0, mine) + swapped(pick(value, 0, 1 - mine), axis, offset)
        offset //= 2
    return value[0]


def shards(
    tokens,
    cotangent,
    lengths,
    norm1_gain,
    in_weight,
    conv_taps,
    out_weight,
    norm2_gain,
    gate_weight,
    up_weight,
    down_weight,
):
    micro_count, group_count, span_len, model_width = tokens.shape
    line_count = micro_count * group_count
    row_count = line_count * span_len
    local_width = conv_taps.shape[1]
    piece = in_weight.shape[0]
    ring = lax.axis_size("fsdp")
    slices = range(0, ring, 2)
    cube = ring == 4 and lax.axis_size("dp") == 8 and row_count == piece
    my_line = lax.axis_index("fsdp")
    my_span = lax.axis_index("dp")
    slot_index = my_span * span_len + jnp.arange(span_len, dtype=jnp.int32)
    position = slot_index % SEQ_LEN
    seq_count = lengths.shape[2]
    seq_pick = (
        slot_index[:, None] // SEQ_LEN == jnp.arange(seq_count, dtype=jnp.int32)[None, :]
    ).astype(jnp.int32)
    valid_taps = [(position >= tap).astype(f32)[None, :, None] for tap in range(TAPS)]

    def from_owners(value):
        return lax.all_gather(value, "dp", axis=0, tiled=True)

    def to_owners(value):
        return lax.psum_scatter(value, "dp", scatter_dimension=0, tiled=True).astype(f32)

    inputs_f = tokens.reshape(row_count, model_width).astype(f32)
    lens = lengths.reshape(line_count, seq_count)
    seq_lens = jnp.sum(seq_pick[None, :, :] * lens[:, None, :], axis=2)
    live_mask = (position[None, :] < seq_lens).astype(f32).reshape(row_count, 1)
    sens_own = live_mask * cotangent.reshape(row_count, model_width).astype(f32)

    mixer_shard = jnp.concatenate([in_weight.reshape(piece, -1), out_weight.T], 1)
    pair_lines, pair_rows = 2 * line_count, 2 * row_count
    if cube:
        sens_low = sens_own.astype(bf16)
        taps_low = jnp.pad(conv_taps.astype(f32), ((0, 8 - TAPS), (0, 0)))
        (
            in_own, in_far, back_own, back_far, gate_full, up_full, down_back, sens1, sens2, sens3,
            normed_pair, proj_own, proj_far, conv_own, conv_far, gated_own, gated_far, rim_own, rim_far,
            hidden_one, normed, normed_next, normed_later, scale_one, scale_two, gain_one, gain_two,
        ) = head_call(
            mixer_shard,
            gate_weight,
            up_weight,
            down_weight.T,
            sens_low,
            tokens.reshape(row_count, model_width),
            jnp.pad(jnp.stack([norm1_gain, norm2_gain]).astype(f32), ((0, 6), (0, 0))),
            taps_low,
            span_len,
        )
        gain_one, gain_two = gain_one[0], gain_two[0]
        sens_all = [sens_low, sens1, sens2, sens3]
    else:
        gains = from_owners(jnp.stack([norm1_gain, norm2_gain], 1)).astype(f32)
        gain_one, gain_two = gains[:, 0], gains[:, 1]
        gain_one, mixer_shard, gate_weight, up_weight, down_weight = lax.optimization_barrier(
            (gain_one, mixer_shard, gate_weight, up_weight, down_weight)
        )
        shards_of = [mixer_shard] + [swapped(mixer_shard, "fsdp", c) for c in slices[1:]]
        taps_of = [conv_taps] + [swapped(conv_taps, "fsdp", c) for c in slices[1:]]
        mixer_widths = (3 * local_width, local_width)
        mixers, sent = [None], ()
        mixers[0], sent = gather_cube(mixer_shard, mixer_widths, sent)
        for shard in shards_of[1:]:
            mixer, sent = gather_cube(shard, mixer_widths, sent)
            mixers.append(mixer)
        gate_full = from_owners(gate_weight)
        up_full = from_owners(up_weight)
        down_back = from_owners(down_weight.T)

        scale_one = rms_scale(inputs_f)
        normed_own = (inputs_f * scale_one * gain_one).astype(bf16)
        normed_pair = jnp.concatenate([normed_own, swapped(normed_own, "fsdp", 1)], 0)
        sens_low, _ = lax.optimization_barrier((sens_own.astype(bf16), shards_of[-1]))
        sens_all = ring_gather(sens_low, "fsdp")

        kept = []
        mixed = jnp.zeros((pair_rows, model_width), f32)
        for (in_full, out_back), taps in zip(mixers, taps_of):
            taps_f = taps.astype(f32)
            early = ring // 2 if not kept else ring - 1
            normed_pair, sens_all[early] = lax.optimization_barrier((normed_pair, sens_all[early]))
            projected = times(normed_pair, in_full)
            b_part = projected[:, :local_width]
            c_part = projected[:, local_width : 2 * local_width]
            x_part = projected[:, 2 * local_width :]
            mixed_in = (b_part * x_part).reshape(pair_lines, span_len, local_width)
            rim_in = passed_along(mixed_in[:, span_len - (TAPS - 1) :], "dp", 1)
            padded = jnp.concatenate([rim_in, mixed_in], 1)
            convolved = jnp.zeros_like(mixed_in)
            for tap in range(TAPS):
                convolved = (
                    convolved
                    + taps_f[tap][None, None, :]
                    * padded[:, TAPS - 1 - tap : TAPS - 1 - tap + span_len]
                    * valid_taps[tap]
                )
            convolved = convolved.reshape(pair_rows, local_width)
            gated = (c_part * convolved).astype(bf16)
            kept.append((in_full, out_back, taps_f, b_part, c_part, x_part, padded, convolved, gated))
            mixed = mixed + times_transposed(gated, out_back)
        moved = swapped(mixed[row_count:].astype(bf16), "fsdp", 1)
        hidden_one = inputs_f + mixed[:row_count] + moved.astype(f32)
        scale_two = rms_scale(hidden_one)
        normed = (hidden_one * scale_two * gain_two).astype(bf16)

    if cube:
        normed_last = passed_round(normed_later, "fsdp")
        *saved, term0, term1, back0, back1 = ffn_pair(
            (normed, normed_next), sens_all[:2], gate_full, up_full, down_back, (), 0, 2
        )
        normed_last, back1 = lax.optimization_barrier((normed_last, back1))
        hop_in = passed_round(back1, "fsdp")
        *saved, term2, term3, back2, back3 = ffn_pair(
            (normed_later, normed_last), sens_all[2:], gate_full, up_full, down_back, saved, 1, 2
        )
        normed_two = [normed, normed_next, normed_later, normed_last]
        terms, back_terms = [term0, term1, term2, term3], [back0, back1, back2, back3]
        hop_in, terms[1] = lax.optimization_barrier((hop_in, terms[1]))
        hop = passed_round(terms[1], "fsdp")
        (
            down_grad, gate_grad, up_own, up_x, up_y, d_hidden, d_mix, gain_two_part,
        ) = turn_call(
            sens_all,
            normed_two,
            saved,
            hop_in,
            (back_terms[0], back_terms[2], back_terms[3]),
            hidden_one,
            scale_two,
            gain_two[None],
            piece,
        )
        hop = wide(hop, terms[2]).astype(bf16)
        mixer_sum, token_grad, gain_grads, taps_grad, *up_from, hop = rear_call(
            (up_x, up_y),
            (in_far, in_own),
            (back_far, back_own),
            (proj_far, proj_own),
            (conv_far, conv_own),
            hop,
            terms[3],
            normed_pair,
            d_mix,
            d_hidden,
            (gated_far, gated_own),
            (rim_far, rim_own),
            tokens.reshape(row_count, model_width),
            scale_one,
            gain_one[None],
            gain_two_part,
            taps_low,
            span_len,
        )
        down_grad, gate_grad, up_grad, in_grad, out_grad, block_out, token_grad = last_call(
            down_grad,
            gate_grad,
            (up_own, *up_from),
            mixer_sum,
            hidden_one,
            hop,
            terms[0],
            live_mask,
            token_grad,
            local_width,
        )
        return (
            block_out.reshape(tokens.shape),
            token_grad.reshape(tokens.shape),
            gain_grads[0],
            in_grad.transpose(1, 0, 2),
            taps_grad[:TAPS],
            out_grad,
            gain_grads[1],
            gate_grad,
            up_grad,
            down_grad,
        )
    normed_two, terms, back_terms, saved = [], [], [], ()
    for step, sens in enumerate(sens_all):
        normed_two.append(normed)
        if step < ring - 1:
            coming = passed_round(normed, "fsdp")
        *saved, term, back_term = ffn_chunk(
            normed, sens, gate_full, up_full, down_back, saved, step, ring
        )
        terms.append(term)
        back_terms.append(back_term)
        normed = coming
    d_normed_two = ring_collect([term.astype(f32) for term in back_terms], "fsdp")
    inner, d_gates, d_ups = saved
    sens_rows = jnp.concatenate(sens_all, 0)
    normed_rows = jnp.concatenate(normed_two, 0)
    down_grad = to_owners(contract_rows(sens_rows, inner).astype(bf16))
    gate_grad = to_owners(contract_rows(normed_rows, d_gates).astype(bf16))
    up_grad = to_owners(contract_rows(normed_rows, d_ups).astype(bf16))
    gain_two_part = jnp.sum(d_normed_two * hidden_one * scale_two, axis=0)
    d_hidden = (
        sens_own
        + scale_two * gain_two * d_normed_two
        - hidden_one
        * scale_two**3
        * jnp.mean(hidden_one * gain_two * d_normed_two, axis=-1, keepdims=True)
    )
    d_hidden_low = d_hidden.astype(bf16)
    d_mix = jnp.concatenate([d_hidden_low, swapped(d_hidden_low, "fsdp", 1)], 0)

    tap_parts, sums = [], []
    d_normed = jnp.zeros((pair_rows, model_width), f32)
    for in_full, out_back, taps_f, b_part, c_part, x_part, padded, convolved, gated in kept[::-1]:
        d_gated = times(d_mix, out_back)
        d_c_part = d_gated * convolved
        d_conv = (d_gated * c_part).reshape(pair_lines, span_len, local_width)
        d_padded = jnp.zeros_like(padded)
        tap_rows = []
        for tap in range(TAPS):
            weighted = d_conv * valid_taps[tap]
            d_padded = d_padded + jnp.pad(
                taps_f[tap][None, None, :] * weighted,
                ((0, 0), (TAPS - 1 - tap, tap), (0, 0)),
            )
            tap_rows.append(
                jnp.sum(weighted * padded[:, TAPS - 1 - tap : TAPS - 1 - tap + span_len], axis=(0, 1))
            )
        tap_parts.append(jnp.stack(tap_rows, 0))
        rim_back = passed_along(d_padded[:, : TAPS - 1], "dp", -1)
        d_mixed = (
            d_padded[:, TAPS - 1 :]
            + jnp.pad(rim_back, ((0, 0), (span_len - (TAPS - 1), 0), (0, 0)))
        ).reshape(pair_rows, local_width)
        d_proj = jnp.concatenate([d_mixed * x_part, d_c_part, d_mixed * b_part], axis=1).astype(bf16)
        d_normed = d_normed + times_transposed(d_proj, in_full)
        parts = weight_grad([([normed_pair], d_proj), ([d_mix], gated)], piece)
        d_mix, d_normed, *parts = lax.optimization_barrier((d_mix, d_normed, *parts))
        sums.append(CubeSum(parts))
    moved = swapped(d_normed[row_count:].astype(bf16), "fsdp", 1)
    for step in sums[:-1]:
        (moved,) = step.diagonal(moved)
    for step in sums[:-1]:
        (moved,) = step.sides(moved)
    (moved,) = sums[-1].diagonal(moved)
    (moved,) = sums[-1].sides(moved)
    d_normed_one = d_normed[:row_count] + moved.astype(f32)
    gain_one_part = jnp.sum(d_normed_one * inputs_f * scale_one, axis=0)
    token_grad = (
        d_hidden
        + scale_one * gain_one * d_normed_one
        - inputs_f
        * scale_one**3
        * jnp.mean(inputs_f * gain_one * d_normed_one, axis=-1, keepdims=True)
    ).astype(bf16)

    mixer_sum = sums[-1].total()
    for c, step in list(zip(slices[::-1], sums))[:-1]:
        mixer_sum = mixer_sum + swapped(step.total().astype(bf16), "fsdp", c).astype(f32)
    in_grad = mixer_sum[:, : 3 * local_width].reshape(in_weight.shape)
    out_grad = mixer_sum[:, 3 * local_width :].T

    ffn_out = ring_collect([term.astype(f32) for term in terms], "fsdp")
    block_out = (live_mask * (hidden_one + ffn_out)).astype(bf16)

    taps_sum = tap_parts[-1]
    for c, part in list(zip(slices[::-1], tap_parts))[:-1]:
        taps_sum = taps_sum + swapped(part, "fsdp", c)
    taps_grad = total_all(taps_sum, "dp")
    gain_grads = total_blocks(
        jnp.concatenate(
            [gain_one_part.reshape(-1, piece), gain_two_part.reshape(-1, piece)], 1
        ),
        "dp",
    )
    gain_grads = total_all(gain_grads, "fsdp").reshape(2, piece)
    return (
        block_out.reshape(tokens.shape),
        token_grad.reshape(tokens.shape),
        gain_grads[0],
        in_grad,
        taps_grad,
        out_grad,
        gain_grads[1],
        gate_grad,
        up_grad,
        down_grad.T,
    )


def solution(mesh):
    rows = P(None, "fsdp", "dp", None)
    return jax.shard_map(
        shards,
        mesh=mesh,
        in_specs=(
            rows,
            rows,
            P(None, "fsdp", None),
            P("dp"),
            P("dp", None, "fsdp"),
            P(None, "fsdp"),
            P("fsdp", "dp"),
            P("dp"),
            P("dp", "fsdp"),
            P("dp", "fsdp"),
            P("fsdp", "dp"),
        ),
        out_specs=(
            rows,
            rows,
            P("dp"),
            P("dp", None, "fsdp"),
            P(None, "fsdp"),
            P("fsdp", "dp"),
            P("dp"),
            P("dp", "fsdp"),
            P("dp", "fsdp"),
            P("fsdp", "dp"),
        ),
        check_vma=False,
    )
```
